128 devices in a mesh: dp: 16 (over y, x), inner: 8 (over z, core).
Axes of the slice: x: 4, y: 4, z: 4, core: 2. Of those that a mesh axis runs over, the one named last changes fastest.
Arguments:
- queries: bfloat16 [64, 512, 1024], P('dp', 'inner'), may hold values from -6 to 6
- passages: bfloat16 [64, 512, 1024], P('dp', 'inner'), may hold values from -6 to 6
- neg_lists: int32 [64, 8], replicated, may hold values from 0 to 63, as said below
Outputs:
- mean_loss: float32 [], replicated
- query_grad: bfloat16 [64, 512, 1024], P('dp', 'inner')
- passage_grad: bfloat16 [64, 512, 1024], P('dp', 'inner')
The draws below stay inside these ranges and needn't reach their ends.
Inputs may be any that keep to these rules, and one draw needn't show every extreme that they name: `neg_lists`: each row lists 8 different passage blocks, none from the row's own group (blocks with the same id // 4). The blocks that the rows of one group list include at least one and at most 2 blocks of every other group; in every draw some group lists exactly 2 blocks of every other group.
All inputs are finite; a program needn't handle non-finite values.
Results may differ from the reference program's by a relative error of at most 0.009.
Values may be sent and summed in bfloat16 or wider, within the bound.
A program may use at most 128 MiB of HBM per device.

```python
import math
import jax
import jax.numpy as jnp
from jax import lax

D = 1024
ROWS = 512
K = 8
CAP = 2
GB = 4
NBLK = 64
N_INNER = 8


def embed_pair(key):
    keys_list = [jax.random.fold_in(key, number) for number in (101, 102, 103, 104, 105)]
    shape_full = (NBLK, ROWS, D)
    base_rows = jnp.clip(jax.random.normal(keys_list[0], shape_full, jnp.float32), -4.0, 4.0)
    noise_rows = jnp.clip(jax.random.normal(keys_list[1], shape_full, jnp.float32), -4.0, 4.0)
    tilt_factor = 0.3
    block_pos = (jnp.arange(NBLK, dtype=jnp.float32) + 1.0) / NBLK
    row_index = jnp.arange(ROWS, dtype=jnp.int32)
    row_pos = (row_index.astype(jnp.float32) + 1.0) / ROWS
    mixing = tilt_factor * block_pos[:, None, None] * row_pos[None, :, None]
    query_rows = jnp.clip(mixing * base_rows + noise_rows, -6.0, 6.0)
    passage_rows = base_rows
    return (query_rows, passage_rows)


def draw_queries(key, part):
    return embed_pair(key)[0].astype(jnp.bfloat16)


def draw_passages(key, part):
    return embed_pair(key)[1].astype(jnp.bfloat16)


def pick_row(ordered_row, index_row):
    return ordered_row[index_row]


def draw_neg_lists(key, part):
    groups = NBLK // GB
    keys_list = [jax.random.fold_in(key, number) for number in (201, 202, 203, 204, 205)]
    group_ids = jnp.arange(groups, dtype=jnp.int32)
    slot_counts = jax.random.randint(keys_list[0], (groups, groups), 1, CAP + 1)
    full_group = jax.random.randint(keys_list[1], (), 0, groups)
    offset_pick = jax.random.randint(keys_list[2], (), 1, groups)
    slot_counts = jnp.where(group_ids[:, None] == full_group, CAP, slot_counts)
    slot_counts = jnp.where(group_ids[None, :] == (group_ids[:, None] + offset_pick) % groups, CAP, slot_counts)
    slot_counts = jnp.where(group_ids[None, :] == group_ids[:, None], 0, slot_counts)
    raw_bits = jax.random.randint(keys_list[3], (groups, groups, GB), 0, 1 << 20)
    local_order = jnp.argsort(raw_bits * GB + jnp.arange(GB, dtype=jnp.int32), axis=-1).astype(jnp.int32)
    cand_blocks = group_ids[None, :, None] * GB + local_order[:, :, :CAP]
    live_slots = jnp.arange(CAP, dtype=jnp.int32)[None, None, :] < slot_counts[:, :, None]
    cand_blocks = cand_blocks.reshape(groups, groups * CAP)
    live_slots = live_slots.reshape(groups, groups * CAP)
    raw_order = jax.random.randint(keys_list[4], (groups, groups * CAP), 0, 1 << 20)
    sort_keys = raw_order * (groups * CAP) + jnp.arange(groups * CAP, dtype=jnp.int32)
    sort_keys = jnp.where(live_slots, sort_keys, sort_keys + (1 << 20) * (groups * CAP))
    sort_order = jnp.argsort(sort_keys, axis=-1)
    ordered = jnp.take_along_axis(cand_blocks, sort_order, axis=-1)
    used_count = jnp.sum(live_slots.astype(jnp.int32), axis=-1)
    positions = jnp.arange(GB, dtype=jnp.int32)[:, None] * K + jnp.arange(K, dtype=jnp.int32)[None, :]
    index_rows = (positions[None, :, :] % used_count[:, None, None]).reshape(groups, GB * K)
    picked = jax.vmap(pick_row)(ordered, index_rows)
    return picked.reshape(NBLK, K).astype(jnp.int32)


def setup_inputs(seed: int = 0) -> dict:
    splits = jax.random.split(jax.random.key(seed), 4)
    queries = draw_queries(jax.random.fold_in(splits[3], 71), 0)
    passages = draw_passages(jax.random.fold_in(splits[3], 71), 0)
    neg_lists = draw_neg_lists(jax.random.fold_in(splits[3], 71), 0)
    return {"queries": queries, "passages": passages, "neg_lists": neg_lists}


def reference(queries, passages, neg_lists):
    block_count, block_rows, embed_width = queries.shape
    pick_count = neg_lists.shape[1]
    score_scale = 1.0 / math.sqrt(embed_width)
    slice_rows = block_rows // N_INNER
    block_ids = jnp.arange(block_count, dtype=jnp.int32)
    cand_ids = jnp.concatenate([block_ids[:, None], neg_lists.astype(jnp.int32)], axis=1)

    def logits_of(block_index):
        chosen = passages[cand_ids[block_index]].reshape((pick_count + 1) * block_rows, embed_width)
        return jnp.dot(chosen, queries[block_index].T, preferred_element_type=jnp.float32) * score_scale

    def first_pass(accum, block_index):
        logits = logits_of(block_index)
        row_lse = jax.nn.logsumexp(logits, axis=0)
        col_lse = jax.nn.logsumexp(logits, axis=1).reshape(pick_count + 1, block_rows)
        chosen_ids = cand_ids[block_index]
        accum = accum.at[chosen_ids].set(jnp.logaddexp(accum[chosen_ids], col_lse))
        return (accum, row_lse)
    start_lse = jnp.full((block_count, block_rows), -jnp.inf, dtype=jnp.float32)
    passage_lse, query_lse = lax.scan(first_pass, start_lse, block_ids)
    cand_total = (pick_count + 1) * block_rows
    own_target = (jnp.arange(cand_total)[:, None] == jnp.arange(block_rows)[None, :]).astype(jnp.float32)

    def block_step(far_sum, block_index):
        logits = logits_of(block_index)
        col_lse = passage_lse[cand_ids[block_index]].reshape(cand_total)
        probs = 0.5 * jnp.exp(logits - query_lse[block_index][None, :]) + 0.5 * jnp.exp(logits - col_lse[:, None]) - own_target
        weights = probs.astype(jnp.bfloat16)
        chosen = passages[cand_ids[block_index]]
        split_weights = weights.reshape(pick_count + 1, N_INNER, slice_rows, block_rows).astype(jnp.float32)
        split_cands = chosen.reshape(pick_count + 1, N_INNER, slice_rows, embed_width).astype(jnp.float32)
        slice_parts = jnp.einsum('kicr,kicd->ird', split_weights, split_cands)
        rounded_parts = lax.optimization_barrier(slice_parts.astype(jnp.bfloat16)).astype(jnp.float32)
        query_grad = lax.optimization_barrier(jnp.sum(rounded_parts, axis=0)).astype(jnp.bfloat16)
        passage_part = jnp.einsum('cr,rd->cd', weights.astype(jnp.float32), queries[block_index].astype(jnp.float32))
        passage_part = passage_part.reshape(pick_count + 1, block_rows, embed_width)
        far_sum = far_sum.at[neg_lists[block_index].astype(jnp.int32)].add(passage_part[1:])
        return (far_sum, (query_grad, passage_part[0]))

    def group_step(group_total, group_index):
        members = group_index * GB + jnp.arange(GB, dtype=jnp.int32)
        start_far = jnp.zeros((block_count, block_rows, embed_width), jnp.float32)
        far_sum, outputs = lax.scan(block_step, start_far, members)
        group_total = group_total + lax.optimization_barrier(far_sum.astype(jnp.bfloat16)).astype(jnp.float32)
        return (group_total, outputs)
    group_ids = jnp.arange(block_count // GB, dtype=jnp.int32)
    start_total = jnp.zeros((block_count, block_rows, embed_width), jnp.float32)
    group_total, (query_all, own_all) = lax.scan(group_step, start_total, group_ids)
    query_grad = query_all.reshape(block_count, block_rows, embed_width)
    passage_grad = (group_total + own_all.reshape(block_count, block_rows, embed_width)).astype(jnp.bfloat16)
    own_scores = jnp.einsum('brd,brd->br', queries.astype(jnp.float32), passages.astype(jnp.float32)) * score_scale
    mean_loss = (jnp.sum(query_lse - own_scores) + jnp.sum(passage_lse - own_scores)) / (2.0 * block_count * block_rows)
    return (mean_loss, query_grad, passage_grad)
```

```python
import functools
import math

import jax
import jax.numpy as jnp
from jax import lax
from jax.experimental import pallas as pl
from jax.experimental.pallas import tpu as pltpu
from jax.sharding import PartitionSpec as P

MESH = pl.DeviceIdType.MESH
NEG = -1e30
SIDE = 4
CAP = 2
VMEM_LIMIT = 60 * 1024 * 1024

VM = pl.BlockSpec(memory_space=pltpu.VMEM)
SM = pl.BlockSpec(memory_space=pltpu.SMEM)


def mod4(v):
    return lax.rem(v + SIDE, SIDE)


class Place:
    def __init__(self):
        self.dp = lax.axis_index("dp")
        self.inner = lax.axis_index("inner")
        self.y, self.x = self.dp // SIDE, lax.rem(self.dp, SIDE)
        self.z, self.c = self.inner // 2, lax.rem(self.inner, 2)

    def move(self, axis, step):
        if axis == "x":
            return (self.y * SIDE + mod4(self.x + step), self.inner)
        if axis == "y":
            return (mod4(self.y + step) * SIDE + self.x, self.inner)
        if axis == "z":
            return (self.dp, mod4(self.z + step) * 2 + self.c)
        return (self.dp, self.z * 2 + (1 - self.c))

    def group(self, first, rf, rt):
        if first == "y":
            return mod4(self.y + rf) * SIDE + mod4(self.x + rt)
        return mod4(self.y + rt) * SIDE + mod4(self.x + rf)


class Copies:
    def __init__(self, send_sem, recv_sem):
        self.send_sem, self.recv_sem, self.count, self.made = send_sem, recv_sem, 0, []

    def send(self, src, dst, device, landing=None):
        i = self.count
        self.count += 1
        copy = pltpu.make_async_remote_copy(
            src_ref=src, dst_ref=dst, send_sem=self.send_sem.at[i], recv_sem=self.recv_sem.at[i],
            device_id=device, device_id_type=MESH)
        copy.start()
        self.made.append(copy)
        if landing is None:
            return copy
        return pltpu.make_async_remote_copy(
            src_ref=src, dst_ref=landing, send_sem=self.send_sem.at[i],
            recv_sem=self.recv_sem.at[i], device_id=device, device_id_type=MESH)

    def drain(self):
        for copy in self.made:
            copy.wait_send()


def meet(devices):
    barrier = pltpu.get_barrier_semaphore()
    for device in devices:
        pl.semaphore_signal(barrier, inc=1, device_id=device, device_id_type=MESH)
    pl.semaphore_wait(barrier, len(devices))


def neighbours(me):
    return [me.move(a, s) for a in "xyz" for s in (1, -1)] + [me.move("core", 0)]


HALVES = (("y", "x"), ("x", "y"))


def gather_kernel(table, q_ref, p_ref, full_ref, got_ref, *scratch):
    near = [(None,) + scratch[3 * h:3 * h + 3] for h in (0, 1)]
    stage, relay, send_sem, recv_sem, local_sem = scratch[6:]
    me = Place()
    per, rows = p_ref.shape[0], p_ref.shape[1]
    half = rows // 2
    two = per // 2
    meet(neighbours(me))
    net = Copies(send_sem, recv_sem)
    mine = [p_ref.at[:, pl.ds(h * half, half)] for h in (0, 1)]

    first = []
    for h, (f, t) in enumerate(HALVES):
        up = net.send(mine[h], near[h][3], me.move(f, 1))
        down = net.send(mine[h], near[h][1], me.move(f, -1))
        first.append((up, down))
    at = lambda z, c: full_ref.at[mod4(z) * 2 + c]
    own_slot = at(me.z, me.c)
    z_up = net.send(q_ref, own_slot, me.move("z", 1), at(me.z - 1, me.c))
    z_down = net.send(q_ref, own_slot, me.move("z", -1), at(me.z + 1, me.c))
    pair = [net.send(q_ref, own_slot, me.move("core", 0), at(me.z, 1 - me.c))]
    keep = pltpu.make_async_copy(q_ref, own_slot, local_sem)
    keep.start()

    arrivals = []
    relays = []

    def spread(h, rf):
        f, t = HALVES[h]
        source = me.group(f, rf, 0)
        for dt in range(SIDE):
            if dt == 0 and rf == 0:
                continue
            group = me.group(f, 0, dt)
            for c in range(CAP):
                pick = table[group, source * CAP + c]
                if rf == 0:
                    block = p_ref[pick, pl.ds(h * half, half)]
                else:
                    block = near[h][rf][pick]
                if dt == 0:
                    got_ref[h, rf * CAP + c] = block
                else:
                    stage[h, dt, rf, c] = block
        up, down = me.move(t, 1), me.move(t, -1)
        a = net.send(stage.at[h, 2, rf, 0], relay.at[h, 0, rf], up)
        b = net.send(stage.at[h, 2, rf, 1], relay.at[h, 1, rf], down)
        relays.append((h, rf, a, b))
        slots = pl.ds
        arrivals.append(net.send(stage.at[h, 1, rf], got_ref.at[h, slots(24 + rf * CAP, CAP)], up))
        arrivals.append(net.send(stage.at[h, 3, rf], got_ref.at[h, slots(8 + rf * CAP, CAP)], down))

    def pass_on(entry):
        h, rf, a, b = entry
        t = HALVES[h][1]
        a.wait_recv()
        arrivals.append(net.send(relay.at[h, 0, rf], got_ref.at[h, 16 + rf * CAP], me.move(t, 1)))
        b.wait_recv()
        arrivals.append(
            net.send(relay.at[h, 1, rf], got_ref.at[h, 16 + rf * CAP + 1], me.move(t, -1)))

    for h in (0, 1):
        spread(h, 0)
        got_ref[h, 0:CAP] = jnp.zeros((CAP,) + got_ref.shape[2:], got_ref.dtype)
    second = []
    for h, (f, t) in enumerate(HALVES):
        up, down = first[h]
        up.wait_recv()
        a = net.send(near[h][3].at[0:two], near[h][2].at[0:two], me.move(f, 1))
        down.wait_recv()
        b = net.send(near[h][1].at[two:per], near[h][2].at[two:per], me.move(f, -1))
        second.append((a, b))
    for h in (0, 1):
        spread(h, 1)
        spread(h, 3)
    z_up.wait_recv()
    behind, ahead = at(me.z - 1, me.c), at(me.z + 1, me.c)
    across = mod4(me.z + 2) * 2
    far = full_ref.at[across + me.c]
    za = net.send(behind.at[0:two], behind.at[0:two], me.move("z", 1), far.at[0:two])
    pair.append(net.send(behind, behind, me.move("core", 0), at(me.z - 1, 1 - me.c)))
    z_down.wait_recv()
    zb = net.send(ahead.at[two:per], ahead.at[two:per], me.move("z", -1), far.at[two:per])
    pair.append(net.send(ahead, ahead, me.move("core", 0), at(me.z + 1, 1 - me.c)))
    for entry in relays[:2]:
        pass_on(entry)
    for h in (0, 1):
        for copy in second[h]:
            copy.wait_recv()
        spread(h, 2)
    za.wait_recv()
    zb.wait_recv()
    pair.append(net.send(far, far, me.move("core", 0), full_ref.at[across + 1 - me.c]))
    for entry in relays[2:]:
        pass_on(entry)
    for copy in pair + arrivals:
        copy.wait_recv()
    keep.wait()
    net.drain()


def slot_pair(rank, lists, dp, b, k):
    block = lists[dp * SIDE + b, k]
    group = block // SIDE
    r = rank[dp, block]
    ry = mod4(group // SIDE - dp // SIDE)
    rx = mod4(lax.rem(group, SIDE) - lax.rem(dp, SIDE))
    return block, rx * 8 + ry * 2 + r, ry * 8 + rx * 2 + r


def load_candidates(where, rank, lists, b, p_ref, got_ref, cand):
    dp = where[0]
    rows = p_ref.shape[1]
    half = rows // 2
    picks = lists.shape[1]
    cand[0:rows] = p_ref[b]
    for k in range(picks):
        _, sa, sb = slot_pair(rank, lists, dp, b, k)
        base = rows * (k + 1)
        cand[base:base + half] = got_ref[0, sa]
        cand[base + half:base + rows] = got_ref[1, sb]


def forward_kernel(where, rank, lists, p_ref, got_ref, full_ref, logit_ref, row_ref, dense_ref,
                   own_ref, cand):
    dp, inner = where[0], where[1]
    per, rows, width = p_ref.shape
    picks = lists.shape[1]
    queries = full_ref.shape[0] * rows
    scale = 1.0 / math.sqrt(width)
    dense_ref[...] = jnp.full(dense_ref.shape, NEG, jnp.float32)
    own_ref[...] = jnp.zeros(own_ref.shape, jnp.float32)
    lane = lax.broadcasted_iota(jnp.int32, (rows, 128), 1)
    sub = lax.broadcasted_iota(jnp.int32, (rows, 128), 0)
    lane1 = lax.broadcasted_iota(jnp.int32, (1, 128), 1)
    wide_lane = lax.broadcasted_iota(jnp.int32, (rows, queries), 1)
    wide_sub = lax.broadcasted_iota(jnp.int32, (rows, queries), 0)

    def step(b, carry):
        load_candidates(where, rank, lists, b, p_ref, got_ref, cand)
        q = full_ref[:, b].reshape(queries, width)
        logit_ref[b] = lax.dot_general(
            cand[...], q, (((1,), (1,)), ((), ())), preferred_element_type=jnp.float32) * scale
        peak = jnp.full((1, queries), NEG, jnp.float32)
        for i in range(picks + 1):
            part = logit_ref[b, i * rows:(i + 1) * rows]
            peak = jnp.maximum(peak, jnp.max(part, axis=0, keepdims=True))
            top = jnp.max(part, axis=1, keepdims=True)
            mass = jnp.sum(jnp.exp(part - top), axis=1, keepdims=True)
            lse = top + jnp.log(mass)
            if i == 0:
                block = dp * SIDE + b
                hit = wide_lane == wide_sub + inner * rows
                own_ref[...] += jnp.sum(jnp.where(hit, part, 0.0))
            else:
                block = lists[dp * SIDE + b, i - 1]
            side = block // 32
            line = lax.rem(block, 32)
            row = jnp.sum(jnp.where(lane == sub + side * 64, lse, 0.0), axis=0, keepdims=True)
            old = dense_ref[pl.ds(line, 1)]
            high = jnp.maximum(old, row)
            joined = high + jnp.log(jnp.exp(old - high) + jnp.exp(row - high))
            dense_ref[pl.ds(line, 1)] = jnp.where(lane1 // 64 == side, joined, old)
        total = jnp.zeros((1, queries), jnp.float32)
        for i in range(picks + 1):
            part = logit_ref[b, i * rows:(i + 1) * rows]
            total = total + jnp.sum(jnp.exp(part - peak), axis=0, keepdims=True)
        row_ref[pl.ds(b, 1)] = peak + jnp.log(total)
        return carry

    lax.fori_loop(0, per, step, 0)


def stats_kernel(groups, inners, rows_per, row_in, dense_in, own_in, row_out, dense_out, loss_out,
                 all_rows, all_dense, send_sem, recv_sem):
    me = Place()
    peers = [("dp", o) for o in range(1, groups)] + [("inner", o) for o in range(1, inners)]

    def peer(kind, o):
        if kind == "dp":
            return (lax.rem(me.dp + o, groups), me.inner)
        return (me.dp, lax.rem(me.inner + o, inners))

    meet([peer(*p) for p in peers])
    net = Copies(send_sem, recv_sem)
    waits = []
    for kind, o in peers:
        if kind == "dp":
            origin = lax.rem(me.dp - o + groups, groups)
            waits.append(net.send(dense_in, all_dense.at[me.dp], peer(kind, o),
                                  all_dense.at[origin]))
        else:
            origin = lax.rem(me.inner - o + inners, inners)
            waits.append(net.send(row_in, all_rows.at[me.inner], peer(kind, o),
                                  all_rows.at[origin]))
    all_dense[me.dp] = dense_in[...]
    all_rows[me.inner] = row_in[...]
    for copy in waits:
        copy.wait_recv()

    def fold(ref):
        top = jnp.max(ref[...], axis=0)
        return top + jnp.log(jnp.sum(jnp.exp(ref[...] - top[None]), axis=0))

    rows = fold(all_rows)
    dense = fold(all_dense)
    row_out[...] = rows
    dense_out[...] = dense
    lane = lax.broadcasted_iota(jnp.int32, rows.shape, 1)
    mine = jnp.sum(jnp.where(lane // rows_per == me.inner, rows, 0.0))
    line = lax.broadcasted_iota(jnp.int32, dense.shape, 0)
    side = lax.broadcasted_iota(jnp.int32, dense.shape, 1) // 64
    owned = (line + 32 * side) // SIDE == me.dp
    mine = mine + jnp.sum(jnp.where(owned, dense, 0.0))
    loss_out[...] = mine - 2.0 * own_in[...]
    net.drain()


def backward_kernel(where, rank, lists, p_ref, got_ref, full_ref, logit_ref, row_ref, dense_ref,
                    part_ref, query_ref, own_ref, cand, weight, prod, total):
    dp, inner = where[0], where[1]
    per, rows, width = p_ref.shape
    half = rows // 2
    picks = lists.shape[1]
    shards = full_ref.shape[0]
    queries = shards * rows
    lane = lax.broadcasted_iota(jnp.int32, (rows, 128), 1)
    sub = lax.broadcasted_iota(jnp.int32, (rows, 128), 0)
    wide_lane = lax.broadcasted_iota(jnp.int32, (rows, queries), 1)
    wide_sub = lax.broadcasted_iota(jnp.int32, (rows, queries), 0)

    def clear(i, carry):
        for h in (0, 1):
            total[h, i] = jnp.zeros(total.shape[2:], jnp.float32)
        return carry

    lax.fori_loop(0, total.shape[1], clear, 0)

    def step(b, carry):
        load_candidates(where, rank, lists, b, p_ref, got_ref, cand)
        q = full_ref[:, b].reshape(queries, width)
        row = row_ref[pl.ds(b, 1)]
        for i in range(picks + 1):
            block = dp * SIDE + b if i == 0 else lists[dp * SIDE + b, i - 1]
            line = dense_ref[pl.ds(lax.rem(block, 32), 1)]
            col = jnp.sum(jnp.where(lane == sub + (block // 32) * 64, line, 0.0), axis=1,
                          keepdims=True)
            part = logit_ref[b, i * rows:(i + 1) * rows]
            probs = 0.5 * jnp.exp(part - row) + 0.5 * jnp.exp(part - col)
            if i == 0:
                probs = probs - jnp.where(wide_lane == wide_sub + inner * rows, 1.0, 0.0)
            weight[i * rows:(i + 1) * rows] = probs.astype(jnp.bfloat16)
        prod[...] = jnp.dot(weight[...], q, preferred_element_type=jnp.float32)
        own_ref[b] = prod[0:rows]
        for k in range(picks):
            _, sa, sb = slot_pair(rank, lists, dp, b, k)
            base = rows * (k + 1)
            total[0, sa] = total[0, sa] + prod[base:base + half]
            total[1, sb] = total[1, sb] + prod[base + half:base + rows]
        grad = lax.dot_general(weight[...], cand[...], (((0,), (0,)), ((), ())),
                               preferred_element_type=jnp.float32)
        query_ref[:, b] = grad.astype(jnp.bfloat16).reshape(shards, rows, width)
        return carry

    lax.fori_loop(0, per, step, 0)

    def finish(i, carry):
        for h in (0, 1):
            part_ref[h, i] = total[h, i].astype(jnp.bfloat16)
        return carry

    lax.fori_loop(0, total.shape[1], finish, 0)


def reduce_kernel(groups, inners, count, rank, part_ref, query_ref, own_ref, loss_in, loss_out,
                  qg_ref, pg_ref, *scratch):
    bank = 2 * (SIDE - 1) * SIDE
    seen = [[scratch[(h * 3 + st) * SIDE:(h * 3 + st + 1) * SIDE] for st in range(3)]
            for h in (0, 1)]
    (relay, dense, merge, last, pair_in, qsum, zmerge, zlast, loss_dp, loss_inner, loss_mid,
     send_sem, recv_sem) = scratch[bank:]
    me = Place()
    per, rows, width = own_ref.shape
    half, two = rows // 2, per // 2
    f32, b16 = jnp.float32, jnp.bfloat16

    def loss_peer(kind, o):
        if kind == "dp":
            return (lax.rem(me.dp + o, groups), me.inner)
        return (me.dp, lax.rem(me.inner + o, inners))

    def dp_offset(o):
        return loss_peer("dp", o)

    def inner_offset(o):
        return loss_peer("inner", o)

    meet([dp_offset(o) for o in range(1, groups)] + [inner_offset(o) for o in range(1, inners)])
    net = Copies(send_sem, recv_sem)

    relays, parts = [], {}
    for rf in (2, 1, 3, 0):
        for h, (f, t) in enumerate(HALVES):
            up, down = me.move(t, 1), me.move(t, -1)
            a = net.send(part_ref.at[h, 16 + rf * CAP], relay.at[h, 0, rf], up)
            b = net.send(part_ref.at[h, 16 + rf * CAP + 1], relay.at[h, 1, rf], down)
            relays.append((h, rf, a, b))
            parts[h, rf] = [
                net.send(part_ref.at[h, pl.ds(8 + rf * CAP, CAP)], seen[h][2][rf], up),
                net.send(part_ref.at[h, pl.ds(24 + rf * CAP, CAP)], seen[h][0][rf], down)]
        if rf == 2:
            swaps = {}
            for dz in (2, 1, 3, 0):
                swaps[dz] = net.send(query_ref.at[mod4(me.z + dz) * 2 + 1 - me.c],
                                     pair_in.at[dz], me.move("core", 0))
            loss_waits = [
                net.send(loss_in, loss_dp.at[me.dp], dp_offset(o),
                         loss_dp.at[lax.rem(me.dp - o + groups, groups)])
                for o in range(1, groups)]
            loss_dp[me.dp] = loss_in[...]

    def pass_on(entry):
        h, rf, a, b = entry
        t = HALVES[h][1]
        a.wait_recv()
        parts[h, rf].append(net.send(relay.at[h, 0, rf], seen[h][1][rf].at[0], me.move(t, 1)))
        b.wait_recv()
        parts[h, rf].append(net.send(relay.at[h, 1, rf], seen[h][1][rf].at[1], me.move(t, -1)))

    def join(dz):
        swaps[dz].wait_recv()
        slot = mod4(me.z + dz) * 2 + me.c

        def body(j, carry):
            both = query_ref[slot, j].astype(f32) + pair_in[dz, j].astype(f32)
            qsum[dz, j] = both.astype(b16)
            return carry

        lax.fori_loop(0, per, body, 0)

    join(2)
    za = net.send(qsum.at[2, 0:two], zmerge.at[0], me.move("z", 1))
    zb = net.send(qsum.at[2, two:per], zmerge.at[1], me.move("z", -1))
    for entry in relays[:2]:
        pass_on(entry)
    join(1)
    join(3)

    def fold_in(target, rd, source, start):
        def body(j, carry):
            both = target[rd, start + j].astype(f32) + source[j].astype(f32)
            target[rd, start + j] = both.astype(b16)
            return carry

        lax.fori_loop(0, two, body, 0)

    za.wait_recv()
    fold_in(qsum, 1, zmerge.at[0], 0)
    z_up = net.send(qsum.at[1], zlast.at[0], me.move("z", 1))
    zb.wait_recv()
    fold_in(qsum, 3, zmerge.at[1], two)
    z_down = net.send(qsum.at[3], zlast.at[1], me.move("z", -1))
    for copy in loss_waits:
        copy.wait_recv()
    mid = jnp.sum(loss_dp[...], axis=0)
    loss_mid[...] = mid
    loss_waits = [
        net.send(loss_mid, loss_inner.at[me.inner], inner_offset(o),
                 loss_inner.at[lax.rem(me.inner - o + inners, inners)])
        for o in range(1, inners)]
    loss_inner[me.inner] = mid

    def collect(h, rf):
        f, t = HALVES[h]
        for copy in parts[h, rf]:
            copy.wait_recv()
        owner = me.group(f, rf, 0)
        for j in range(per):
            acc = jnp.zeros((half, width), f32)
            for st in range(SIDE):
                if st == 0 and rf == 0:
                    continue
                r = rank[me.group(f, 0, st), owner * per + j]
                live = (r >= 0).astype(f32)
                c = jnp.maximum(r, 0)
                if st == 0:
                    block = part_ref[h, rf * CAP + c]
                else:
                    block = seen[h][st - 1][rf][c]
                acc = acc + block.astype(f32) * live
            if rf == 0:
                own = own_ref[j, h * half:(h + 1) * half]
                own_ref[j, h * half:(h + 1) * half] = own + acc
            else:
                dense[h, rf, j] = acc.astype(b16)

    for h, (f, t) in enumerate(HALVES):
        collect(h, 2)
        merges = [net.send(dense.at[h, 2, 0:two], merge.at[h, 0], me.move(f, 1)),
                  net.send(dense.at[h, 2, two:per], merge.at[h, 1], me.move(f, -1))]
        parts[h, "merge"] = merges
    for entry in relays[2:6]:
        pass_on(entry)
    ends = []
    for h, (f, t) in enumerate(HALVES):
        for rf, slot in ((1, 0), (3, 1)):
            collect(h, rf)
            parts[h, "merge"][slot].wait_recv()
            fold_in(dense.at[h], rf, merge.at[h, slot], slot * two)
            ends.append(net.send(dense.at[h, rf], last.at[h, slot],
                                 me.move(f, 1 if slot == 0 else -1)))
    for entry in relays[6:]:
        pass_on(entry)
    join_final = swaps[0]
    join_final.wait_recv()
    z_up.wait_recv()
    z_down.wait_recv()
    own_slot = me.z * 2 + me.c

    def finish_query(j, carry):
        both = query_ref[own_slot, j].astype(f32) + pair_in[0, j].astype(f32)
        both = both + zlast[0, j].astype(f32) + zlast[1, j].astype(f32)
        qg_ref[j] = both.astype(b16)
        return carry

    lax.fori_loop(0, per, finish_query, 0)
    for copy in loss_waits:
        copy.wait_recv()
    loss_out[...] = jnp.sum(loss_inner[...], axis=0) * (1.0 / count)
    for h in (0, 1):
        collect(h, 0)
    for copy in ends:
        copy.wait_recv()
    for h in (0, 1):
        def finish(j, carry, h=h):
            span = pl.ds(h * half, half)
            both = own_ref[j, span] + last[h, 0, j].astype(f32) + last[h, 1, j].astype(f32)
            pg_ref[j, span] = both.astype(b16)
            return carry

        lax.fori_loop(0, per, finish, 0)
    net.drain()


def params(cid=None):
    if cid is None:
        return pltpu.CompilerParams(vmem_limit_bytes=VMEM_LIMIT)
    return pltpu.CompilerParams(vmem_limit_bytes=VMEM_LIMIT, collective_id=cid,
                                has_side_effects=True)


def sems(n):
    return [pltpu.SemaphoreType.DMA((n,)), pltpu.SemaphoreType.DMA((n,))]


def tables(neg_lists, groups, per):
    blocks = neg_lists.shape[0]
    ids = jnp.arange(blocks, dtype=jnp.int32)
    lists = neg_lists.reshape(groups, -1)
    present = jnp.any(lists[:, :, None] == ids[None, None, :], axis=1)
    quads = present.reshape(groups, groups, per).astype(jnp.int32)
    earlier = (jnp.arange(per)[:, None] < jnp.arange(per)[None, :]).astype(jnp.int32)
    rank = jnp.sum(quads[:, :, :, None] * earlier[None, None], axis=2)
    rank = jnp.where(quads == 1, rank, -1)
    slot = jnp.arange(CAP, dtype=jnp.int32)
    local = jnp.arange(per, dtype=jnp.int32)
    block = jnp.sum(
        jnp.where(rank[..., None] == slot, local[None, None, :, None], 0), axis=2)
    return rank.reshape(groups, blocks), block.reshape(groups, groups * CAP)


def body(queries, passages, neg_lists):
    per, rows, width = queries.shape
    groups, inners = lax.axis_size("dp"), lax.axis_size("inner")
    picks = neg_lists.shape[1]
    half, two = rows // 2, per // 2
    slots = groups * CAP
    cands, full_rows = (picks + 1) * rows, rows * inners
    b16, f32 = jnp.bfloat16, jnp.float32
    sds = jax.ShapeDtypeStruct
    rank, block = tables(neg_lists, groups, per)
    where = jnp.stack([lax.axis_index("dp"), lax.axis_index("inner")]).astype(jnp.int32)

    full, got = pl.pallas_call(
        gather_kernel,
        out_shape=(sds((inners, per, rows, width), b16), sds((2, slots, half, width), b16)),
        in_specs=[SM, VM, VM], out_specs=(VM, VM),
        scratch_shapes=[
            pltpu.VMEM((per, half, width), b16) for _ in range(2 * (SIDE - 1))] + [
            pltpu.VMEM((2, SIDE, SIDE, CAP, half, width), b16),
            pltpu.VMEM((2, 2, SIDE, half, width), b16)] + sems(72) + [pltpu.SemaphoreType.DMA],
        compiler_params=params(0), name="gather",
    )(block, queries, passages)

    logits, row_lse, dense, own = pl.pallas_call(
        forward_kernel,
        out_shape=(sds((per, cands, full_rows), f32), sds((per, full_rows), f32),
                   sds((32, 128), f32), sds((8, 128), f32)),
        in_specs=[SM, SM, SM, VM, VM, VM], out_specs=(VM, VM, VM, VM),
        scratch_shapes=[pltpu.VMEM((cands, width), b16)],
        compiler_params=params(), name="forward",
    )(where, rank, neg_lists, passages, got, full)

    row_all, dense_all, loss = pl.pallas_call(
        functools.partial(stats_kernel, groups, inners, rows),
        out_shape=(sds((per, full_rows), f32), sds((32, 128), f32), sds((8, 128), f32)),
        in_specs=[VM, VM, VM], out_specs=(VM, VM, VM),
        scratch_shapes=[pltpu.VMEM((inners, per, full_rows), f32),
                        pltpu.VMEM((groups, 32, 128), f32)] + sems(24),
        compiler_params=params(1), name="stats",
    )(row_lse, dense, own)

    parts, qparts, own_grad = pl.pallas_call(
        backward_kernel,
        out_shape=(sds((2, slots, half, width), b16), sds((inners, per, rows, width), b16),
                   sds((per, rows, width), f32)),
        in_specs=[SM, SM, SM, VM, VM, VM, VM, VM, VM], out_specs=(VM, VM, VM),
        scratch_shapes=[
            pltpu.VMEM((cands, width), b16), pltpu.VMEM((cands, full_rows), b16),
            pltpu.VMEM((cands, width), f32), pltpu.VMEM((2, slots, half, width), f32)],
        compiler_params=params(), name="backward",
    )(where, rank, neg_lists, passages, got, full, logits, row_all, dense_all)

    loss_all, query_grad, passage_grad, _ = reduce_call(
        groups, inners, 2.0 * groups * per * full_rows, rank, parts, qparts, own_grad, loss)
    return (loss_all[0, 0], query_grad, passage_grad)


def reduce_call(groups, inners, count, rank, parts, qparts, own_grad, loss):
    per, rows, width = own_grad.shape
    half, two = rows // 2, per // 2
    b16, f32 = jnp.bfloat16, jnp.float32
    sds = jax.ShapeDtypeStruct

    def kernel(rank, part_ref, query_ref, own_in, loss_in, loss_out, qg_ref, pg_ref, own_ref,
               *scratch):
        own_ref[...] = own_in[...]
        reduce_kernel(groups, inners, count, rank, part_ref, query_ref, own_ref, loss_in, loss_out,
                      qg_ref, pg_ref, *scratch)

    return pl.pallas_call(
        kernel,
        out_shape=(sds((8, 128), f32), sds((per, rows, width), b16), sds((per, rows, width), b16),
                   sds((per, rows, width), f32)),
        in_specs=[SM, VM, VM, VM, VM], out_specs=(VM, VM, VM, VM),
        scratch_shapes=[
            pltpu.VMEM((CAP, half, width), b16) for _ in range(2 * (SIDE - 1) * SIDE)] + [
            pltpu.VMEM((2, 2, SIDE, half, width), b16),
            pltpu.VMEM((2, SIDE, per, half, width), b16),
            pltpu.VMEM((2, 2, two, half, width), b16),
            pltpu.VMEM((2, 2, per, half, width), b16),
            pltpu.VMEM((SIDE, per, rows, width), b16),
            pltpu.VMEM((SIDE, per, rows, width), b16),
            pltpu.VMEM((2, two, rows, width), b16),
            pltpu.VMEM((2, per, rows, width), b16),
            pltpu.VMEM((groups, 8, 128), f32),
            pltpu.VMEM((inners, 8, 128), f32),
            pltpu.VMEM((8, 128), f32)] + sems(96),
        compiler_params=params(2), name="reduce",
    )(rank, parts, qparts, own_grad, loss)


def solution(mesh):
    in_specs = (P("dp", "inner", None), P("dp", "inner", None), P())
    out_specs = (P(), P("dp", "inner", None), P("dp", "inner", None))
    return jax.shard_map(body, mesh=mesh, in_specs=in_specs, out_specs=out_specs, check_vma=False)
```

```python
import functools
import math

import jax
import jax.numpy as jnp
from jax import lax
from jax.experimental import pallas as pl
from jax.experimental.pallas import tpu as pltpu
from jax.sharding import PartitionSpec as P

MESH = pl.DeviceIdType.MESH
NEG = -1e30
SIDE = 4
CAP = 2
VMEM_LIMIT = 62 * 1024 * 1024

VM = pl.BlockSpec(memory_space=pltpu.VMEM)
SM = pl.BlockSpec(memory_space=pltpu.SMEM)


def mod4(v):
    return lax.rem(v + SIDE, SIDE)


class Place:
    def __init__(self):
        self.dp = lax.axis_index("dp")
        self.inner = lax.axis_index("inner")
        self.y, self.x = self.dp // SIDE, lax.rem(self.dp, SIDE)
        self.z, self.c = self.inner // 2, lax.rem(self.inner, 2)

    def move(self, axis, step):
        if axis == "x":
            return (self.y * SIDE + mod4(self.x + step), self.inner)
        if axis == "y":
            return (mod4(self.y + step) * SIDE + self.x, self.inner)
        if axis == "z":
            return (self.dp, mod4(self.z + step) * 2 + self.c)
        return (self.dp, self.z * 2 + (1 - self.c))

    def group(self, first, rf, rt):
        if first == "y":
            return mod4(self.y + rf) * SIDE + mod4(self.x + rt)
        return mod4(self.y + rt) * SIDE + mod4(self.x + rf)


class Copies:
    def __init__(self, send_sem, recv_sem):
        self.send_sem, self.recv_sem, self.count, self.made = send_sem, recv_sem, 0, []

    def send(self, src, dst, device, landing=None):
        i = self.count
        self.count += 1
        copy = pltpu.make_async_remote_copy(
            src_ref=src, dst_ref=dst, send_sem=self.send_sem.at[i], recv_sem=self.recv_sem.at[i],
            device_id=device, device_id_type=MESH)
        copy.start()
        self.made.append(copy)
        if landing is None:
            return copy
        return pltpu.make_async_remote_copy(
            src_ref=src, dst_ref=landing, send_sem=self.send_sem.at[i],
            recv_sem=self.recv_sem.at[i], device_id=device, device_id_type=MESH)

    def drain(self):
        for copy in self.made:
            copy.wait_send()


def meet(devices):
    barrier = pltpu.get_barrier_semaphore()
    for device in devices:
        pl.semaphore_signal(barrier, inc=1, device_id=device, device_id_type=MESH)
    pl.semaphore_wait(barrier, len(devices))


def neighbours(me):
    return [me.move(a, s) for a in "xyz" for s in (1, -1)] + [me.move("core", 0)]


HALVES = (("y", "x"), ("x", "y"))


def fused_kernel(dims, spec, table, rank, spot, lists, q_ref, p_ref, loss_out, qg_ref, pg_ref,
                 *scratch):
    chunks, groups, inners = dims
    me = Place()
    per, rows, width = p_ref.shape
    half, two = rows // 2, per // 2
    deep = half // chunks
    picks = lists.shape[1]
    cands = picks + 1
    queries = inners * rows
    slots = groups * CAP
    f32, b16 = jnp.float32, jnp.bfloat16
    scale = 1.0 / math.sqrt(width)
    count = 2.0 * groups * per * queries
    take = dict(zip(spec, split_list(scratch, spec.values())))
    one = lambda name: take[name][0]
    full, stage, relay, relay2 = one("full"), one("stage"), one("relay"), one("relay2")
    got, logit, weight, prod = take["got"], take["logit"], take["weight"], take["prod"]
    cand, cols, row_part = one("cand"), one("cols"), one("row_part")
    row_src, dense_src, all_rows = one("row_src"), one("dense_src"), one("all_rows")
    all_dense, row_lse, pass_lse = one("all_dense"), one("row_lse"), one("pass_lse")
    part, query_part, own_sum = one("part"), one("query_part"), one("own_sum")
    dense, merge, last = one("dense"), one("merge"), one("last")
    pair_in, qsum, zmerge, zlast = one("pair_in"), one("qsum"), one("zmerge"), one("zlast")
    loss_dp, loss_inner, loss_mid = one("loss_dp"), one("loss_inner"), one("loss_mid")
    near = [[(None,) + take["near"][(ch * 2 + h) * 3:(ch * 2 + h) * 3 + 3] for h in (0, 1)]
            for ch in range(chunks)]
    seen = [[take["seen"][(h * 3 + st) * SIDE:(h * 3 + st + 1) * SIDE] for st in range(3)]
            for h in (0, 1)]
    net = Copies(one("send_sem"), one("recv_sem"))

    dp_peers = [(lax.rem(me.dp + o, groups), me.inner) for o in range(1, groups)]
    dp_from = [lax.rem(me.dp - o + groups, groups) for o in range(1, groups)]
    in_peers = [(me.dp, lax.rem(me.inner + o, inners)) for o in range(1, inners)]
    in_from = [lax.rem(me.inner - o + inners, inners) for o in range(1, inners)]
    meet(dp_peers + in_peers)

    span = lambda h, ch: pl.ds(h * half + ch * deep, deep)
    first, second, relays, arrivals = {}, {}, {}, {ch: [] for ch in range(chunks)}

    def send_own(ch):
        for h, (f, t) in enumerate(HALVES):
            mine = p_ref.at[:, span(h, ch)]
            first[ch, h] = (net.send(mine, near[ch][h][3], me.move(f, 1)),
                            net.send(mine, near[ch][h][1], me.move(f, -1)))

    def send_second(ch):
        for h, (f, t) in enumerate(HALVES):
            up, down = first[ch, h]
            up.wait_recv()
            a = net.send(near[ch][h][3].at[0:two], near[ch][h][2].at[0:two], me.move(f, 1))
            down.wait_recv()
            b = net.send(near[ch][h][1].at[two:per], near[ch][h][2].at[two:per], me.move(f, -1))
            second[ch, h] = (a, b)

    def spread(ch, rf):
        for h, (f, t) in enumerate(HALVES):
            if rf == 2:
                for copy in second[ch, h]:
                    copy.wait_recv()
            source = me.group(f, rf, 0)
            for dt in (2, 1, 3, 0):
                if dt == 0 and rf == 0:
                    got[ch][h, 0:CAP] = jnp.zeros((CAP, deep, width), b16)
                    continue
                group = me.group(f, 0, dt)
                for c in range(CAP):
                    pick = table[group, source * CAP + c]
                    block = p_ref[pick, span(h, ch)] if rf == 0 else near[ch][h][rf][pick]
                    if dt == 0:
                        got[ch][h, rf * CAP + c] = block
                    else:
                        stage[ch, h, dt - 1, rf, c] = block
            up, down = me.move(t, 1), me.move(t, -1)
            relays[ch, h, rf] = (
                net.send(stage.at[ch, h, 1, rf, 0], relay.at[ch, h, 0, rf], up),
                net.send(stage.at[ch, h, 1, rf, 1], relay.at[ch, h, 1, rf], down))
            arrivals[ch].append(net.send(
                stage.at[ch, h, 0, rf], got[ch].at[h, pl.ds(24 + rf * CAP, CAP)], up))
            arrivals[ch].append(net.send(
                stage.at[ch, h, 2, rf], got[ch].at[h, pl.ds(8 + rf * CAP, CAP)], down))

    def pass_on(ch, *rfs):
        for rf in rfs:
            for h, (f, t) in enumerate(HALVES):
                for side, copy in enumerate(relays[ch, h, rf]):
                    copy.wait_recv()
                    arrivals[ch].append(net.send(
                        relay.at[ch, h, side, rf], got[ch].at[h, 16 + rf * CAP + side],
                        me.move(t, 1 - 2 * side)))

    at = lambda z, c: full.at[mod4(z) * 2 + c]
    own_slot = at(me.z, me.c)
    send_own(0)
    z_up = net.send(q_ref, own_slot, me.move("z", 1), at(me.z - 1, me.c))
    z_down = net.send(q_ref, own_slot, me.move("z", -1), at(me.z + 1, me.c))
    pair = [net.send(q_ref, own_slot, me.move("core", 0), at(me.z, 1 - me.c))]
    keep = pltpu.make_async_copy(q_ref, own_slot, one("local_sem"))
    keep.start()
    spread(0, 0)
    for ch in range(1, chunks):
        send_own(ch)
    send_second(0)
    spread(0, 1)
    spread(0, 3)
    z_up.wait_recv()
    behind, ahead = at(me.z - 1, me.c), at(me.z + 1, me.c)
    across = mod4(me.z + 2) * 2
    far = full.at[across + me.c]
    za = net.send(behind.at[0:two], behind.at[0:two], me.move("z", 1), far.at[0:two])
    pair.append(net.send(behind, behind, me.move("core", 0), at(me.z - 1, 1 - me.c)))
    z_down.wait_recv()
    zb = net.send(ahead.at[two:per], ahead.at[two:per], me.move("z", -1), far.at[two:per])
    pair.append(net.send(ahead, ahead, me.move("core", 0), at(me.z + 1, 1 - me.c)))
    pass_on(0, 0)
    for ch in range(1, chunks):
        send_second(ch)
    spread(0, 2)
    for ch in range(1, chunks):
        spread(ch, 0)
        pass_on(ch - 1, 1, 3)
        spread(ch, 1)
        spread(ch, 3)
        if ch == 1:
            za.wait_recv()
            zb.wait_recv()
            pair.append(
                net.send(far, far, me.move("core", 0), full.at[across + 1 - me.c]))
        pass_on(ch - 1, 2)
        spread(ch, 2)
        pass_on(ch, 0)
    if chunks == 1:
        za.wait_recv()
        zb.wait_recv()
        pair.append(net.send(far, far, me.move("core", 0), full.at[across + 1 - me.c]))

    lane = lax.broadcasted_iota(jnp.int32, (2 * deep, 128), 1)
    sub = lax.broadcasted_iota(jnp.int32, (2 * deep, 128), 0)
    wide_lane = lax.broadcasted_iota(jnp.int32, (2 * deep, queries), 1)
    wide_sub = lax.broadcasted_iota(jnp.int32, (2 * deep, queries), 0)

    def true_row(ch, sub):
        return (sub // deep) * half + ch * deep + lax.rem(sub, deep)

    def load_candidates(ch, b):
        cand[0:deep] = p_ref[b, span(0, ch)]
        cand[deep:2 * deep] = p_ref[b, span(1, ch)]
        for k in range(picks):
            block = lists[me.dp * per + b, k]
            group = block // per
            r = rank[me.dp, block]
            ry = mod4(group // SIDE - me.y)
            rx = mod4(lax.rem(group, SIDE) - me.x)
            base = 2 * deep * (k + 1)
            cand[base:base + deep] = got[ch][0, rx * 8 + ry * 2 + r]
            cand[base + deep:base + 2 * deep] = got[ch][1, ry * 8 + rx * 2 + r]

    def forward(ch, b):
        load_candidates(ch, b)
        q = full[:, b].reshape(queries, width)
        logit[ch][b] = lax.dot_general(
            cand[...], q, (((1,), (1,)), ((), ())), preferred_element_type=f32) * scale
        peak = jnp.full((1, queries), NEG, f32)
        for i in range(cands):
            block = logit[ch][b, i * 2 * deep:(i + 1) * 2 * deep]
            peak = jnp.maximum(peak, jnp.max(block, axis=0, keepdims=True))
            top = jnp.max(block, axis=1, keepdims=True)
            lse = top + jnp.log(jnp.sum(jnp.exp(block - top), axis=1, keepdims=True))
            if i == 0:
                hit = wide_lane == true_row(ch, wide_sub) + me.inner * rows
                own_sum[...] += jnp.sum(jnp.where(hit, block, 0.0))
            row = jnp.sum(jnp.where(lax.rem(lane, 64) == true_row(ch, sub), lse, 0.0), axis=0,
                          keepdims=True)
            if ch:
                row = row + cols[b, i:i + 1]
            cols[b, i:i + 1] = row
        total = jnp.zeros((1, queries), f32)
        for i in range(cands):
            block = logit[ch][b, i * 2 * deep:(i + 1) * 2 * deep]
            total = total + jnp.sum(jnp.exp(block - peak), axis=0, keepdims=True)
        row_part[ch, pl.ds(b, 1)] = peak + jnp.log(total)

    def run(fn, ch, start, stop):
        def step(b, carry):
            fn(ch, b)
            return carry

        lax.fori_loop(start, stop, step, 0)

    own_sum[...] = jnp.zeros(own_sum.shape, f32)
    for ch in range(chunks):
        last_one = ch == chunks - 1
        if last_one:
            if ch == 0:
                pass_on(ch, 1, 3)
            pass_on(ch, 2)
        for copy in arrivals[ch]:
            copy.wait_recv()
        if ch == 0:
            for copy in pair:
                copy.wait_recv()
            keep.wait()
        run(forward, ch, 0, two)
        if not last_one:
            pass_on(ch + 1, 1, 3)
        run(forward, ch, two, per)

    def fold(values):
        top = jnp.max(values, axis=0)
        return top + jnp.log(jnp.sum(jnp.exp(values - top[None]), axis=0))

    rows_mine = fold(row_part[...])
    row_src[...] = rows_mine
    stat_waits = [net.send(row_src, all_rows.at[me.inner], to, all_rows.at[origin])
                  for to, origin in zip(in_peers, in_from)]
    line = lax.broadcasted_iota(jnp.int32, (32, 128), 0)
    side = lax.broadcasted_iota(jnp.int32, (32, 128), 1) // 64
    home = line + 32 * side

    def block_of(b, i):
        return me.dp * per + b if i == 0 else lists[me.dp * per + b, i - 1]

    def raise_peak(b, peak):
        for i in range(cands):
            peak = jnp.where(home == block_of(b, i), jnp.maximum(peak, cols[b, i:i + 1]), peak)
        return peak

    peaks = lax.fori_loop(0, per, raise_peak, jnp.full((32, 128), NEG, f32))

    def add_mass(b, mass):
        for i in range(cands):
            mass = mass + jnp.where(home == block_of(b, i), jnp.exp(cols[b, i:i + 1] - peaks), 0.0)
        return mass

    mass = lax.fori_loop(0, per, add_mass, jnp.zeros((32, 128), f32))
    dense_mine = jnp.where(mass > 0.0, peaks + jnp.log(jnp.where(mass > 0.0, mass, 1.0)), NEG)
    dense_src[...] = dense_mine
    stat_waits += [net.send(dense_src, all_dense.at[me.dp], to, all_dense.at[origin])
                   for to, origin in zip(dp_peers, dp_from)]
    all_rows[me.inner] = rows_mine
    all_dense[me.dp] = dense_mine
    for copy in stat_waits:
        copy.wait_recv()
    rows_all, dense_all = fold(all_rows[...]), fold(all_dense[...])
    row_lse[...] = rows_all
    pass_lse[...] = dense_all
    where = lax.broadcasted_iota(jnp.int32, rows_all.shape, 1) // rows
    local = jnp.sum(jnp.where(where == me.inner, rows_all, 0.0))
    local = local + jnp.sum(jnp.where(home // per == me.dp, dense_all, 0.0))
    loss_mid[0] = local - 2.0 * own_sum[...]

    def weigh(ch, b):
        q = full[:, b].reshape(queries, width)
        row = row_lse[pl.ds(b, 1)]
        for i in range(cands):
            block = block_of(b, i)
            values = pass_lse[pl.ds(lax.rem(block, 32), 1)]
            pick = lane == true_row(ch, sub) + (block // 32) * 64
            col = jnp.sum(jnp.where(pick, values, 0.0), axis=1, keepdims=True)
            z = logit[ch][b, i * 2 * deep:(i + 1) * 2 * deep]
            probs = 0.5 * jnp.exp(z - row) + 0.5 * jnp.exp(z - col)
            if i == 0:
                hit = wide_lane == true_row(ch, wide_sub) + me.inner * rows
                probs = probs - jnp.where(hit, 1.0, 0.0)
            weight[ch][b, i * 2 * deep:(i + 1) * 2 * deep] = probs.astype(b16)
        out = jnp.dot(weight[ch][b], q, preferred_element_type=f32)
        prod[ch][b] = out.reshape(2 * cands, deep, width)

    send_rows, parts = {}, {(h, rf): [] for h in (0, 1) for rf in range(SIDE)}

    def emit(ch, rf):
        for h, (f, t) in enumerate(HALVES):
            def slot(i, carry, h=h, f=f):
                rt, c = i // CAP, lax.rem(i, CAP)
                owner = me.group(f, rf, rt)
                block = owner * per + table[me.dp, owner * CAP + c]
                acc = jnp.zeros((deep, width), f32)
                for b in range(per):
                    k = spot[me.dp * per + b, block]
                    live = (k >= 0).astype(f32)
                    acc = acc + prod[ch][b, 2 * (jnp.maximum(k, 0) + 1) + h] * live
                part[ch, h, rt * 8 + rf * CAP + c] = acc.astype(b16)
                return carry

            lax.fori_loop(CAP if rf == 0 else 0, SIDE * CAP, slot, 0)
            up, down = me.move(t, 1), me.move(t, -1)
            rel = pl.ds(ch * deep, deep)
            send_rows[ch, h, rf] = (
                net.send(part.at[ch, h, 16 + rf * CAP], relay2.at[ch, h, 0, rf], up),
                net.send(part.at[ch, h, 16 + rf * CAP + 1], relay2.at[ch, h, 1, rf], down))
            parts[h, rf] += [
                net.send(part.at[ch, h, pl.ds(8 + rf * CAP, CAP)], seen[h][2][rf].at[:, rel], up),
                net.send(part.at[ch, h, pl.ds(24 + rf * CAP, CAP)], seen[h][0][rf].at[:, rel],
                         down)]

    def forward_parts(ch, *rfs):
        for rf in rfs:
            for h, (f, t) in enumerate(HALVES):
                for side_, copy in enumerate(send_rows[ch, h, rf]):
                    copy.wait_recv()
                    parts[h, rf].append(net.send(
                        relay2.at[ch, h, side_, rf],
                        seen[h][1][rf].at[side_, pl.ds(ch * deep, deep)],
                        me.move(t, 1 - 2 * side_)))

    for ch in range(chunks):
        run(weigh, ch, 0, per)
        for rf in (2, 1, 3, 0):
            emit(ch, rf)

    loss_waits = [net.send(loss_mid.at[0], loss_dp.at[me.dp], to, loss_dp.at[origin])
                  for to, origin in zip(dp_peers, dp_from)]
    loss_dp[me.dp] = loss_mid[0]

    def query_grad(_, b):
        acc = None
        for ch in range(chunks):
            load_candidates(ch, b)
            grad = lax.dot_general(weight[ch][b], cand[...], (((0,), (0,)), ((), ())),
                                   preferred_element_type=f32)
            acc = grad if acc is None else acc + grad
        query_part[:, b] = acc.astype(b16).reshape(inners, rows, width)

    swaps = {}

    def swap(lo):
        for dz in (2, 1, 3, 0):
            src = query_part.at[mod4(me.z + dz) * 2 + 1 - me.c, pl.ds(lo, two)]
            swaps[dz, lo] = net.send(src, pair_in.at[dz, pl.ds(lo, two)], me.move("core", 0))

    def join(dz, lo):
        swaps[dz, lo].wait_recv()
        slot = mod4(me.z + dz) * 2 + me.c

        def step(j, carry):
            both = query_part[slot, j].astype(f32) + pair_in[dz, j].astype(f32)
            qsum[dz, j] = both.astype(b16)
            return carry

        lax.fori_loop(lo, lo + two, step, 0)

    def fold_in(target, rd, source, start):
        def step(j, carry):
            both = target[rd, start + j].astype(f32) + source[j].astype(f32)
            target[rd, start + j] = both.astype(b16)
            return carry

        lax.fori_loop(0, two, step, 0)

    run(query_grad, 0, 0, two)
    swap(0)
    forward_parts(0, 2)
    run(query_grad, 0, two, per)
    swap(two)
    forward_parts(0, 1, 3)
    join(2, 0)
    za = net.send(qsum.at[2, 0:two], zmerge.at[0], me.move("z", 1))
    join(2, two)
    zb = net.send(qsum.at[2, two:per], zmerge.at[1], me.move("z", -1))
    for lo in (0, two):
        join(1, lo)
        join(3, lo)
    forward_parts(0, 0)
    for ch in range(1, chunks):
        forward_parts(ch, 2)
    za.wait_recv()
    fold_in(qsum, 1, zmerge.at[0], 0)
    z_up = net.send(qsum.at[1], zlast.at[0], me.move("z", 1))
    zb.wait_recv()
    fold_in(qsum, 3, zmerge.at[1], two)
    z_down = net.send(qsum.at[3], zlast.at[1], me.move("z", -1))
    for copy in loss_waits:
        copy.wait_recv()
    mid = jnp.sum(loss_dp[...], axis=0)
    loss_mid[1] = mid
    loss_waits = [net.send(loss_mid.at[1], loss_inner.at[me.inner], to, loss_inner.at[origin])
                  for to, origin in zip(in_peers, in_from)]
    loss_inner[me.inner] = mid

    def collect(h, rf, j):
        f, t = HALVES[h]
        owner = me.group(f, rf, 0)
        acc = [jnp.zeros((deep, width), f32) for _ in range(chunks)]
        for st in range(SIDE):
            if st == 0 and rf == 0:
                continue
            r = rank[me.group(f, 0, st), owner * per + j]
            live = (r >= 0).astype(f32)
            c = jnp.maximum(r, 0)
            for ch in range(chunks):
                if st == 0:
                    block = part[ch, h, rf * CAP + c]
                else:
                    block = seen[h][st - 1][rf][c, ch * deep:(ch + 1) * deep]
                acc[ch] = acc[ch] + block.astype(f32) * live
        return acc

    def gather_parts(h, rf):
        for copy in parts[h, rf]:
            copy.wait_recv()

        def step(j, carry):
            for ch, acc in enumerate(collect(h, rf, j)):
                dense[h, rf - 1, j, ch * deep:(ch + 1) * deep] = acc.astype(b16)
            return carry

        lax.fori_loop(0, per, step, 0)

    merges = {}
    for ch in range(1, chunks):
        forward_parts(ch, 1, 3)
    for h, (f, t) in enumerate(HALVES):
        gather_parts(h, 2)
        merges[h] = [net.send(dense.at[h, 1, 0:two], merge.at[h, 0], me.move(f, 1)),
                     net.send(dense.at[h, 1, two:per], merge.at[h, 1], me.move(f, -1))]
    for ch in range(1, chunks):
        forward_parts(ch, 0)
    ends = []
    for h, (f, t) in enumerate(HALVES):
        for rf, slot in ((1, 0), (3, 1)):
            gather_parts(h, rf)
            merges[h][slot].wait_recv()
            fold_in(dense.at[h], rf - 1, merge.at[h, slot], slot * two)
            ends.append(net.send(dense.at[h, rf - 1], last.at[h, slot],
                                 me.move(f, 1 if slot == 0 else -1)))
    for lo in (0, two):
        swaps[0, lo].wait_recv()
    z_up.wait_recv()
    z_down.wait_recv()
    mine = me.z * 2 + me.c

    def finish_query(j, carry):
        both = query_part[mine, j].astype(f32) + pair_in[0, j].astype(f32)
        both = both + zlast[0, j].astype(f32) + zlast[1, j].astype(f32)
        qg_ref[j] = both.astype(b16)
        return carry

    lax.fori_loop(0, per, finish_query, 0)
    for copy in loss_waits:
        copy.wait_recv()
    loss_out[...] = jnp.sum(loss_inner[...], axis=0) * (1.0 / count)
    for copy in parts[0, 0] + parts[1, 0] + ends:
        copy.wait_recv()
    for h in (0, 1):
        def finish(j, carry, h=h):
            for ch, acc in enumerate(collect(h, 0, j)):
                near_rows = slice(ch * deep, (ch + 1) * deep)
                acc = acc + prod[ch][j, h]
                acc = acc + last[h, 0, j, near_rows].astype(f32)
                acc = acc + last[h, 1, j, near_rows].astype(f32)
                pg_ref[j, h * half + ch * deep:h * half + (ch + 1) * deep] = acc.astype(b16)
            return carry

        lax.fori_loop(0, per, finish, 0)
    net.drain()


def split_list(items, counts):
    out, start = [], 0
    for n in counts:
        out.append(tuple(items[start:start + n]))
        start += n
    return out


def tables(neg_lists, groups, per):
    blocks = neg_lists.shape[0]
    ids = jnp.arange(blocks, dtype=jnp.int32)
    lists = neg_lists.reshape(groups, -1)
    present = jnp.any(lists[:, :, None] == ids[None, None, :], axis=1)
    quads = present.reshape(groups, groups, per).astype(jnp.int32)
    earlier = (jnp.arange(per)[:, None] < jnp.arange(per)[None, :]).astype(jnp.int32)
    rank = jnp.sum(quads[:, :, :, None] * earlier[None, None], axis=2)
    rank = jnp.where(quads == 1, rank, -1)
    slot = jnp.arange(CAP, dtype=jnp.int32)
    local = jnp.arange(per, dtype=jnp.int32)
    block = jnp.sum(
        jnp.where(rank[..., None] == slot, local[None, None, :, None], 0), axis=2)
    order = jnp.arange(neg_lists.shape[1], dtype=jnp.int32)
    match = neg_lists[:, :, None] == ids[None, None, :]
    spot = jnp.max(jnp.where(match, order[None, :, None], -1), axis=1)
    return rank.reshape(groups, blocks), block.reshape(groups, groups * CAP), spot


CHUNKS = 1


def body(queries, passages, neg_lists):
    per, rows, width = queries.shape
    groups, inners = lax.axis_size("dp"), lax.axis_size("inner")
    picks = neg_lists.shape[1]
    half, two = rows // 2, per // 2
    slots = groups * CAP
    chunks = CHUNKS
    deep = half // chunks
    cands, full_rows = picks + 1, rows * inners
    tall = cands * 2 * deep
    b16, f32 = jnp.bfloat16, jnp.float32
    sds = jax.ShapeDtypeStruct
    rank, block, spot = tables(neg_lists, groups, per)
    v = pltpu.VMEM
    sem_count = 100 + 160 * chunks
    need = {
        "full": [v((inners, per, rows, width), b16)],
        "stage": [v((chunks, 2, SIDE - 1, SIDE, CAP, deep, width), b16)],
        "relay": [v((chunks, 2, 2, SIDE, deep, width), b16)],
        "relay2": [v((chunks, 2, 2, SIDE, deep, width), b16)],
        "got": [v((2, slots, deep, width), b16)] * chunks,
        "logit": [v((per, tall, full_rows), f32)] * chunks,
        "weight": [v((per, tall, full_rows), b16)] * chunks,
        "prod": [v((per, 2 * cands, deep, width), f32)] * chunks,
        "cand": [v((tall, width), b16)],
        "cols": [v((per, cands, 128), f32)],
        "row_part": [v((chunks, per, full_rows), f32)],
        "row_src": [v((per, full_rows), f32)],
        "dense_src": [v((32, 128), f32)],
        "all_rows": [v((inners, per, full_rows), f32)],
        "all_dense": [v((groups, 32, 128), f32)],
        "row_lse": [v((per, full_rows), f32)],
        "pass_lse": [v((32, 128), f32)],
        "part": [v((chunks, 2, slots, deep, width), b16)],
        "query_part": [v((inners, per, rows, width), b16)],
        "own_sum": [v((8, 128), f32)],
        "dense": [v((2, SIDE - 1, per, half, width), b16)],
        "merge": [v((2, 2, two, half, width), b16)],
        "last": [v((2, 2, per, half, width), b16)],
        "pair_in": [v((SIDE, per, rows, width), b16)],
        "qsum": [v((SIDE, per, rows, width), b16)],
        "zmerge": [v((2, two, rows, width), b16)],
        "zlast": [v((2, per, rows, width), b16)],
        "loss_dp": [v((groups, 8, 128), f32)],
        "loss_inner": [v((inners, 8, 128), f32)],
        "loss_mid": [v((2, 8, 128), f32)],
        "near": [v((per, deep, width), b16)] * (2 * 3 * chunks),
        "seen": [v((CAP, half, width), b16)] * (2 * 3 * SIDE),
        "send_sem": [pltpu.SemaphoreType.DMA((sem_count,))],
        "recv_sem": [pltpu.SemaphoreType.DMA((sem_count,))],
        "local_sem": [pltpu.SemaphoreType.DMA],
    }
    spec = {name: len(refs) for name, refs in need.items()}
    loss, query_grad, passage_grad = pl.pallas_call(
        functools.partial(fused_kernel, (chunks, groups, inners), spec),
        out_shape=(sds((8, 128), f32), sds((per, rows, width), b16), sds((per, rows, width), b16)),
        in_specs=[SM, SM, SM, SM, VM, VM], out_specs=(VM, VM, VM),
        scratch_shapes=[ref for refs in need.values() for ref in refs],
        compiler_params=pltpu.CompilerParams(
            vmem_limit_bytes=VMEM_LIMIT, collective_id=0, has_side_effects=True),
        name="fused",
    )(block, rank, spot, neg_lists, queries, passages)
    return (loss[0, 0], query_grad, passage_grad)


def solution(mesh):
    in_specs = (P("dp", "inner", None), P("dp", "inner", None), P())
    out_specs = (P(), P("dp", "inner", None), P("dp", "inner", None))
    return jax.shard_map(body, mesh=mesh, in_specs=in_specs, out_specs=out_specs, check_vma=False)
```

```python
import functools
import math

import jax
import jax.numpy as jnp
from jax import lax
from jax.experimental import pallas as pl
from jax.experimental.pallas import tpu as pltpu
from jax.sharding import PartitionSpec as P

MESH = pl.DeviceIdType.MESH
NEG = -1e30
SIDE = 4
CAP = 2
VMEM_LIMIT = 62 * 1024 * 1024

VM = pl.BlockSpec(memory_space=pltpu.VMEM)
SM = pl.BlockSpec(memory_space=pltpu.SMEM)
AN = pl.BlockSpec(memory_space=pl.ANY)


def mod4(v):
    return lax.rem(v + SIDE, SIDE)


class Place:
    def __init__(self):
        self.dp = lax.axis_index("dp")
        self.inner = lax.axis_index("inner")
        self.y, self.x = self.dp // SIDE, lax.rem(self.dp, SIDE)
        self.z, self.c = self.inner // 2, lax.rem(self.inner, 2)

    def move(self, axis, step):
        if axis == "x":
            return (self.y * SIDE + mod4(self.x + step), self.inner)
        if axis == "y":
            return (mod4(self.y + step) * SIDE + self.x, self.inner)
        if axis == "z":
            return (self.dp, mod4(self.z + step) * 2 + self.c)
        return (self.dp, self.z * 2 + (1 - self.c))

    def group(self, first, rf, rt):
        if first == "y":
            return mod4(self.y + rf) * SIDE + mod4(self.x + rt)
        return mod4(self.y + rt) * SIDE + mod4(self.x + rf)


class Copies:
    def __init__(self, send_sem, recv_sem):
        self.send_sem, self.recv_sem, self.count, self.made = send_sem, recv_sem, 0, []

    def send(self, src, dst, device, landing=None):
        i = self.count
        self.count += 1
        copy = pltpu.make_async_remote_copy(
            src_ref=src, dst_ref=dst, send_sem=self.send_sem.at[i], recv_sem=self.recv_sem.at[i],
            device_id=device, device_id_type=MESH)
        copy.start()
        self.made.append(copy)
        if landing is None:
            return copy
        return pltpu.make_async_remote_copy(
            src_ref=src, dst_ref=landing, send_sem=self.send_sem.at[i],
            recv_sem=self.recv_sem.at[i], device_id=device, device_id_type=MESH)

    def drain(self):
        for copy in self.made:
            copy.wait_send()


def neighbours(me):
    return [me.move(a, s) for a in "xyz" for s in (1, -1)] + [me.move("core", 0)]


HALVES = (("y", "x"), ("x", "y"))


def fused_kernel(dims, spec, list_ref, q_hbm, p_hbm, loss_out, qg_hbm, pg_hbm, *scratch):
    chunks, groups, inners = dims
    me = Place()
    per, rows, width = p_hbm.shape
    half, two = rows // 2, per // 2
    deep = half // chunks
    picks = list_ref.shape[1]
    cands = picks + 1
    queries = inners * rows
    slots = groups * CAP
    f32, b16 = jnp.float32, jnp.bfloat16
    scale = 1.0 / math.sqrt(width)
    count = 2.0 * groups * per * queries
    take = dict(zip(spec, split_list(scratch, spec.values())))
    one = lambda name: take[name][0]
    full, stage, relay, relay2 = one("full"), one("stage"), one("relay"), one("relay2")
    got, logit, weight, prod = take["got"], take["logit"], take["weight"], take["prod"]
    cand, cols, row_part = one("cand"), one("cols"), one("row_part")
    row_src, dense_src, all_rows = one("row_src"), one("dense_src"), one("all_rows")
    all_dense, row_lse, pass_lse = one("all_dense"), one("row_lse"), one("pass_lse")
    part, query_part, own_sum = one("part"), one("query_part"), one("own_sum")
    dense, merge, last = one("dense"), one("merge"), one("last")
    pair_in, qsum, zmerge, zlast = one("pair_in"), one("qsum"), one("zmerge"), one("zlast")
    loss_dp, loss_inner, loss_mid = one("loss_dp"), one("loss_inner"), one("loss_mid")
    near = [[(None,) + take["near"][(ch * 2 + h) * 3:(ch * 2 + h) * 3 + 3] for h in (0, 1)]
            for ch in range(chunks)]
    seen = [[take["seen"][(h * 3 + st) * SIDE:(h * 3 + st + 1) * SIDE] for st in range(3)]
            for h in (0, 1)]
    net = Copies(one("send_sem"), one("recv_sem"))

    dp_peers = [(lax.rem(me.dp + o, groups), me.inner) for o in range(1, groups)]
    dp_from = [lax.rem(me.dp - o + groups, groups) for o in range(1, groups)]
    in_peers = [(me.dp, lax.rem(me.inner + o, inners)) for o in range(1, inners)]
    in_from = [lax.rem(me.inner - o + inners, inners) for o in range(1, inners)]
    p_ref, qg_ref, pg_ref = one("p_own"), one("qg"), one("pg")
    local = one("local_sem")
    mine = me.z * 2 + me.c
    own_slot = full.at[mine]
    load_q = pltpu.make_async_copy(q_hbm, own_slot, local.at[0])
    load_p = pltpu.make_async_copy(p_hbm, p_ref, local.at[1])
    load_q.start()
    load_p.start()
    barrier = pltpu.get_barrier_semaphore()
    near_devices = neighbours(me)
    for device in near_devices:
        pl.semaphore_signal(barrier, inc=1, device_id=device, device_id_type=MESH)

    tab_v, tab_s, spot_v, spot_s = one("tab_v"), one("tab_s"), one("spot_v"), one("spot_s")
    every = list_ref[...]
    blocks = every.shape[0]
    lanes = lax.broadcasted_iota(jnp.int32, (blocks, 128), 1)
    spots = jnp.full((blocks, 128), -1, jnp.int32)
    for k in range(picks):
        entry = every[:, k:k + 1]
        spots = jnp.where(entry == lanes, k, spots)
        spots = jnp.where(lanes == blocks + k, entry, spots)
    spots = spots.reshape(groups, per, 128)
    present = jnp.max(jnp.where(spots >= 0, 1, 0), axis=1)
    quad = lax.rem(lax.broadcasted_iota(jnp.int32, (groups, 128), 1), per)
    earlier = jnp.zeros((groups, 128), jnp.int32)
    for j in range(1, per):
        earlier = earlier + jnp.where(quad >= j, pltpu.roll(present, j, 1), 0)
    ranks = jnp.where(present == 1, earlier, -1)
    tab_v[0] = ranks
    for c in range(CAP):
        first_of = jnp.zeros((groups, 128), jnp.int32)
        for j in range(1, per):
            first_of = first_of + jnp.where(pltpu.roll(ranks, 128 - j, 1) == c, j, 0)
        tab_v[1 + c] = first_of
    spot_v[...] = spots
    tab_copy = pltpu.make_async_copy(tab_v, tab_s, local.at[2])
    spot_copy = pltpu.make_async_copy(spot_v.at[me.dp], spot_s, local.at[3])
    tab_copy.start()
    spot_copy.start()

    def rank_of(group, block):
        return tab_s[0, group, block]

    def pick_of(group, source, c):
        return tab_s[1 + c, group, source * per]

    def listed(b, k):
        return spot_s[b, blocks + k]

    pl.semaphore_wait(barrier, len(near_devices))
    load_p.wait()

    span = lambda h, ch: pl.ds(h * half + ch * deep, deep)
    first, second, relays, arrivals = {}, {}, {}, {ch: [] for ch in range(chunks)}

    def send_own(ch):
        for h, (f, t) in enumerate(HALVES):
            mine = p_ref.at[:, span(h, ch)]
            first[ch, h] = (net.send(mine, near[ch][h][3], me.move(f, 1)),
                            net.send(mine, near[ch][h][1], me.move(f, -1)))

    def send_second(ch):
        for h, (f, t) in enumerate(HALVES):
            up, down = first[ch, h]
            up.wait_recv()
            a = net.send(near[ch][h][3].at[0:two], near[ch][h][2].at[0:two], me.move(f, 1))
            down.wait_recv()
            b = net.send(near[ch][h][1].at[two:per], near[ch][h][2].at[two:per], me.move(f, -1))
            second[ch, h] = (a, b)

    def spread(ch, rf):
        for h, (f, t) in enumerate(HALVES):
            if rf == 2:
                for copy in second[ch, h]:
                    copy.wait_recv()
            source = me.group(f, rf, 0)
            for dt in (2, 1, 3, 0):
                if dt == 0 and rf == 0:
                    got[ch][h, 0:CAP] = jnp.zeros((CAP, deep, width), b16)
                    continue
                group = me.group(f, 0, dt)
                for c in range(CAP):
                    pick = pick_of(group, source, c)
                    block = p_ref[pick, span(h, ch)] if rf == 0 else near[ch][h][rf][pick]
                    if dt == 0:
                        got[ch][h, rf * CAP + c] = block
                    else:
                        stage[ch, h, dt - 1, rf, c] = block
            up, down = me.move(t, 1), me.move(t, -1)
            relays[ch, h, rf] = (
                net.send(stage.at[ch, h, 1, rf, 0], relay.at[ch, h, 0, rf], up),
                net.send(stage.at[ch, h, 1, rf, 1], relay.at[ch, h, 1, rf], down))
            arrivals[ch].append(net.send(
                stage.at[ch, h, 0, rf], got[ch].at[h, pl.ds(24 + rf * CAP, CAP)], up))
            arrivals[ch].append(net.send(
                stage.at[ch, h, 2, rf], got[ch].at[h, pl.ds(8 + rf * CAP, CAP)], down))

    def pass_on(ch, *rfs):
        for rf in rfs:
            for h, (f, t) in enumerate(HALVES):
                for side, copy in enumerate(relays[ch, h, rf]):
                    copy.wait_recv()
                    arrivals[ch].append(net.send(
                        relay.at[ch, h, side, rf], got[ch].at[h, 16 + rf * CAP + side],
                        me.move(t, 1 - 2 * side)))

    at = lambda z, c: full.at[mod4(z) * 2 + c]
    send_own(0)
    load_q.wait()
    z_up = net.send(own_slot, own_slot, me.move("z", 1), at(me.z - 1, me.c))
    z_down = net.send(own_slot, own_slot, me.move("z", -1), at(me.z + 1, me.c))
    pair = [net.send(own_slot, own_slot, me.move("core", 0), at(me.z, 1 - me.c))]
    tab_copy.wait()
    spot_copy.wait()
    spread(0, 0)
    for ch in range(1, chunks):
        send_own(ch)
    send_second(0)
    spread(0, 1)
    spread(0, 3)
    z_up.wait_recv()
    behind, ahead = at(me.z - 1, me.c), at(me.z + 1, me.c)
    across = mod4(me.z + 2) * 2
    far = full.at[across + me.c]
    za = net.send(behind.at[0:two], behind.at[0:two], me.move("z", 1), far.at[0:two])
    pair.append(net.send(behind, behind, me.move("core", 0), at(me.z - 1, 1 - me.c)))
    z_down.wait_recv()
    zb = net.send(ahead.at[two:per], ahead.at[two:per], me.move("z", -1), far.at[two:per])
    pair.append(net.send(ahead, ahead, me.move("core", 0), at(me.z + 1, 1 - me.c)))
    pass_on(0, 0)
    for ch in range(1, chunks):
        send_second(ch)
    spread(0, 2)
    for ch in range(1, chunks):
        spread(ch, 0)
        pass_on(ch - 1, 1, 3)
        spread(ch, 1)
        spread(ch, 3)
        if ch == 1:
            za.wait_recv()
            zb.wait_recv()
            pair.append(
                net.send(far, far, me.move("core", 0), full.at[across + 1 - me.c]))
        pass_on(ch - 1, 2)
        spread(ch, 2)
        pass_on(ch, 0)
    if chunks == 1:
        za.wait_recv()
        zb.wait_recv()
        pair.append(net.send(far, far, me.move("core", 0), full.at[across + 1 - me.c]))

    lane = lax.broadcasted_iota(jnp.int32, (2 * deep, 128), 1)
    sub = lax.broadcasted_iota(jnp.int32, (2 * deep, 128), 0)
    wide_lane = lax.broadcasted_iota(jnp.int32, (2 * deep, queries), 1)
    wide_sub = lax.broadcasted_iota(jnp.int32, (2 * deep, queries), 0)

    def true_row(ch, sub):
        return (sub // deep) * half + ch * deep + lax.rem(sub, deep)

    def load_candidates(ch, b):
        cand[0:deep] = p_ref[b, span(0, ch)]
        cand[deep:2 * deep] = p_ref[b, span(1, ch)]
        for k in range(picks):
            block = listed(b, k)
            group = block // per
            r = rank_of(me.dp, block)
            ry = mod4(group // SIDE - me.y)
            rx = mod4(lax.rem(group, SIDE) - me.x)
            base = 2 * deep * (k + 1)
            cand[base:base + deep] = got[ch][0, rx * 8 + ry * 2 + r]
            cand[base + deep:base + 2 * deep] = got[ch][1, ry * 8 + rx * 2 + r]

    def forward(ch, b):
        load_candidates(ch, b)
        q = full[:, b].reshape(queries, width)
        logit[ch][b] = lax.dot_general(
            cand[...], q, (((1,), (1,)), ((), ())), preferred_element_type=f32) * scale
        peak = jnp.full((1, queries), NEG, f32)
        for i in range(cands):
            block = logit[ch][b, i * 2 * deep:(i + 1) * 2 * deep]
            peak = jnp.maximum(peak, jnp.max(block, axis=0, keepdims=True))
            top = jnp.max(block, axis=1, keepdims=True)
            lse = top + jnp.log(jnp.sum(jnp.exp(block - top), axis=1, keepdims=True))
            if i == 0:
                hit = wide_lane == true_row(ch, wide_sub) + me.inner * rows
                own_sum[...] += jnp.sum(jnp.where(hit, block, 0.0))
            row = jnp.sum(jnp.where(lax.rem(lane, 64) == true_row(ch, sub), lse, 0.0), axis=0,
                          keepdims=True)
            if ch:
                row = row + cols[b, i:i + 1]
            cols[b, i:i + 1] = row
        total = jnp.zeros((1, queries), f32)
        for i in range(cands):
            block = logit[ch][b, i * 2 * deep:(i + 1) * 2 * deep]
            total = total + jnp.sum(jnp.exp(block - peak), axis=0, keepdims=True)
        row_part[ch, pl.ds(b, 1)] = peak + jnp.log(total)

    def run(fn, ch, start, stop):
        def step(b, carry):
            fn(ch, b)
            return carry

        lax.fori_loop(start, stop, step, 0)

    own_sum[...] = jnp.zeros(own_sum.shape, f32)
    for ch in range(chunks):
        last_one = ch == chunks - 1
        if last_one:
            if ch == 0:
                pass_on(ch, 1, 3)
            pass_on(ch, 2)
        for copy in arrivals[ch]:
            copy.wait_recv()
        if ch == 0:
            for copy in pair:
                copy.wait_recv()
        run(forward, ch, 0, two)
        if not last_one:
            pass_on(ch + 1, 1, 3)
        run(forward, ch, two, per)

    def fold(values):
        top = jnp.max(values, axis=0)
        return top + jnp.log(jnp.sum(jnp.exp(values - top[None]), axis=0))

    rows_mine = fold(row_part[...])
    row_src[...] = rows_mine
    stat_waits = [net.send(row_src, all_rows.at[me.inner], to, all_rows.at[origin])
                  for to, origin in zip(in_peers, in_from)]
    line = lax.broadcasted_iota(jnp.int32, (32, 128), 0)
    side = lax.broadcasted_iota(jnp.int32, (32, 128), 1) // 64
    home = line + 32 * side

    def block_of(b, i):
        return me.dp * per + b if i == 0 else listed(b, i - 1)

    def raise_peak(b, peak):
        for i in range(cands):
            peak = jnp.where(home == block_of(b, i), jnp.maximum(peak, cols[b, i:i + 1]), peak)
        return peak

    peaks = lax.fori_loop(0, per, raise_peak, jnp.full((32, 128), NEG, f32))

    def add_mass(b, mass):
        for i in range(cands):
            mass = mass + jnp.where(home == block_of(b, i), jnp.exp(cols[b, i:i + 1] - peaks), 0.0)
        return mass

    mass = lax.fori_loop(0, per, add_mass, jnp.zeros((32, 128), f32))
    dense_mine = jnp.where(mass > 0.0, peaks + jnp.log(jnp.where(mass > 0.0, mass, 1.0)), NEG)
    dense_src[...] = dense_mine
    stat_waits += [net.send(dense_src, all_dense.at[me.dp], to, all_dense.at[origin])
                   for to, origin in zip(dp_peers, dp_from)]
    all_rows[me.inner] = rows_mine
    all_dense[me.dp] = dense_mine
    for copy in stat_waits:
        copy.wait_recv()
    rows_all, dense_all = fold(all_rows[...]), fold(all_dense[...])
    row_lse[...] = rows_all
    pass_lse[...] = dense_all
    where = lax.broadcasted_iota(jnp.int32, rows_all.shape, 1) // rows
    loss_own = jnp.sum(jnp.where(where == me.inner, rows_all, 0.0))
    loss_own = loss_own + jnp.sum(jnp.where(home // per == me.dp, dense_all, 0.0))
    loss_mid[0] = loss_own - 2.0 * own_sum[...]

    def weigh(ch, b):
        q = full[:, b].reshape(queries, width)
        row = row_lse[pl.ds(b, 1)]
        for i in range(cands):
            block = block_of(b, i)
            values = pass_lse[pl.ds(lax.rem(block, 32), 1)]
            pick = lane == true_row(ch, sub) + (block // 32) * 64
            col = jnp.sum(jnp.where(pick, values, 0.0), axis=1, keepdims=True)
            z = logit[ch][b, i * 2 * deep:(i + 1) * 2 * deep]
            probs = 0.5 * jnp.exp(z - row) + 0.5 * jnp.exp(z - col)
            if i == 0:
                hit = wide_lane == true_row(ch, wide_sub) + me.inner * rows
                probs = probs - jnp.where(hit, 1.0, 0.0)
            weight[ch][b, i * 2 * deep:(i + 1) * 2 * deep] = probs.astype(b16)
        out = jnp.dot(weight[ch][b], q, preferred_element_type=f32)
        prod[ch][b] = out.reshape(2 * cands, deep, width)

    send_rows, parts = {}, {(h, rf): [] for h in (0, 1) for rf in range(SIDE)}

    def emit(ch, rf):
        for h, (f, t) in enumerate(HALVES):
            def slot(i, carry, h=h, f=f):
                rt, c = i // CAP, lax.rem(i, CAP)
                owner = me.group(f, rf, rt)
                block = owner * per + jnp.where(
                    c == 0, pick_of(me.dp, owner, 0), pick_of(me.dp, owner, 1))
                acc = jnp.zeros((deep, width), f32)
                for b in range(per):
                    k = spot_s[b, block]
                    live = (k >= 0).astype(f32)
                    acc = acc + prod[ch][b, 2 * (jnp.maximum(k, 0) + 1) + h] * live
                part[ch, h, rt * 8 + rf * CAP + c] = acc.astype(b16)
                return carry

            lax.fori_loop(CAP if rf == 0 else 0, SIDE * CAP, slot, 0)
            up, down = me.move(t, 1), me.move(t, -1)
            rel = pl.ds(ch * deep, deep)
            send_rows[ch, h, rf] = (
                net.send(part.at[ch, h, 16 + rf * CAP], relay2.at[ch, h, 0, rf], up),
                net.send(part.at[ch, h, 16 + rf * CAP + 1], relay2.at[ch, h, 1, rf], down))
            parts[h, rf] += [
                net.send(part.at[ch, h, pl.ds(8 + rf * CAP, CAP)], seen[h][2][rf].at[:, rel], up),
                net.send(part.at[ch, h, pl.ds(24 + rf * CAP, CAP)], seen[h][0][rf].at[:, rel],
                         down)]

    def forward_parts(ch, *rfs):
        for rf in rfs:
            for h, (f, t) in enumerate(HALVES):
                for side_, copy in enumerate(send_rows[ch, h, rf]):
                    copy.wait_recv()
                    parts[h, rf].append(net.send(
                        relay2.at[ch, h, side_, rf],
                        seen[h][1][rf].at[side_, pl.ds(ch * deep, deep)],
                        me.move(t, 1 - 2 * side_)))

    for ch in range(chunks):
        run(weigh, ch, 0, per)
        for rf in (2, 1, 3, 0):
            emit(ch, rf)

    loss_waits = [net.send(loss_mid.at[0], loss_dp.at[me.dp], to, loss_dp.at[origin])
                  for to, origin in zip(dp_peers, dp_from)]
    loss_dp[me.dp] = loss_mid[0]

    def query_grad(_, b):
        acc = None
        for ch in range(chunks):
            load_candidates(ch, b)
            grad = lax.dot_general(weight[ch][b], cand[...], (((0,), (0,)), ((), ())),
                                   preferred_element_type=f32)
            acc = grad if acc is None else acc + grad
        query_part[:, b] = acc.astype(b16).reshape(inners, rows, width)

    swaps = {}

    def swap(lo):
        for dz in (2, 1, 3, 0):
            src = query_part.at[mod4(me.z + dz) * 2 + 1 - me.c, pl.ds(lo, two)]
            swaps[dz, lo] = net.send(src, pair_in.at[dz, pl.ds(lo, two)], me.move("core", 0))

    def join(dz, lo):
        swaps[dz, lo].wait_recv()
        slot = mod4(me.z + dz) * 2 + me.c

        def step(j, carry):
            both = query_part[slot, j].astype(f32) + pair_in[dz, j].astype(f32)
            qsum[dz, j] = both.astype(b16)
            return carry

        lax.fori_loop(lo, lo + two, step, 0)

    def fold_in(target, rd, source, start):
        def step(j, carry):
            both = target[rd, start + j].astype(f32) + source[j].astype(f32)
            target[rd, start + j] = both.astype(b16)
            return carry

        lax.fori_loop(0, two, step, 0)

    run(query_grad, 0, 0, two)
    swap(0)
    forward_parts(0, 2)
    run(query_grad, 0, two, per)
    swap(two)
    forward_parts(0, 1, 3)
    join(2, 0)
    za = net.send(qsum.at[2, 0:two], zmerge.at[0], me.move("z", 1))
    join(2, two)
    zb = net.send(qsum.at[2, two:per], zmerge.at[1], me.move("z", -1))
    for lo in (0, two):
        join(1, lo)
        join(3, lo)
    forward_parts(0, 0)
    for ch in range(1, chunks):
        forward_parts(ch, 2)
    za.wait_recv()
    fold_in(qsum, 1, zmerge.at[0], 0)
    z_up = net.send(qsum.at[1], zlast.at[0], me.move("z", 1))
    zb.wait_recv()
    fold_in(qsum, 3, zmerge.at[1], two)
    z_down = net.send(qsum.at[3], zlast.at[1], me.move("z", -1))
    for copy in loss_waits:
        copy.wait_recv()
    mid = jnp.sum(loss_dp[...], axis=0)
    loss_mid[1] = mid
    loss_waits = [net.send(loss_mid.at[1], loss_inner.at[me.inner], to, loss_inner.at[origin])
                  for to, origin in zip(in_peers, in_from)]
    loss_inner[me.inner] = mid

    def collect(h, rf, j):
        f, t = HALVES[h]
        owner = me.group(f, rf, 0)
        acc = [jnp.zeros((deep, width), f32) for _ in range(chunks)]
        for st in range(SIDE):
            if st == 0 and rf == 0:
                continue
            r = rank_of(me.group(f, 0, st), owner * per + j)
            live = (r >= 0).astype(f32)
            c = jnp.maximum(r, 0)
            for ch in range(chunks):
                if st == 0:
                    block = part[ch, h, rf * CAP + c]
                else:
                    block = seen[h][st - 1][rf][c, ch * deep:(ch + 1) * deep]
                acc[ch] = acc[ch] + block.astype(f32) * live
        return acc

    def gather_parts(h, rf):
        for copy in parts[h, rf]:
            copy.wait_recv()

        def step(j, carry):
            for ch, acc in enumerate(collect(h, rf, j)):
                dense[h, rf - 1, j, ch * deep:(ch + 1) * deep] = acc.astype(b16)
            return carry

        lax.fori_loop(0, per, step, 0)

    merges = {}
    for ch in range(1, chunks):
        forward_parts(ch, 1, 3)
    for h, (f, t) in enumerate(HALVES):
        gather_parts(h, 2)
        merges[h] = [net.send(dense.at[h, 1, 0:two], merge.at[h, 0], me.move(f, 1)),
                     net.send(dense.at[h, 1, two:per], merge.at[h, 1], me.move(f, -1))]
    for ch in range(1, chunks):
        forward_parts(ch, 0)
    ends = []
    for h, (f, t) in enumerate(HALVES):
        for rf, slot in ((1, 0), (3, 1)):
            gather_parts(h, rf)
            merges[h][slot].wait_recv()
            fold_in(dense.at[h], rf - 1, merge.at[h, slot], slot * two)
            ends.append(net.send(dense.at[h, rf - 1], last.at[h, slot],
                                 me.move(f, 1 if slot == 0 else -1)))
    for lo in (0, two):
        swaps[0, lo].wait_recv()
    z_up.wait_recv()
    z_down.wait_recv()
    def finish_query(j, carry):
        both = query_part[mine, j].astype(f32) + pair_in[0, j].astype(f32)
        both = both + zlast[0, j].astype(f32) + zlast[1, j].astype(f32)
        qg_ref[j] = both.astype(b16)
        return carry

    lax.fori_loop(0, per, finish_query, 0)
    store_q = pltpu.make_async_copy(qg_ref, qg_hbm, local.at[0])
    store_q.start()
    for copy in loss_waits:
        copy.wait_recv()
    loss_out[...] = jnp.sum(loss_inner[...], axis=0) * (1.0 / count)
    for copy in parts[0, 0] + parts[1, 0] + ends:
        copy.wait_recv()
    for h in (0, 1):
        def finish(j, carry, h=h):
            for ch, acc in enumerate(collect(h, 0, j)):
                near_rows = slice(ch * deep, (ch + 1) * deep)
                acc = acc + prod[ch][j, h]
                acc = acc + last[h, 0, j, near_rows].astype(f32)
                acc = acc + last[h, 1, j, near_rows].astype(f32)
                pg_ref[j, h * half + ch * deep:h * half + (ch + 1) * deep] = acc.astype(b16)
            return carry

        lax.fori_loop(0, per, finish, 0)
    store_p = pltpu.make_async_copy(pg_ref, pg_hbm, local.at[1])
    store_p.start()
    net.drain()
    store_q.wait()
    store_p.wait()


def split_list(items, counts):
    out, start = [], 0
    for n in counts:
        out.append(tuple(items[start:start + n]))
        start += n
    return out


def finish_kernel(loss_ref, q_ref, p_ref, loss_out, q_out, p_out, q_buf, p_buf, sem):
    loads = [pltpu.make_async_copy(a, b, sem.at[i])
             for i, (a, b) in enumerate(((q_ref, q_buf), (p_ref, p_buf)))]
    stores = [pltpu.make_async_copy(b, a, sem.at[2 + i])
              for i, (a, b) in enumerate(((q_out, q_buf), (p_out, p_buf)))]
    for copy in loads:
        copy.start()
    loss_out[0, 0] = loss_ref[0, 0]
    for copy, after in zip(loads, stores):
        copy.wait()
        after.start()
    for copy in stores:
        copy.wait()


CHUNKS = 1


def body(queries, passages, neg_lists):
    per, rows, width = queries.shape
    groups, inners = lax.axis_size("dp"), lax.axis_size("inner")
    picks = neg_lists.shape[1]
    half, two = rows // 2, per // 2
    slots = groups * CAP
    chunks = CHUNKS
    deep = half // chunks
    cands, full_rows = picks + 1, rows * inners
    tall = cands * 2 * deep
    b16, f32 = jnp.bfloat16, jnp.float32
    sds = jax.ShapeDtypeStruct
    v = pltpu.VMEM
    sem_count = 100 + 160 * chunks
    need = {
        "full": [v((inners, per, rows, width), b16)],
        "stage": [v((chunks, 2, SIDE - 1, SIDE, CAP, deep, width), b16)],
        "relay": [v((chunks, 2, 2, SIDE, deep, width), b16)],
        "relay2": [v((chunks, 2, 2, SIDE, deep, width), b16)],
        "got": [v((2, slots, deep, width), b16)] * chunks,
        "logit": [v((per, tall, full_rows), f32)] * chunks,
        "weight": [v((per, tall, full_rows), b16)] * chunks,
        "prod": [v((per, 2 * cands, deep, width), f32)] * chunks,
        "cand": [v((tall, width), b16)],
        "cols": [v((per, cands, 128), f32)],
        "row_part": [v((chunks, per, full_rows), f32)],
        "row_src": [v((per, full_rows), f32)],
        "dense_src": [v((32, 128), f32)],
        "all_rows": [v((inners, per, full_rows), f32)],
        "all_dense": [v((groups, 32, 128), f32)],
        "row_lse": [v((per, full_rows), f32)],
        "pass_lse": [v((32, 128), f32)],
        "part": [v((chunks, 2, slots, deep, width), b16)],
        "query_part": [v((inners, per, rows, width), b16)],
        "own_sum": [v((8, 128), f32)],
        "dense": [v((2, SIDE - 1, per, half, width), b16)],
        "merge": [v((2, 2, two, half, width), b16)],
        "last": [v((2, 2, per, half, width), b16)],
        "pair_in": [v((SIDE, per, rows, width), b16)],
        "qsum": [v((SIDE, per, rows, width), b16)],
        "zmerge": [v((2, two, rows, width), b16)],
        "zlast": [v((2, per, rows, width), b16)],
        "loss_dp": [v((groups, 8, 128), f32)],
        "loss_inner": [v((inners, 8, 128), f32)],
        "loss_mid": [v((2, 8, 128), f32)],
        "near": [v((per, deep, width), b16)] * (2 * 3 * chunks),
        "seen": [v((CAP, half, width), b16)] * (2 * 3 * SIDE),
        "send_sem": [pltpu.SemaphoreType.DMA((sem_count,))],
        "recv_sem": [pltpu.SemaphoreType.DMA((sem_count,))],
        "local_sem": [pltpu.SemaphoreType.DMA((4,))],
        "p_own": [v((per, rows, width), b16)],
        "qg": [v((per, rows, width), b16)],
        "pg": [v((per, rows, width), b16)],
        "tab_v": [v((1 + CAP, groups, 128), jnp.int32)],
        "tab_s": [pltpu.SMEM((1 + CAP, groups, 128), jnp.int32)],
        "spot_v": [v((groups, per, 128), jnp.int32)],
        "spot_s": [pltpu.SMEM((per, 128), jnp.int32)],
    }
    spec = {name: len(refs) for name, refs in need.items()}
    loss, query_grad, passage_grad = pl.pallas_call(
        functools.partial(fused_kernel, (chunks, groups, inners), spec),
        out_shape=(sds((8, 128), f32), sds((per, rows, width), b16), sds((per, rows, width), b16)),
        in_specs=[VM, AN, AN], out_specs=(VM, AN, AN),
        scratch_shapes=[ref for refs in need.values() for ref in refs],
        compiler_params=pltpu.CompilerParams(
            vmem_limit_bytes=VMEM_LIMIT, collective_id=0, has_side_effects=True),
        name="fused",
    )(neg_lists, queries, passages)
    shape = (per, rows, width)
    loss, query_grad, passage_grad = pl.pallas_call(
        finish_kernel,
        out_shape=(sds((1, 1), f32), sds(shape, b16), sds(shape, b16)),
        in_specs=[SM, AN, AN], out_specs=(SM, AN, AN),
        scratch_shapes=[v(shape, b16), v(shape, b16), pltpu.SemaphoreType.DMA((4,))],
        name="finish",
    )(loss, query_grad, passage_grad)
    return (loss.reshape(()), query_grad, passage_grad)


def solution(mesh):
    in_specs = (P("dp", "inner", None), P("dp", "inner", None), P())
    out_specs = (P(), P("dp", "inner", None), P("dp", "inner", None))
    return jax.shard_map(body, mesh=mesh, in_specs=in_specs, out_specs=out_specs, check_vma=False)
```

```python
import functools
import math

import jax
import jax.numpy as jnp
from jax import lax
from jax.experimental import pallas as pl
from jax.experimental.pallas import tpu as pltpu
from jax.sharding import PartitionSpec as P

MESH = pl.DeviceIdType.MESH
NEG = -1e30
SIDE = 4
CAP = 2
VMEM_LIMIT = 62 * 1024 * 1024

VM = pl.BlockSpec(memory_space=pltpu.VMEM)
SM = pl.BlockSpec(memory_space=pltpu.SMEM)
AN = pl.BlockSpec(memory_space=pl.ANY)


def mod4(v):
    return lax.rem(v + SIDE, SIDE)


class Place:
    def __init__(self):
        self.dp = lax.axis_index("dp")
        self.inner = lax.axis_index("inner")
        self.y, self.x = self.dp // SIDE, lax.rem(self.dp, SIDE)
        self.z, self.c = self.inner // 2, lax.rem(self.inner, 2)

    def move(self, axis, step):
        if axis == "x":
            return (self.y * SIDE + mod4(self.x + step), self.inner)
        if axis == "y":
            return (mod4(self.y + step) * SIDE + self.x, self.inner)
        if axis == "z":
            return (self.dp, mod4(self.z + step) * 2 + self.c)
        return (self.dp, self.z * 2 + (1 - self.c))

    def group(self, first, rf, rt):
        if first == "y":
            return mod4(self.y + rf) * SIDE + mod4(self.x + rt)
        return mod4(self.y + rt) * SIDE + mod4(self.x + rf)


class Copies:
    def __init__(self, send_sem, recv_sem):
        self.send_sem, self.recv_sem, self.count, self.made = send_sem, recv_sem, 0, []

    def send(self, src, dst, device, landing=None):
        i = self.count
        self.count += 1
        copy = pltpu.make_async_remote_copy(
            src_ref=src, dst_ref=dst, send_sem=self.send_sem.at[i], recv_sem=self.recv_sem.at[i],
            device_id=device, device_id_type=MESH)
        copy.start()
        self.made.append(copy)
        if landing is None:
            return copy
        return pltpu.make_async_remote_copy(
            src_ref=src, dst_ref=landing, send_sem=self.send_sem.at[i],
            recv_sem=self.recv_sem.at[i], device_id=device, device_id_type=MESH)

    def drain(self):
        for copy in self.made:
            copy.wait_send()


def neighbours(me):
    return [me.move(a, s) for a in "xyz" for s in (1, -1)] + [me.move("core", 0)]


HALVES = (("y", "x"), ("x", "y"))


def fused_kernel(dims, spec, list_ref, q_hbm, p_hbm, loss_out, qg_hbm, pg_hbm, *scratch):
    chunks, groups, inners = dims
    me = Place()
    per, rows, width = p_hbm.shape
    half, two = rows // 2, per // 2
    deep = half // chunks
    picks = list_ref.shape[0]
    cands = picks + 1
    queries = inners * rows
    slots = groups * CAP
    f32, b16 = jnp.float32, jnp.bfloat16
    scale = 1.0 / math.sqrt(width)
    count = 2.0 * groups * per * queries
    take = dict(zip(spec, split_list(scratch, spec.values())))
    one = lambda name: take[name][0]
    full, stage, relay, relay2 = one("full"), one("stage"), one("relay"), one("relay2")
    got, logit, weight, prod = take["got"], take["logit"], take["weight"], take["prod"]
    cand, cols, row_part = take["cand"], one("cols"), one("row_part")
    row_src, dense_src, all_rows = one("row_src"), one("dense_src"), one("all_rows")
    all_dense, row_lse, pass_lse = one("all_dense"), one("row_lse"), one("pass_lse")
    part, query_part, own_sum = one("part"), one("query_part"), one("own_sum")
    dense, merge, last = one("dense"), one("merge"), one("last")
    pair_in, qsum, zmerge, zlast = one("pair_in"), one("qsum"), one("zmerge"), one("zlast")
    loss_dp, loss_inner, loss_mid = one("loss_dp"), one("loss_inner"), one("loss_mid")
    near = [[(None,) + take["near"][(ch * 2 + h) * 3:(ch * 2 + h) * 3 + 3] for h in (0, 1)]
            for ch in range(chunks)]
    seen = [[take["seen"][(h * 3 + st) * SIDE:(h * 3 + st + 1) * SIDE] for st in range(3)]
            for h in (0, 1)]
    net = Copies(one("send_sem"), one("recv_sem"))

    dp_peers = [(lax.rem(me.dp + o, groups), me.inner) for o in range(1, groups)]
    dp_from = [lax.rem(me.dp - o + groups, groups) for o in range(1, groups)]
    in_peers = [(me.dp, lax.rem(me.inner + o, inners)) for o in range(1, inners)]
    in_from = [lax.rem(me.inner - o + inners, inners) for o in range(1, inners)]
    p_ref, qg_ref, pg_ref = one("p_own"), one("qg"), one("pg")
    local = one("local_sem")
    mine = me.z * 2 + me.c
    own_slot = full.at[mine]
    load_q = pltpu.make_async_copy(q_hbm, own_slot, local.at[0])
    load_p = pltpu.make_async_copy(p_hbm, p_ref, local.at[1])
    load_q.start()
    load_p.start()
    barrier = pltpu.get_barrier_semaphore()
    near_devices = neighbours(me)
    for device in near_devices:
        pl.semaphore_signal(barrier, inc=1, device_id=device, device_id_type=MESH)

    tab_v, tab_s, spot_v, spot_s = one("tab_v"), one("tab_s"), one("spot_v"), one("spot_s")
    blocks = list_ref.shape[1]
    every = jnp.transpose(jnp.concatenate(
        [list_ref[...], jnp.zeros((picks, 128 - blocks), jnp.int32)], axis=1))[0:blocks]
    lanes = lax.broadcasted_iota(jnp.int32, (blocks, 128), 1)
    spots = jnp.full((blocks, 128), -1, jnp.int32)
    for k in range(picks):
        entry = every[:, k:k + 1]
        spots = jnp.where(entry == lanes, k, spots)
        spots = jnp.where(lanes == blocks + k, entry, spots)
    spots = spots.reshape(groups, per, 128)
    present = jnp.max(jnp.where(spots >= 0, 1, 0), axis=1)
    quad = lax.rem(lax.broadcasted_iota(jnp.int32, (groups, 128), 1), per)
    earlier = jnp.zeros((groups, 128), jnp.int32)
    for j in range(1, per):
        earlier = earlier + jnp.where(quad >= j, pltpu.roll(present, j, 1), 0)
    ranks = jnp.where(present == 1, earlier, -1)
    tab_v[0] = ranks
    for c in range(CAP):
        first_of = jnp.zeros((groups, 128), jnp.int32)
        for j in range(1, per):
            first_of = first_of + jnp.where(pltpu.roll(ranks, 128 - j, 1) == c, j, 0)
        tab_v[1 + c] = first_of
    spot_v[...] = spots
    tab_copy = pltpu.make_async_copy(tab_v, tab_s, local.at[2])
    spot_copy = pltpu.make_async_copy(spot_v.at[me.dp], spot_s, local.at[3])
    tab_copy.start()
    spot_copy.start()

    def rank_of(group, block):
        return tab_s[0, group, block]

    def pick_of(group, source, c):
        return tab_s[1 + c, group, source * per]

    def listed(b, k):
        return spot_s[b, blocks + k]

    pl.semaphore_wait(barrier, len(near_devices))
    load_p.wait()

    span = lambda h, ch: pl.ds(h * half + ch * deep, deep)
    first, second, relays, arrivals = {}, {}, {}, {ch: [] for ch in range(chunks)}

    def send_own(ch):
        for h, (f, t) in enumerate(HALVES):
            mine = p_ref.at[:, span(h, ch)]
            first[ch, h] = (net.send(mine, near[ch][h][3], me.move(f, 1)),
                            net.send(mine, near[ch][h][1], me.move(f, -1)))

    def send_second(ch):
        for h, (f, t) in enumerate(HALVES):
            up, down = first[ch, h]
            up.wait_recv()
            a = net.send(near[ch][h][3].at[0:two], near[ch][h][2].at[0:two], me.move(f, 1))
            down.wait_recv()
            b = net.send(near[ch][h][1].at[two:per], near[ch][h][2].at[two:per], me.move(f, -1))
            second[ch, h] = (a, b)

    def spread(ch, rf):
        for h, (f, t) in enumerate(HALVES):
            if rf == 2:
                for copy in second[ch, h]:
                    copy.wait_recv()
            source = me.group(f, rf, 0)
            for dt in (2, 1, 3, 0):
                if dt == 0 and rf == 0:
                    got[ch][h, 0:CAP] = jnp.zeros((CAP, deep, width), b16)
                    continue
                group = me.group(f, 0, dt)
                for c in range(CAP):
                    pick = pick_of(group, source, c)
                    block = p_ref[pick, span(h, ch)] if rf == 0 else near[ch][h][rf][pick]
                    if dt == 0:
                        got[ch][h, rf * CAP + c] = block
                    else:
                        stage[ch, h, dt - 1, rf, c] = block
            up, down = me.move(t, 1), me.move(t, -1)
            relays[ch, h, rf] = (
                net.send(stage.at[ch, h, 1, rf, 0], relay.at[ch, h, 0, rf], up),
                net.send(stage.at[ch, h, 1, rf, 1], relay.at[ch, h, 1, rf], down))
            arrivals[ch].append(net.send(
                stage.at[ch, h, 0, rf], got[ch].at[h, pl.ds(24 + rf * CAP, CAP)], up))
            arrivals[ch].append(net.send(
                stage.at[ch, h, 2, rf], got[ch].at[h, pl.ds(8 + rf * CAP, CAP)], down))

    def pass_on(ch, *rfs):
        for rf in rfs:
            for h, (f, t) in enumerate(HALVES):
                for side, copy in enumerate(relays[ch, h, rf]):
                    copy.wait_recv()
                    arrivals[ch].append(net.send(
                        relay.at[ch, h, side, rf], got[ch].at[h, 16 + rf * CAP + side],
                        me.move(t, 1 - 2 * side)))

    at = lambda z, c: full.at[mod4(z) * 2 + c]
    send_own(0)
    load_q.wait()
    z_up = net.send(own_slot, own_slot, me.move("z", 1), at(me.z - 1, me.c))
    z_down = net.send(own_slot, own_slot, me.move("z", -1), at(me.z + 1, me.c))
    pair = [net.send(own_slot, own_slot, me.move("core", 0), at(me.z, 1 - me.c))]
    tab_copy.wait()
    spot_copy.wait()
    spread(0, 0)
    for ch in range(1, chunks):
        send_own(ch)
    send_second(0)
    spread(0, 1)
    spread(0, 3)
    z_up.wait_recv()
    behind, ahead = at(me.z - 1, me.c), at(me.z + 1, me.c)
    across = mod4(me.z + 2) * 2
    far = full.at[across + me.c]
    za = net.send(behind.at[0:two], behind.at[0:two], me.move("z", 1), far.at[0:two])
    pair.append(net.send(behind, behind, me.move("core", 0), at(me.z - 1, 1 - me.c)))
    z_down.wait_recv()
    zb = net.send(ahead.at[two:per], ahead.at[two:per], me.move("z", -1), far.at[two:per])
    pair.append(net.send(ahead, ahead, me.move("core", 0), at(me.z + 1, 1 - me.c)))
    pass_on(0, 0)
    for ch in range(1, chunks):
        send_second(ch)
    spread(0, 2)
    for ch in range(1, chunks):
        spread(ch, 0)
        pass_on(ch - 1, 1, 3)
        spread(ch, 1)
        spread(ch, 3)
        if ch == 1:
            za.wait_recv()
            zb.wait_recv()
            pair.append(
                net.send(far, far, me.move("core", 0), full.at[across + 1 - me.c]))
        pass_on(ch - 1, 2)
        spread(ch, 2)
        pass_on(ch, 0)
    if chunks == 1:
        za.wait_recv()
        zb.wait_recv()
        pair.append(net.send(far, far, me.move("core", 0), full.at[across + 1 - me.c]))

    lane = lax.broadcasted_iota(jnp.int32, (2 * deep, 128), 1)
    sub = lax.broadcasted_iota(jnp.int32, (2 * deep, 128), 0)
    wide_lane = lax.broadcasted_iota(jnp.int32, (2 * deep, queries), 1)
    wide_sub = lax.broadcasted_iota(jnp.int32, (2 * deep, queries), 0)

    def true_row(ch, sub):
        return (sub // deep) * half + ch * deep + lax.rem(sub, deep)

    def load_candidates(b):
        to = cand[b % 2]
        to[0:half] = p_ref[b, 0:half]
        to[half:rows] = p_ref[b, half:rows]
        for k in range(picks):
            block = listed(b, k)
            group = block // per
            r = rank_of(me.dp, block)
            ry = mod4(group // SIDE - me.y)
            rx = mod4(lax.rem(group, SIDE) - me.x)
            base = rows * (k + 1)
            to[base:base + half] = got[0][0, rx * 8 + ry * 2 + r]
            to[base + half:base + rows] = got[0][1, ry * 8 + rx * 2 + r]

    def score(b):
        load_candidates(b)
        q = full[:, b].reshape(queries, width)
        logit[b][...] = lax.dot_general(
            cand[b % 2][...], q, (((1,), (1,)), ((), ())), preferred_element_type=f32) * scale

    def summarise(b):
        peak = jnp.full((1, queries), NEG, f32)
        for i in range(cands):
            block = logit[b][i * rows:(i + 1) * rows]
            peak = jnp.maximum(peak, jnp.max(block, axis=0, keepdims=True))
            top = jnp.max(block, axis=1, keepdims=True)
            lse = top + jnp.log(jnp.sum(jnp.exp(block - top), axis=1, keepdims=True))
            if i == 0:
                hit = wide_lane == wide_sub + me.inner * rows
                own_sum[...] += jnp.sum(jnp.where(hit, block, 0.0))
            cols[b, i:i + 1] = jnp.sum(jnp.where(lax.rem(lane, 64) == sub, lse, 0.0), axis=0,
                                       keepdims=True)
        total = jnp.zeros((1, queries), f32)
        for i in range(cands):
            block = logit[b][i * rows:(i + 1) * rows]
            total = total + jnp.sum(jnp.exp(block - peak), axis=0, keepdims=True)
        row_part[0, b:b + 1] = peak + jnp.log(total)

    own_sum[...] = jnp.zeros(own_sum.shape, f32)
    pass_on(0, 1, 3)
    pass_on(0, 2)
    for copy in arrivals[0] + pair:
        copy.wait_recv()
    score(0)
    for b in range(1, per):
        score(b)
        summarise(b - 1)
    summarise(per - 1)

    def fold(values):
        top = jnp.max(values, axis=0)
        return top + jnp.log(jnp.sum(jnp.exp(values - top[None]), axis=0))

    rows_mine = fold(row_part[...])
    row_src[...] = rows_mine
    stat_waits = [net.send(row_src, all_rows.at[me.inner], to, all_rows.at[origin])
                  for to, origin in zip(in_peers, in_from)]
    line = lax.broadcasted_iota(jnp.int32, (32, 128), 0)
    side = lax.broadcasted_iota(jnp.int32, (32, 128), 1) // 64
    home = line + 32 * side

    def block_of(b, i):
        return me.dp * per + b if i == 0 else listed(b, i - 1)

    def raise_peak(b, peak):
        for i in range(cands):
            peak = jnp.where(home == block_of(b, i), jnp.maximum(peak, cols[b, i:i + 1]), peak)
        return peak

    peaks = lax.fori_loop(0, per, raise_peak, jnp.full((32, 128), NEG, f32))

    def add_mass(b, mass):
        for i in range(cands):
            mass = mass + jnp.where(home == block_of(b, i), jnp.exp(cols[b, i:i + 1] - peaks), 0.0)
        return mass

    mass = lax.fori_loop(0, per, add_mass, jnp.zeros((32, 128), f32))
    dense_mine = jnp.where(mass > 0.0, peaks + jnp.log(jnp.where(mass > 0.0, mass, 1.0)), NEG)
    dense_src[...] = dense_mine
    stat_waits += [net.send(dense_src, all_dense.at[me.dp], to, all_dense.at[origin])
                   for to, origin in zip(dp_peers, dp_from)]
    all_rows[me.inner] = rows_mine
    all_dense[me.dp] = dense_mine
    for copy in stat_waits:
        copy.wait_recv()
    rows_all, dense_all = fold(all_rows[...]), fold(all_dense[...])
    row_lse[...] = rows_all
    pass_lse[...] = dense_all
    where = lax.broadcasted_iota(jnp.int32, rows_all.shape, 1) // rows
    loss_own = jnp.sum(jnp.where(where == me.inner, rows_all, 0.0))
    loss_own = loss_own + jnp.sum(jnp.where(home // per == me.dp, dense_all, 0.0))
    loss_mid[0] = loss_own - 2.0 * own_sum[...]

    def weigh(b):
        row = row_lse[b:b + 1]
        for i in range(cands):
            block = block_of(b, i)
            values = pass_lse[pl.ds(lax.rem(block, 32), 1)]
            pick = lane == sub + (block // 32) * 64
            col = jnp.sum(jnp.where(pick, values, 0.0), axis=1, keepdims=True)
            z = logit[b][i * rows:(i + 1) * rows]
            probs = 0.5 * jnp.exp(z - row) + 0.5 * jnp.exp(z - col)
            if i == 0:
                hit = wide_lane == wide_sub + me.inner * rows
                probs = probs - jnp.where(hit, 1.0, 0.0)
            weight[b][i * rows:(i + 1) * rows] = probs.astype(b16)

    def multiply(b):
        q = full[:, b].reshape(queries, width)
        out = jnp.dot(weight[b][...], q, preferred_element_type=f32)
        prod[b][...] = out.reshape(2 * cands, deep, width)

    send_rows, parts = {}, {(h, rf): [] for h in (0, 1) for rf in range(SIDE)}

    def emit(ch, rf):
        for h, (f, t) in enumerate(HALVES):
            def slot(i, carry, h=h, f=f):
                rt, c = i // CAP, lax.rem(i, CAP)
                owner = me.group(f, rf, rt)
                block = owner * per + jnp.where(
                    c == 0, pick_of(me.dp, owner, 0), pick_of(me.dp, owner, 1))
                acc = jnp.zeros((deep, width), f32)
                for b in range(per):
                    k = spot_s[b, block]
                    live = (k >= 0).astype(f32)
                    acc = acc + prod[b][2 * (jnp.maximum(k, 0) + 1) + h] * live
                part[ch, h, rt * 8 + rf * CAP + c] = acc.astype(b16)
                return carry

            lax.fori_loop(CAP if rf == 0 else 0, SIDE * CAP, slot, 0)
            up, down = me.move(t, 1), me.move(t, -1)
            rel = pl.ds(ch * deep, deep)
            send_rows[ch, h, rf] = (
                net.send(part.at[ch, h, 16 + rf * CAP], relay2.at[ch, h, 0, rf], up),
                net.send(part.at[ch, h, 16 + rf * CAP + 1], relay2.at[ch, h, 1, rf], down))
            parts[h, rf] += [
                net.send(part.at[ch, h, pl.ds(8 + rf * CAP, CAP)], seen[h][2][rf].at[:, rel], up),
                net.send(part.at[ch, h, pl.ds(24 + rf * CAP, CAP)], seen[h][0][rf].at[:, rel],
                         down)]

    def forward_parts(ch, *rfs):
        for rf in rfs:
            for h, (f, t) in enumerate(HALVES):
                for side_, copy in enumerate(send_rows[ch, h, rf]):
                    copy.wait_recv()
                    parts[h, rf].append(net.send(
                        relay2.at[ch, h, side_, rf],
                        seen[h][1][rf].at[side_, pl.ds(ch * deep, deep)],
                        me.move(t, 1 - 2 * side_)))

    def query_grad(b):
        load_candidates(b)
        grad = lax.dot_general(weight[b][...], cand[b % 2][...], (((0,), (0,)), ((), ())),
                               preferred_element_type=f32)
        query_part[:, b] = grad.astype(b16).reshape(inners, rows, width)

    swaps = {}

    def swap(lo):
        for dz in (2, 1, 3, 0):
            src = query_part.at[mod4(me.z + dz) * 2 + 1 - me.c, pl.ds(lo, two)]
            swaps[dz, lo] = net.send(src, pair_in.at[dz, pl.ds(lo, two)], me.move("core", 0))

    def join(dz, lo):
        swaps[dz, lo].wait_recv()
        slot = mod4(me.z + dz) * 2 + me.c

        def step(j, carry):
            both = query_part[slot, j].astype(f32) + pair_in[dz, j].astype(f32)
            qsum[dz, j] = both.astype(b16)
            return carry

        lax.fori_loop(lo, lo + two, step, 0)

    def fold_in(target, rd, source, start):
        def step(j, carry):
            both = target[rd, start + j].astype(f32) + source[j].astype(f32)
            target[rd, start + j] = both.astype(b16)
            return carry

        lax.fori_loop(0, two, step, 0)

    def collect(h, rf, j):
        f, t = HALVES[h]
        owner = me.group(f, rf, 0)
        acc = [jnp.zeros((deep, width), f32) for _ in range(chunks)]
        for st in range(SIDE):
            if st == 0 and rf == 0:
                continue
            r = rank_of(me.group(f, 0, st), owner * per + j)
            live = (r >= 0).astype(f32)
            c = jnp.maximum(r, 0)
            for ch in range(chunks):
                if st == 0:
                    block = part[ch, h, rf * CAP + c]
                else:
                    block = seen[h][st - 1][rf][c, ch * deep:(ch + 1) * deep]
                acc[ch] = acc[ch] + block.astype(f32) * live
        return acc

    def gather_parts(h, rf):
        for copy in parts[h, rf]:
            copy.wait_recv()

        def step(j, carry):
            for ch, acc in enumerate(collect(h, rf, j)):
                dense[h, rf - 1, j, ch * deep:(ch + 1) * deep] = acc.astype(b16)
            return carry

        lax.fori_loop(0, per, step, 0)

    merges, ends = {}, []
    weigh(0)
    for b in range(1, per):
        multiply(b - 1)
        weigh(b)
    multiply(per - 1)
    emit(0, 2)
    emit(0, 1)
    loss_waits = [net.send(loss_mid.at[0], loss_dp.at[me.dp], to, loss_dp.at[origin])
                  for to, origin in zip(dp_peers, dp_from)]
    loss_dp[me.dp] = loss_mid[0]
    for b in range(0, two):
        query_grad(b)
    swap(0)
    forward_parts(0, 2)
    emit(0, 3)
    for b in range(two, per):
        query_grad(b)
    swap(two)
    forward_parts(0, 1)
    join(2, 0)
    za = net.send(qsum.at[2, 0:two], zmerge.at[0], me.move("z", 1))
    join(2, two)
    zb = net.send(qsum.at[2, two:per], zmerge.at[1], me.move("z", -1))
    forward_parts(0, 3)
    for h, (f, t) in enumerate(HALVES):
        gather_parts(h, 2)
        merges[h] = [net.send(dense.at[h, 1, 0:two], merge.at[h, 0], me.move(f, 1)),
                     net.send(dense.at[h, 1, two:per], merge.at[h, 1], me.move(f, -1))]
    emit(0, 0)
    for lo in (0, two):
        join(1, lo)
        join(3, lo)
    za.wait_recv()
    fold_in(qsum, 1, zmerge.at[0], 0)
    z_up = net.send(qsum.at[1], zlast.at[0], me.move("z", 1))
    zb.wait_recv()
    fold_in(qsum, 3, zmerge.at[1], two)
    z_down = net.send(qsum.at[3], zlast.at[1], me.move("z", -1))
    for rf, slot in ((1, 0), (3, 1)):
        for h, (f, t) in enumerate(HALVES):
            gather_parts(h, rf)
            merges[h][slot].wait_recv()
            fold_in(dense.at[h], rf - 1, merge.at[h, slot], slot * two)
            ends.append(net.send(dense.at[h, rf - 1], last.at[h, slot],
                                 me.move(f, 1 if slot == 0 else -1)))
    forward_parts(0, 0)
    for copy in loss_waits:
        copy.wait_recv()
    mid = jnp.sum(loss_dp[...], axis=0)
    loss_mid[1] = mid
    loss_waits = [net.send(loss_mid.at[1], loss_inner.at[me.inner], to, loss_inner.at[origin])
                  for to, origin in zip(in_peers, in_from)]
    loss_inner[me.inner] = mid
    for lo in (0, two):
        swaps[0, lo].wait_recv()
    z_up.wait_recv()
    z_down.wait_recv()
    def finish_query(j, carry):
        both = query_part[mine, j].astype(f32) + pair_in[0, j].astype(f32)
        both = both + zlast[0, j].astype(f32) + zlast[1, j].astype(f32)
        qg_ref[j] = both.astype(b16)
        return carry

    lax.fori_loop(0, per, finish_query, 0)
    store_q = pltpu.make_async_copy(qg_ref, qg_hbm, local.at[0])
    store_q.start()
    for copy in loss_waits:
        copy.wait_recv()
    loss_out[0, 0] = jnp.max(jnp.sum(loss_inner[...], axis=0)) * (1.0 / count)
    for copy in parts[0, 0] + parts[1, 0] + ends:
        copy.wait_recv()
    for h in (0, 1):
        for j in range(per):
            acc = collect(h, 0, j)[0] + prod[j][h]
            acc = acc + last[h, 0, j].astype(f32) + last[h, 1, j].astype(f32)
            pg_ref[j, h * half:(h + 1) * half] = acc.astype(b16)
    store_p = pltpu.make_async_copy(pg_ref, pg_hbm, local.at[1])
    store_p.start()
    net.drain()
    store_q.wait()
    store_p.wait()


def split_list(items, counts):
    out, start = [], 0
    for n in counts:
        out.append(tuple(items[start:start + n]))
        start += n
    return out


def finish_kernel(loss_ref, q_ref, p_ref, loss_out, q_out, p_out, loss_buf, q_buf, p_buf, sem):
    moves = [(loss_ref, loss_buf, loss_out)]
    for j in range(q_ref.shape[0]):
        moves += [(q_ref.at[j], q_buf.at[j], q_out.at[j]), (p_ref.at[j], p_buf.at[j], p_out.at[j])]
    loads = [pltpu.make_async_copy(a, b, sem.at[0, i]) for i, (a, b, c) in enumerate(moves)]
    stores = [pltpu.make_async_copy(b, c, sem.at[1, i]) for i, (a, b, c) in enumerate(moves)]
    for copy in loads:
        copy.start()
    for copy, after in zip(loads, stores):
        copy.wait()
        after.start()
    for copy in stores:
        copy.wait()


CHUNKS = 1


def body(queries, passages, neg_lists):
    per, rows, width = queries.shape
    groups, inners = lax.axis_size("dp"), lax.axis_size("inner")
    picks = neg_lists.shape[1]
    half, two = rows // 2, per // 2
    slots = groups * CAP
    chunks = CHUNKS
    deep = half // chunks
    cands, full_rows = picks + 1, rows * inners
    tall = cands * 2 * deep
    b16, f32 = jnp.bfloat16, jnp.float32
    sds = jax.ShapeDtypeStruct
    v = pltpu.VMEM
    sem_count = 100 + 160 * chunks
    need = {
        "full": [v((inners, per, rows, width), b16)],
        "stage": [v((chunks, 2, SIDE - 1, SIDE, CAP, deep, width), b16)],
        "relay": [v((chunks, 2, 2, SIDE, deep, width), b16)],
        "relay2": [v((chunks, 2, 2, SIDE, deep, width), b16)],
        "got": [v((2, slots, deep, width), b16)] * chunks,
        "logit": [v((tall, full_rows), f32)] * per,
        "weight": [v((tall, full_rows), b16)] * per,
        "prod": [v((2 * cands, deep, width), f32)] * per,
        "cand": [v((tall, width), b16)] * 2,
        "cols": [v((per, cands, 128), f32)],
        "row_part": [v((chunks, per, full_rows), f32)],
        "row_src": [v((per, full_rows), f32)],
        "dense_src": [v((32, 128), f32)],
        "all_rows": [v((inners, per, full_rows), f32)],
        "all_dense": [v((groups, 32, 128), f32)],
        "row_lse": [v((per, full_rows), f32)],
        "pass_lse": [v((32, 128), f32)],
        "part": [v((chunks, 2, slots, deep, width), b16)],
        "query_part": [v((inners, per, rows, width), b16)],
        "own_sum": [v((8, 128), f32)],
        "dense": [v((2, SIDE - 1, per, half, width), b16)],
        "merge": [v((2, 2, two, half, width), b16)],
        "last": [v((2, 2, per, half, width), b16)],
        "pair_in": [v((SIDE, per, rows, width), b16)],
        "qsum": [v((SIDE, per, rows, width), b16)],
        "zmerge": [v((2, two, rows, width), b16)],
        "zlast": [v((2, per, rows, width), b16)],
        "loss_dp": [v((groups, 8, 128), f32)],
        "loss_inner": [v((inners, 8, 128), f32)],
        "loss_mid": [v((2, 8, 128), f32)],
        "near": [v((per, deep, width), b16)] * (2 * 3 * chunks),
        "seen": [v((CAP, half, width), b16)] * (2 * 3 * SIDE),
        "send_sem": [pltpu.SemaphoreType.DMA((sem_count,))],
        "recv_sem": [pltpu.SemaphoreType.DMA((sem_count,))],
        "local_sem": [pltpu.SemaphoreType.DMA((4,))],
        "p_own": [v((per, rows, width), b16)],
        "qg": [v((per, rows, width), b16)],
        "pg": [v((per, rows, width), b16)],
        "tab_v": [v((1 + CAP, groups, 128), jnp.int32)],
        "tab_s": [pltpu.SMEM((1 + CAP, groups, 128), jnp.int32)],
        "spot_v": [v((groups, per, 128), jnp.int32)],
        "spot_s": [pltpu.SMEM((per, 128), jnp.int32)],
    }
    spec = {name: len(refs) for name, refs in need.items()}
    loss, query_grad, passage_grad = pl.pallas_call(
        functools.partial(fused_kernel, (chunks, groups, inners), spec),
        out_shape=(sds((1, 1), f32), sds((per, rows, width), b16), sds((per, rows, width), b16)),
        in_specs=[VM, AN, AN], out_specs=(SM, AN, AN),
        scratch_shapes=[ref for refs in need.values() for ref in refs],
        compiler_params=pltpu.CompilerParams(
            vmem_limit_bytes=VMEM_LIMIT, collective_id=0, has_side_effects=True),
        name="fused",
    )(neg_lists.T, queries, passages)
    shape = (per, rows, width)
    loss, query_grad, passage_grad = pl.pallas_call(
        finish_kernel,
        out_shape=(sds((1, 1), f32), sds(shape, b16), sds(shape, b16)),
        in_specs=[AN, AN, AN], out_specs=(AN, AN, AN),
        scratch_shapes=[pltpu.SMEM((1, 1), f32), v(shape, b16), v(shape, b16),
                        pltpu.SemaphoreType.DMA((2, 1 + 2 * per))],
        name="finish",
    )(loss, query_grad, passage_grad)
    return (loss.reshape(()), query_grad, passage_grad)


def solution(mesh):
    in_specs = (P("dp", "inner", None), P("dp", "inner", None), P())
    out_specs = (P(), P("dp", "inner", None), P("dp", "inner", None))
    return jax.shard_map(body, mesh=mesh, in_specs=in_specs, out_specs=out_specs, check_vma=False)
```

```python
import functools
import math

import jax
import jax.numpy as jnp
from jax import lax
from jax.experimental import pallas as pl
from jax.experimental.pallas import tpu as pltpu
from jax.sharding import PartitionSpec as P

MESH = pl.DeviceIdType.MESH
NEG = -1e30
SIDE = 4
CAP = 2
VMEM_LIMIT = 62 * 1024 * 1024

VM = pl.BlockSpec(memory_space=pltpu.VMEM)
SM = pl.BlockSpec(memory_space=pltpu.SMEM)
AN = pl.BlockSpec(memory_space=pl.ANY)


def mod4(v):
    return lax.rem(v + SIDE, SIDE)


class Place:
    def __init__(self):
        self.dp = lax.axis_index("dp")
        self.inner = lax.axis_index("inner")
        self.y, self.x = self.dp // SIDE, lax.rem(self.dp, SIDE)
        self.z, self.c = self.inner // 2, lax.rem(self.inner, 2)

    def move(self, axis, step):
        if axis == "x":
            return (self.y * SIDE + mod4(self.x + step), self.inner)
        if axis == "y":
            return (mod4(self.y + step) * SIDE + self.x, self.inner)
        if axis == "z":
            return (self.dp, mod4(self.z + step) * 2 + self.c)
        return (self.dp, self.z * 2 + (1 - self.c))

    def group(self, first, rf, rt):
        if first == "y":
            return mod4(self.y + rf) * SIDE + mod4(self.x + rt)
        return mod4(self.y + rt) * SIDE + mod4(self.x + rf)


class Copies:
    def __init__(self, send_sem, recv_sem):
        self.send_sem, self.recv_sem, self.count, self.made = send_sem, recv_sem, 0, []

    def send(self, src, dst, device, landing=None):
        i = self.count
        self.count += 1
        copy = pltpu.make_async_remote_copy(
            src_ref=src, dst_ref=dst, send_sem=self.send_sem.at[i], recv_sem=self.recv_sem.at[i],
            device_id=device, device_id_type=MESH)
        copy.start()
        self.made.append(copy)
        if landing is None:
            return copy
        return pltpu.make_async_remote_copy(
            src_ref=src, dst_ref=landing, send_sem=self.send_sem.at[i],
            recv_sem=self.recv_sem.at[i], device_id=device, device_id_type=MESH)

    def drain(self):
        for copy in self.made:
            copy.wait_send()


def neighbours(me):
    return [me.move(a, s) for a in "xyz" for s in (1, -1)] + [me.move("core", 0)]


HUBS = ((0, 1), (0, 3), (1, 1), (3, 3), (2, 3))
TREE = (
    ((0, 1), (0, 0), "x", 1), ((0, 3), (0, 0), "x", -1), ((1, 1), (0, 1), "y", 1),
    ((3, 3), (0, 3), "y", -1), ((2, 3), (3, 3), "y", -1), ((1, 0), (0, 0), "y", 1),
    ((3, 1), (0, 1), "y", -1), ((0, 2), (0, 3), "x", -1), ((1, 3), (0, 3), "y", 1),
    ((1, 2), (1, 1), "x", 1), ((2, 1), (1, 1), "y", 1), ((3, 0), (3, 3), "x", 1),
    ((3, 2), (3, 3), "x", -1), ((2, 0), (2, 3), "x", 1), ((2, 2), (2, 3), "x", -1))


def turn(h, node):
    return node if h == 0 else node[::-1]


HALVES = (("y", "x"), ("x", "y"))


def fused_kernel(dims, spec, list_ref, q_hbm, p_hbm, loss_out, qg_hbm, pg_hbm, *scratch):
    chunks, groups, inners = dims
    me = Place()
    per, rows, width = p_hbm.shape
    half, two = rows // 2, per // 2
    deep = half // chunks
    picks = list_ref.shape[0]
    cands = picks + 1
    queries = inners * rows
    slots = groups * CAP
    f32, b16 = jnp.float32, jnp.bfloat16
    ln2 = math.log(2.0)
    scale = 1.0 / (math.sqrt(width) * ln2)
    count = 2.0 * groups * per * queries
    take = dict(zip(spec, split_list(scratch, spec.values())))
    one = lambda name: take[name][0]
    full, stage, relay2 = one("full"), one("stage"), one("relay2")
    got, logit, weight, prod = take["got"], take["logit"], take["weight"], take["prod"]
    cand, cols, row_part = take["cand"], one("cols"), one("row_part")
    row_src, dense_src, all_rows = one("row_src"), one("dense_src"), one("all_rows")
    all_dense, row_lse, pass_lse = one("all_dense"), one("row_lse"), one("pass_lse")
    part, query_part, own_sum = one("part"), one("query_part"), one("own_sum")
    dense, merge, last = one("dense"), one("merge"), one("last")
    pair_in, qsum, zmerge, zlast = one("pair_in"), one("qsum"), one("zmerge"), one("zlast")
    loss_dp, loss_inner, loss_mid = one("loss_dp"), one("loss_inner"), one("loss_mid")
    near = [dict(zip(HUBS, take["near"][h * len(HUBS):(h + 1) * len(HUBS)])) for h in (0, 1)]
    seen = [[take["seen"][(h * 3 + st) * SIDE:(h * 3 + st + 1) * SIDE] for st in range(3)]
            for h in (0, 1)]
    net = Copies(one("send_sem"), one("recv_sem"))

    dp_peers = [(lax.rem(me.dp + o, groups), me.inner) for o in range(1, groups)]
    dp_from = [lax.rem(me.dp - o + groups, groups) for o in range(1, groups)]
    in_peers = [(me.dp, lax.rem(me.inner + o, inners)) for o in range(1, inners)]
    in_from = [lax.rem(me.inner - o + inners, inners) for o in range(1, inners)]
    p_ref, qg_ref, pg_ref = one("p_own"), one("qg"), one("pg")
    local = one("local_sem")
    mine = me.z * 2 + me.c
    own_slot = full.at[mine]
    load_q = pltpu.make_async_copy(q_hbm, own_slot, local.at[0])
    load_p = pltpu.make_async_copy(p_hbm, p_ref, local.at[1])
    load_q.start()
    load_p.start()
    barrier = pltpu.get_barrier_semaphore()
    near_devices = neighbours(me)
    for device in near_devices:
        pl.semaphore_signal(barrier, inc=1, device_id=device, device_id_type=MESH)

    pl.semaphore_wait(barrier, len(near_devices))
    load_p.wait()

    whole = lambda h: pl.ds(h * half, half)
    pieces = (0, two)
    hub_in, arrivals = {}, []

    def away(h, node):
        dy, dx = turn(h, node)
        return mod4(me.y + dy) * SIDE + mod4(me.x + dx)

    def toward(h, axis, step):
        return me.move(axis if h == 0 else {"x": "y", "y": "x"}[axis], step)

    def slot_from(h, node):
        dy, dx = turn(h, node)
        return ((-dy % SIDE) * SIDE + (-dx % SIDE)) * CAP

    def feed(h, parent, lo):
        for node, up, axis, step in TREE:
            if up == parent and node in HUBS:
                src = p_ref.at[pl.ds(lo, two), whole(h)] if parent == (0, 0) else (
                    near[h][parent].at[pl.ds(lo, two)])
                hub_in[h, node, lo] = net.send(
                    src, near[h][node].at[pl.ds(lo, two)], toward(h, axis, step))

    def await_hub(h, node, lo):
        hub_in[h, node, lo].wait_recv()

    def pick_block(h, parent, group, c):
        back = tuple(-v % SIDE for v in parent)
        pick = pick_of(group, away(h, back), c)
        return p_ref[pick, whole(h)] if parent == (0, 0) else near[h][parent][pick]

    def serve(h, parent):
        for n, (node, up, axis, step) in enumerate(TREE):
            if up != parent or node in HUBS:
                continue
            hop = tuple((a - b) % SIDE for a, b in zip(node, up))
            group = away(h, hop)
            for c in range(CAP):
                stage[h, n - len(HUBS), c] = pick_block(h, parent, group, c)
            arrivals.append(net.send(
                stage.at[h, n - len(HUBS)], got[0].at[h, pl.ds(slot_from(h, node), CAP)],
                toward(h, axis, step)))

    def keep_own(h, node):
        for c in range(CAP):
            got[0][h, slot_from(h, node) + c] = pick_block(h, node, me.dp, c)

    at = lambda z, c: full.at[mod4(z) * 2 + c]
    for lo in pieces:
        for h in (0, 1):
            feed(h, (0, 0), lo)
    load_q.wait()
    z_up = net.send(own_slot, own_slot, me.move("z", 1), at(me.z - 1, me.c))
    z_down = net.send(own_slot, own_slot, me.move("z", -1), at(me.z + 1, me.c))
    pair = [net.send(own_slot, own_slot, me.move("core", 0), at(me.z, 1 - me.c))]
    tab_v, tab_s, spot_v, spot_s = one("tab_v"), one("tab_s"), one("spot_v"), one("spot_s")
    blocks = list_ref.shape[1]
    every = jnp.transpose(jnp.concatenate(
        [list_ref[...], jnp.zeros((picks, 128 - blocks), jnp.int32)], axis=1))[0:blocks]
    lanes = lax.broadcasted_iota(jnp.int32, (blocks, 128), 1)
    spots = jnp.full((blocks, 128), -1, jnp.int32)
    for k in range(picks):
        entry = every[:, k:k + 1]
        spots = jnp.where(entry == lanes, k, spots)
        spots = jnp.where(lanes == blocks + k, entry, spots)
    spots = spots.reshape(groups, per, 128)
    present = jnp.max(jnp.where(spots >= 0, 1, 0), axis=1)
    quad = lax.rem(lax.broadcasted_iota(jnp.int32, (groups, 128), 1), per)
    earlier = jnp.zeros((groups, 128), jnp.int32)
    for j in range(1, per):
        earlier = earlier + jnp.where(quad >= j, pltpu.roll(present, j, 1), 0)
    ranks = jnp.where(present == 1, earlier, -1)
    tab_v[0] = ranks
    for c in range(CAP):
        first_of = jnp.zeros((groups, 128), jnp.int32)
        for j in range(1, per):
            first_of = first_of + jnp.where(pltpu.roll(ranks, 128 - j, 1) == c, j, 0)
        tab_v[1 + c] = first_of
    spot_v[...] = spots
    tab_copy = pltpu.make_async_copy(tab_v, tab_s, local.at[2])
    spot_copy = pltpu.make_async_copy(spot_v.at[me.dp], spot_s, local.at[3])
    tab_copy.start()
    spot_copy.start()

    def rank_of(group, block):
        return tab_s[0, group, block]

    def pick_of(group, source, c):
        return tab_s[1 + c, group, source * per]

    def listed(b, k):
        return spot_s[b, blocks + k]

    tab_copy.wait()
    spot_copy.wait()
    for h in (0, 1):
        serve(h, (0, 0))
        got[0][h, 0:CAP] = jnp.zeros((CAP, half, width), b16)
    for lo in pieces:
        for node in ((0, 3), (0, 1)):
            for h in (0, 1):
                await_hub(h, node, lo)
                feed(h, node, lo)
    for node in ((0, 3), (0, 1)):
        for h in (0, 1):
            serve(h, node)
    for lo in pieces:
        for h in (0, 1):
            await_hub(h, (3, 3), lo)
            feed(h, (3, 3), lo)
    z_up.wait_recv()
    behind, ahead = at(me.z - 1, me.c), at(me.z + 1, me.c)
    across = mod4(me.z + 2) * 2
    far = full.at[across + me.c]
    za = net.send(behind.at[0:two], behind.at[0:two], me.move("z", 1), far.at[0:two])
    pair.append(net.send(behind, behind, me.move("core", 0), at(me.z - 1, 1 - me.c)))
    z_down.wait_recv()
    zb = net.send(ahead.at[two:per], ahead.at[two:per], me.move("z", -1), far.at[two:per])
    pair.append(net.send(ahead, ahead, me.move("core", 0), at(me.z + 1, 1 - me.c)))
    for h in (0, 1):
        serve(h, (3, 3))
    for h in (0, 1):
        for lo in pieces:
            await_hub(h, (1, 1), lo)
        serve(h, (1, 1))
    for h in (0, 1):
        for lo in pieces:
            await_hub(h, (2, 3), lo)
        serve(h, (2, 3))
    za.wait_recv()
    zb.wait_recv()
    pair.append(net.send(far, far, me.move("core", 0), full.at[across + 1 - me.c]))
    for node in HUBS:
        for h in (0, 1):
            keep_own(h, node)

    lane = lax.broadcasted_iota(jnp.int32, (2 * deep, 128), 1)
    sub = lax.broadcasted_iota(jnp.int32, (2 * deep, 128), 0)
    wide_lane = lax.broadcasted_iota(jnp.int32, (2 * deep, queries), 1)
    wide_sub = lax.broadcasted_iota(jnp.int32, (2 * deep, queries), 0)

    def true_row(ch, sub):
        return (sub // deep) * half + ch * deep + lax.rem(sub, deep)

    def load_candidates(b):
        to = cand[b % 2]
        to[0:half] = p_ref[b, 0:half]
        to[half:rows] = p_ref[b, half:rows]
        for k in range(picks):
            block = listed(b, k)
            group = block // per
            r = rank_of(me.dp, block)
            ry = mod4(group // SIDE - me.y)
            rx = mod4(lax.rem(group, SIDE) - me.x)
            base = rows * (k + 1)
            slot = (ry * SIDE + rx) * CAP + r
            to[base:base + half] = got[0][0, slot]
            to[base + half:base + rows] = got[0][1, slot]

    def score(b):
        load_candidates(b)
        q = full[:, b].reshape(queries, width)
        logit[b][...] = lax.dot_general(
            cand[b % 2][...], q, (((1,), (1,)), ((), ())), preferred_element_type=f32) * scale

    line = lax.broadcasted_iota(jnp.int32, (32, 128), 0)
    side = lax.broadcasted_iota(jnp.int32, (32, 128), 1) // 64
    home = line + 32 * side

    def block_of(b, i):
        return me.dp * per + b if i == 0 else listed(b, i - 1)

    def summarise(b):
        peak = jnp.full((1, queries), NEG, f32)
        placed = jnp.full((32, 128), NEG, f32)
        for i in range(cands):
            block = logit[b][i * rows:(i + 1) * rows]
            peak = jnp.maximum(peak, jnp.max(block, axis=0, keepdims=True))
            top = jnp.max(block, axis=1, keepdims=True)
            lse = top + jnp.log2(jnp.sum(jnp.exp2(block - top), axis=1, keepdims=True))
            if i == 0:
                hit = wide_lane == wide_sub + me.inner * rows
                own_sum[...] += jnp.sum(jnp.where(hit, block, 0.0))
            line_of = jnp.sum(jnp.where(lax.rem(lane, 64) == sub, lse, 0.0), axis=0, keepdims=True)
            placed = jnp.where(home == block_of(b, i), line_of, placed)
        cols[b] = placed
        total = jnp.zeros((1, queries), f32)
        for i in range(cands):
            block = logit[b][i * rows:(i + 1) * rows]
            total = total + jnp.sum(jnp.exp2(block - peak), axis=0, keepdims=True)
        row_part[0, b:b + 1] = peak + jnp.log2(total)

    own_sum[...] = jnp.zeros(own_sum.shape, f32)
    for copy in arrivals + pair:
        copy.wait_recv()
    score(0)
    for b in range(1, per):
        score(b)
        summarise(b - 1)
    summarise(per - 1)

    def fold(values):
        top = jnp.max(values, axis=0)
        return top + jnp.log2(jnp.sum(jnp.exp2(values - top[None]), axis=0))

    rows_mine = row_part[0]
    row_src[...] = rows_mine
    stat_waits = [net.send(row_src, all_rows.at[me.inner], to, all_rows.at[origin])
                  for to, origin in zip(in_peers, in_from)]
    dense_mine = fold(cols[...])
    dense_src[...] = dense_mine
    stat_waits += [net.send(dense_src, all_dense.at[me.dp], to, all_dense.at[origin])
                   for to, origin in zip(dp_peers, dp_from)]
    all_rows[me.inner] = rows_mine
    all_dense[me.dp] = dense_mine
    for copy in stat_waits:
        copy.wait_recv()
    rows_all, dense_all = fold(all_rows[...]), fold(all_dense[...])
    row_lse[...] = rows_all
    pass_lse[...] = dense_all
    where = lax.broadcasted_iota(jnp.int32, rows_all.shape, 1) // rows
    loss_own = jnp.sum(jnp.where(where == me.inner, rows_all, 0.0))
    loss_own = loss_own + jnp.sum(jnp.where(home // per == me.dp, dense_all, 0.0))
    loss_mid[0] = loss_own - 2.0 * own_sum[...]

    def weigh(b):
        row = row_lse[b:b + 1] + 1.0
        for i in range(cands):
            block = block_of(b, i)
            values = pass_lse[pl.ds(lax.rem(block, 32), 1)]
            pick = lane == sub + (block // 32) * 64
            col = jnp.sum(jnp.where(pick, values, 0.0), axis=1, keepdims=True) + 1.0
            z = logit[b][i * rows:(i + 1) * rows]
            probs = jnp.exp2(z - row) + jnp.exp2(z - col)
            if i == 0:
                hit = wide_lane == wide_sub + me.inner * rows
                probs = probs - jnp.where(hit, 1.0, 0.0)
            weight[b][i * rows:(i + 1) * rows] = probs.astype(b16)

    def multiply(b):
        q = full[:, b].reshape(queries, width)
        out = jnp.dot(weight[b][...], q, preferred_element_type=f32)
        prod[b][...] = out.reshape(2 * cands, deep, width)

    send_rows, parts = {}, {(h, rf): [] for h in (0, 1) for rf in range(SIDE)}

    def emit(ch, rf):
        for h, (f, t) in enumerate(HALVES):
            def slot(i, carry, h=h, f=f):
                rt, c = i // CAP, lax.rem(i, CAP)
                owner = me.group(f, rf, rt)
                block = owner * per + jnp.where(
                    c == 0, pick_of(me.dp, owner, 0), pick_of(me.dp, owner, 1))
                acc = jnp.zeros((deep, width), f32)
                for b in range(per):
                    k = spot_s[b, block]
                    live = (k >= 0).astype(f32)
                    acc = acc + prod[b][2 * (jnp.maximum(k, 0) + 1) + h] * live
                part[ch, h, rt * 8 + rf * CAP + c] = acc.astype(b16)
                return carry

            lax.fori_loop(CAP if rf == 0 else 0, SIDE * CAP, slot, 0)
            up, down = me.move(t, 1), me.move(t, -1)
            rel = pl.ds(ch * deep, deep)
            send_rows[ch, h, rf] = (
                net.send(part.at[ch, h, 16 + rf * CAP], relay2.at[ch, h, 0, rf], up),
                net.send(part.at[ch, h, 16 + rf * CAP + 1], relay2.at[ch, h, 1, rf], down))
            parts[h, rf] += [
                net.send(part.at[ch, h, pl.ds(8 + rf * CAP, CAP)], seen[h][2][rf].at[:, rel], up),
                net.send(part.at[ch, h, pl.ds(24 + rf * CAP, CAP)], seen[h][0][rf].at[:, rel],
                         down)]

    def forward_parts(ch, *rfs):
        for rf in rfs:
            for h, (f, t) in enumerate(HALVES):
                for side_, copy in enumerate(send_rows[ch, h, rf]):
                    copy.wait_recv()
                    parts[h, rf].append(net.send(
                        relay2.at[ch, h, side_, rf],
                        seen[h][1][rf].at[side_, pl.ds(ch * deep, deep)],
                        me.move(t, 1 - 2 * side_)))

    def query_grad(b):
        load_candidates(b)
        grad = lax.dot_general(weight[b][...], cand[b % 2][...], (((0,), (0,)), ((), ())),
                               preferred_element_type=f32)
        query_part[:, b] = grad.astype(b16).reshape(inners, rows, width)

    swaps = {}

    def swap(lo):
        for dz in (2, 1, 3, 0):
            src = query_part.at[mod4(me.z + dz) * 2 + 1 - me.c, pl.ds(lo, two)]
            swaps[dz, lo] = net.send(src, pair_in.at[dz, pl.ds(lo, two)], me.move("core", 0))

    def join(dz, lo):
        swaps[dz, lo].wait_recv()
        slot = mod4(me.z + dz) * 2 + me.c

        def step(j, carry):
            both = query_part[slot, j].astype(f32) + pair_in[dz, j].astype(f32)
            qsum[dz, j] = both.astype(b16)
            return carry

        lax.fori_loop(lo, lo + two, step, 0)

    def fold_in(target, rd, source, start):
        def step(j, carry):
            both = target[rd, start + j].astype(f32) + source[j].astype(f32)
            target[rd, start + j] = both.astype(b16)
            return carry

        lax.fori_loop(0, two, step, 0)

    def collect(h, rf, j, sources, acc):
        f, t = HALVES[h]
        owner = me.group(f, rf, 0)
        for st in sources:
            r = rank_of(me.group(f, 0, st), owner * per + j)
            live = (r >= 0).astype(f32)
            c = jnp.maximum(r, 0)
            block = part[0, h, rf * CAP + c] if st == 0 else seen[h][st - 1][rf][c]
            acc = acc + block.astype(f32) * live
        return acc

    def gather_parts(h, rf):
        for copy in parts[h, rf]:
            copy.wait_recv()

        def step(j, carry):
            acc = collect(h, rf, j, range(SIDE), jnp.zeros((half, width), f32))
            dense[h, rf - 1, j] = acc.astype(b16)
            return carry

        lax.fori_loop(0, per, step, 0)

    merges, ends = {}, []
    weigh(0)
    for b in range(1, per):
        multiply(b - 1)
        weigh(b)
    multiply(per - 1)
    emit(0, 2)
    emit(0, 1)
    loss_waits = [net.send(loss_mid.at[0], loss_dp.at[me.dp], to, loss_dp.at[origin])
                  for to, origin in zip(dp_peers, dp_from)]
    loss_dp[me.dp] = loss_mid[0]
    for b in range(0, two):
        query_grad(b)
    swap(0)
    forward_parts(0, 2)
    emit(0, 3)
    for b in range(two, per):
        query_grad(b)
    swap(two)
    forward_parts(0, 1)
    join(2, 0)
    za = net.send(qsum.at[2, 0:two], zmerge.at[0], me.move("z", 1))
    join(2, two)
    zb = net.send(qsum.at[2, two:per], zmerge.at[1], me.move("z", -1))
    forward_parts(0, 3)
    for h, (f, t) in enumerate(HALVES):
        gather_parts(h, 2)
        merges[h] = [net.send(dense.at[h, 1, 0:two], merge.at[h, 0], me.move(f, 1)),
                     net.send(dense.at[h, 1, two:per], merge.at[h, 1], me.move(f, -1))]
    emit(0, 0)
    for lo in (0, two):
        join(1, lo)
        join(3, lo)
    za.wait_recv()
    fold_in(qsum, 1, zmerge.at[0], 0)
    z_up = net.send(qsum.at[1], zlast.at[0], me.move("z", 1))
    zb.wait_recv()
    fold_in(qsum, 3, zmerge.at[1], two)
    z_down = net.send(qsum.at[3], zlast.at[1], me.move("z", -1))
    for rf, slot in ((1, 0), (3, 1)):
        for h, (f, t) in enumerate(HALVES):
            gather_parts(h, rf)
            merges[h][slot].wait_recv()
            fold_in(dense.at[h], rf - 1, merge.at[h, slot], slot * two)
            ends.append(net.send(dense.at[h, rf - 1], last.at[h, slot],
                                 me.move(f, 1 if slot == 0 else -1)))
    forward_parts(0, 0)
    for h in (0, 1):
        for copy in parts[h, 0][:2]:
            copy.wait_recv()
        for j in range(per):
            prod[j][h] = collect(h, 0, j, (1, 3), prod[j][h])
    for copy in loss_waits:
        copy.wait_recv()
    mid = jnp.sum(loss_dp[...], axis=0)
    loss_mid[1] = mid
    loss_waits = [net.send(loss_mid.at[1], loss_inner.at[me.inner], to, loss_inner.at[origin])
                  for to, origin in zip(in_peers, in_from)]
    loss_inner[me.inner] = mid
    for lo in (0, two):
        swaps[0, lo].wait_recv()
    z_up.wait_recv()
    z_down.wait_recv()
    def finish_query(j, carry):
        both = query_part[mine, j].astype(f32) + pair_in[0, j].astype(f32)
        both = both + zlast[0, j].astype(f32) + zlast[1, j].astype(f32)
        qg_ref[j] = both.astype(b16)
        return carry

    lax.fori_loop(0, per, finish_query, 0)
    store_q = pltpu.make_async_copy(qg_ref, qg_hbm, local.at[0])
    store_q.start()
    for copy in loss_waits:
        copy.wait_recv()
    loss_out[0, 0] = jnp.max(jnp.sum(loss_inner[...], axis=0)) * (ln2 / count)
    for h in (0, 1):
        for copy in parts[h, 0][2:]:
            copy.wait_recv()
    for copy in ends:
        copy.wait_recv()
    store_p = []
    for j in range(per):
        for h in (0, 1):
            acc = collect(h, 0, j, (2,), prod[j][h])
            acc = acc + last[h, 0, j].astype(f32) + last[h, 1, j].astype(f32)
            pg_ref[j, h * half:(h + 1) * half] = acc.astype(b16)
        store_p.append(pltpu.make_async_copy(pg_ref.at[j], pg_hbm.at[j], local.at[4 + j]))
        store_p[-1].start()
    net.drain()
    store_q.wait()
    for copy in store_p:
        copy.wait()


def split_list(items, counts):
    out, start = [], 0
    for n in counts:
        out.append(tuple(items[start:start + n]))
        start += n
    return out


def finish_kernel(loss_ref, q_ref, p_ref, loss_out, q_out, p_out, loss_buf, q_buf, p_buf, sem):
    moves = [(loss_ref, loss_buf, loss_out)]
    for j in range(q_ref.shape[0]):
        moves += [(q_ref.at[j], q_buf.at[j], q_out.at[j]), (p_ref.at[j], p_buf.at[j], p_out.at[j])]
    loads = [pltpu.make_async_copy(a, b, sem.at[0, i]) for i, (a, b, c) in enumerate(moves)]
    stores = [pltpu.make_async_copy(b, c, sem.at[1, i]) for i, (a, b, c) in enumerate(moves)]
    for copy in loads:
        copy.start()
    for copy, after in zip(loads, stores):
        copy.wait()
        after.start()
    for copy in stores:
        copy.wait()


CHUNKS = 1


def body(queries, passages, neg_lists):
    per, rows, width = queries.shape
    groups, inners = lax.axis_size("dp"), lax.axis_size("inner")
    picks = neg_lists.shape[1]
    half, two = rows // 2, per // 2
    slots = groups * CAP
    chunks = CHUNKS
    deep = half // chunks
    cands, full_rows = picks + 1, rows * inners
    tall = cands * 2 * deep
    b16, f32 = jnp.bfloat16, jnp.float32
    sds = jax.ShapeDtypeStruct
    v = pltpu.VMEM
    sem_count = 100 + 160 * chunks
    need = {
        "full": [v((inners, per, rows, width), b16)],
        "stage": [v((2, len(TREE) - len(HUBS), CAP, half, width), b16)],
        "relay2": [v((chunks, 2, 2, SIDE, deep, width), b16)],
        "got": [v((2, slots, deep, width), b16)] * chunks,
        "logit": [v((tall, full_rows), f32)] * per,
        "weight": [v((tall, full_rows), b16)] * per,
        "prod": [v((2 * cands, deep, width), f32)] * per,
        "cand": [v((tall, width), b16)] * 2,
        "cols": [v((per, 32, 128), f32)],
        "row_part": [v((chunks, per, full_rows), f32)],
        "row_src": [v((per, full_rows), f32)],
        "dense_src": [v((32, 128), f32)],
        "all_rows": [v((inners, per, full_rows), f32)],
        "all_dense": [v((groups, 32, 128), f32)],
        "row_lse": [v((per, full_rows), f32)],
        "pass_lse": [v((32, 128), f32)],
        "part": [v((chunks, 2, slots, deep, width), b16)],
        "query_part": [v((inners, per, rows, width), b16)],
        "own_sum": [v((8, 128), f32)],
        "dense": [v((2, SIDE - 1, per, half, width), b16)],
        "merge": [v((2, 2, two, half, width), b16)],
        "last": [v((2, 2, per, half, width), b16)],
        "pair_in": [v((SIDE, per, rows, width), b16)],
        "qsum": [v((SIDE, per, rows, width), b16)],
        "zmerge": [v((2, two, rows, width), b16)],
        "zlast": [v((2, per, rows, width), b16)],
        "loss_dp": [v((groups, 8, 128), f32)],
        "loss_inner": [v((inners, 8, 128), f32)],
        "loss_mid": [v((2, 8, 128), f32)],
        "near": [v((per, half, width), b16)] * (2 * len(HUBS)),
        "seen": [v((CAP, half, width), b16)] * (2 * 3 * SIDE),
        "send_sem": [pltpu.SemaphoreType.DMA((sem_count,))],
        "recv_sem": [pltpu.SemaphoreType.DMA((sem_count,))],
        "local_sem": [pltpu.SemaphoreType.DMA((4 + per,))],
        "p_own": [v((per, rows, width), b16)],
        "qg": [v((per, rows, width), b16)],
        "pg": [v((per, rows, width), b16)],
        "tab_v": [v((1 + CAP, groups, 128), jnp.int32)],
        "tab_s": [pltpu.SMEM((1 + CAP, groups, 128), jnp.int32)],
        "spot_v": [v((groups, per, 128), jnp.int32)],
        "spot_s": [pltpu.SMEM((per, 128), jnp.int32)],
    }
    spec = {name: len(refs) for name, refs in need.items()}
    loss, query_grad, passage_grad = pl.pallas_call(
        functools.partial(fused_kernel, (chunks, groups, inners), spec),
        out_shape=(sds((1, 1), f32), sds((per, rows, width), b16), sds((per, rows, width), b16)),
        in_specs=[VM, AN, AN], out_specs=(SM, AN, AN),
        scratch_shapes=[ref for refs in need.values() for ref in refs],
        compiler_params=pltpu.CompilerParams(
            vmem_limit_bytes=VMEM_LIMIT, collective_id=0, has_side_effects=True),
        name="fused",
    )(neg_lists.T, queries, passages)
    shape = (per, rows, width)
    loss, query_grad, passage_grad = pl.pallas_call(
        finish_kernel,
        out_shape=(sds((1, 1), f32), sds(shape, b16), sds(shape, b16)),
        in_specs=[AN, AN, AN], out_specs=(AN, AN, AN),
        scratch_shapes=[pltpu.SMEM((1, 1), f32), v(shape, b16), v(shape, b16),
                        pltpu.SemaphoreType.DMA((2, 1 + 2 * per))],
        name="finish",
    )(loss, query_grad, passage_grad)
    return (loss.reshape(()), query_grad, passage_grad)


def solution(mesh):
    in_specs = (P("dp", "inner", None), P("dp", "inner", None), P())
    out_specs = (P(), P("dp", "inner", None), P("dp", "inner", None))
    return jax.shard_map(body, mesh=mesh, in_specs=in_specs, out_specs=out_specs, check_vma=False)
```

```python
import functools
import math

import jax
import jax.numpy as jnp
from jax import lax
from jax.experimental import pallas as pl
from jax.experimental.pallas import tpu as pltpu
from jax.sharding import PartitionSpec as P

MESH = pl.DeviceIdType.MESH
NEG = -1e30
SIDE = 4
CAP = 2
VMEM_LIMIT = 62 * 1024 * 1024

VM = pl.BlockSpec(memory_space=pltpu.VMEM)
SM = pl.BlockSpec(memory_space=pltpu.SMEM)
AN = pl.BlockSpec(memory_space=pl.ANY)


def mod4(v):
    return lax.rem(v + SIDE, SIDE)


class Place:
    def __init__(self):
        self.dp = lax.axis_index("dp")
        self.inner = lax.axis_index("inner")
        self.y, self.x = self.dp // SIDE, lax.rem(self.dp, SIDE)
        self.z, self.c = self.inner // 2, lax.rem(self.inner, 2)

    def move(self, axis, step):
        if axis == "x":
            return (self.y * SIDE + mod4(self.x + step), self.inner)
        if axis == "y":
            return (mod4(self.y + step) * SIDE + self.x, self.inner)
        if axis == "z":
            return (self.dp, mod4(self.z + step) * 2 + self.c)
        return (self.dp, self.z * 2 + (1 - self.c))

    def group(self, first, rf, rt):
        if first == "y":
            return mod4(self.y + rf) * SIDE + mod4(self.x + rt)
        return mod4(self.y + rt) * SIDE + mod4(self.x + rf)


class Copies:
    def __init__(self, send_sem, recv_sem):
        self.send_sem, self.recv_sem, self.count, self.made = send_sem, recv_sem, 0, []

    def send(self, src, dst, device, landing=None):
        i = self.count
        self.count += 1
        copy = pltpu.make_async_remote_copy(
            src_ref=src, dst_ref=dst, send_sem=self.send_sem.at[i], recv_sem=self.recv_sem.at[i],
            device_id=device, device_id_type=MESH)
        copy.start()
        self.made.append(copy)
        if landing is None:
            return copy
        return pltpu.make_async_remote_copy(
            src_ref=src, dst_ref=landing, send_sem=self.send_sem.at[i],
            recv_sem=self.recv_sem.at[i], device_id=device, device_id_type=MESH)

    def drain(self):
        for copy in self.made:
            copy.wait_send()


def neighbours(me):
    return [me.move(a, s) for a in "xyz" for s in (1, -1)] + [me.move("core", 0)]


HUBS = ((0, 1), (0, 3), (1, 1), (3, 3), (2, 3))
TREE = (
    ((0, 1), (0, 0), "x", 1), ((0, 3), (0, 0), "x", -1), ((1, 1), (0, 1), "y", 1),
    ((3, 3), (0, 3), "y", -1), ((2, 3), (3, 3), "y", -1), ((1, 0), (0, 0), "y", 1),
    ((3, 1), (0, 1), "y", -1), ((0, 2), (0, 3), "x", -1), ((1, 3), (0, 3), "y", 1),
    ((1, 2), (1, 1), "x", 1), ((2, 1), (1, 1), "y", 1), ((3, 0), (3, 3), "x", 1),
    ((3, 2), (3, 3), "x", -1), ((2, 0), (2, 3), "x", 1), ((2, 2), (2, 3), "x", -1))


def turn(h, node):
    return node if h == 0 else node[::-1]


HALVES = (("y", "x"), ("x", "y"))


def fused_kernel(dims, spec, list_ref, q_hbm, p_hbm, loss_out, qg_hbm, pg_hbm, *scratch):
    chunks, groups, inners = dims
    me = Place()
    per, rows, width = p_hbm.shape
    half, two = rows // 2, per // 2
    deep = half // chunks
    picks = list_ref.shape[0]
    cands = picks + 1
    queries = inners * rows
    slots = groups * CAP
    f32, b16 = jnp.float32, jnp.bfloat16
    ln2 = math.log(2.0)
    scale = 1.0 / (math.sqrt(width) * ln2)
    count = 2.0 * groups * per * queries
    take = dict(zip(spec, split_list(scratch, spec.values())))
    one = lambda name: take[name][0]
    full, stage = one("full"), one("stage")
    got, logit, weight, prod = take["got"], take["logit"], take["weight"], take["prod"]
    cand, cols, row_part = take["cand"], one("cols"), one("row_part")
    row_src, dense_src, all_rows = one("row_src"), one("dense_src"), one("all_rows")
    all_dense, row_lse, pass_lse = one("all_dense"), one("row_lse"), one("pass_lse")
    part, query_part, own_sum = one("part"), one("query_part"), one("own_sum")
    dense = one("dense")
    pair_in, qsum, zmerge, zlast = one("pair_in"), one("qsum"), one("zmerge"), one("zlast")
    loss_dp, loss_inner, loss_mid = one("loss_dp"), one("loss_inner"), one("loss_mid")
    near = [dict(zip(HUBS, take["near"][h * len(HUBS):(h + 1) * len(HUBS)])) for h in (0, 1)]
    leaves = [node for node, *_ in TREE if node not in HUBS]
    seen = [dict(zip(leaves, take["seen"][h * len(leaves):])) for h in (0, 1)]
    hub_sum = [dict(zip(HUBS, take["hub_sum"][h * len(HUBS):])) for h in (0, 1)]
    net = Copies(one("send_sem"), one("recv_sem"))

    dp_peers = [(lax.rem(me.dp + o, groups), me.inner) for o in range(1, groups)]
    dp_from = [lax.rem(me.dp - o + groups, groups) for o in range(1, groups)]
    in_peers = [(me.dp, lax.rem(me.inner + o, inners)) for o in range(1, inners)]
    in_from = [lax.rem(me.inner - o + inners, inners) for o in range(1, inners)]
    p_ref, qg_ref, pg_ref = one("p_own"), one("qg"), one("pg")
    local = one("local_sem")
    mine = me.z * 2 + me.c
    own_slot = full.at[mine]
    load_q = pltpu.make_async_copy(q_hbm, own_slot, local.at[0])
    load_p = pltpu.make_async_copy(p_hbm, p_ref, local.at[1])
    load_q.start()
    load_p.start()
    barrier = pltpu.get_barrier_semaphore()
    near_devices = neighbours(me)
    for device in near_devices:
        pl.semaphore_signal(barrier, inc=1, device_id=device, device_id_type=MESH)

    pl.semaphore_wait(barrier, len(near_devices))
    load_p.wait()

    whole = lambda h: pl.ds(h * half, half)
    pieces = (0, two)
    hub_in, arrivals = {}, []

    def away(h, node):
        dy, dx = turn(h, node)
        return mod4(me.y + dy) * SIDE + mod4(me.x + dx)

    def toward(h, axis, step):
        return me.move(axis if h == 0 else {"x": "y", "y": "x"}[axis], step)

    def slot_from(h, node):
        dy, dx = turn(h, node)
        return ((-dy % SIDE) * SIDE + (-dx % SIDE)) * CAP

    def feed(h, parent, lo):
        for node, up, axis, step in TREE:
            if up == parent and node in HUBS:
                src = p_ref.at[pl.ds(lo, two), whole(h)] if parent == (0, 0) else (
                    near[h][parent].at[pl.ds(lo, two)])
                hub_in[h, node, lo] = net.send(
                    src, near[h][node].at[pl.ds(lo, two)], toward(h, axis, step))

    def await_hub(h, node, lo):
        hub_in[h, node, lo].wait_recv()

    def pick_block(h, parent, group, c):
        back = tuple(-v % SIDE for v in parent)
        pick = pick_of(group, away(h, back), c)
        return p_ref[pick, whole(h)] if parent == (0, 0) else near[h][parent][pick]

    def serve(h, parent):
        for n, (node, up, axis, step) in enumerate(TREE):
            if up != parent or node in HUBS:
                continue
            hop = tuple((a - b) % SIDE for a, b in zip(node, up))
            group = away(h, hop)
            for c in range(CAP):
                stage[h, n - len(HUBS), c] = pick_block(h, parent, group, c)
            arrivals.append(net.send(
                stage.at[h, n - len(HUBS)], got[0].at[h, pl.ds(slot_from(h, node), CAP)],
                toward(h, axis, step)))

    def keep_own(h, node):
        for c in range(CAP):
            got[0][h, slot_from(h, node) + c] = pick_block(h, node, me.dp, c)

    at = lambda z, c: full.at[mod4(z) * 2 + c]
    for lo in pieces:
        for h in (0, 1):
            feed(h, (0, 0), lo)
    load_q.wait()
    z_up = net.send(own_slot, own_slot, me.move("z", 1), at(me.z - 1, me.c))
    z_down = net.send(own_slot, own_slot, me.move("z", -1), at(me.z + 1, me.c))
    pair = [net.send(own_slot, own_slot, me.move("core", 0), at(me.z, 1 - me.c))]
    tab_v, tab_s, spot_v, spot_s = one("tab_v"), one("tab_s"), one("spot_v"), one("spot_s")
    blocks = list_ref.shape[1]
    every = jnp.transpose(jnp.concatenate(
        [list_ref[...], jnp.zeros((picks, 128 - blocks), jnp.int32)], axis=1))[0:blocks]
    lanes = lax.broadcasted_iota(jnp.int32, (blocks, 128), 1)
    spots = jnp.full((blocks, 128), -1, jnp.int32)
    for k in range(picks):
        entry = every[:, k:k + 1]
        spots = jnp.where(entry == lanes, k, spots)
        spots = jnp.where(lanes == blocks + k, entry, spots)
    spots = spots.reshape(groups, per, 128)
    present = jnp.max(jnp.where(spots >= 0, 1, 0), axis=1)
    quad = lax.rem(lax.broadcasted_iota(jnp.int32, (groups, 128), 1), per)
    earlier = jnp.zeros((groups, 128), jnp.int32)
    for j in range(1, per):
        earlier = earlier + jnp.where(quad >= j, pltpu.roll(present, j, 1), 0)
    ranks = jnp.where(present == 1, earlier, -1)
    tab_v[0] = ranks
    for c in range(CAP):
        first_of = jnp.zeros((groups, 128), jnp.int32)
        for j in range(1, per):
            first_of = first_of + jnp.where(pltpu.roll(ranks, 128 - j, 1) == c, j, 0)
        tab_v[1 + c] = first_of
    spot_v[...] = spots
    tab_copy = pltpu.make_async_copy(tab_v, tab_s, local.at[2])
    spot_copy = pltpu.make_async_copy(spot_v.at[me.dp], spot_s, local.at[3])
    tab_copy.start()
    spot_copy.start()

    def rank_of(group, block):
        return tab_s[0, group, block]

    def pick_of(group, source, c):
        return tab_s[1 + c, group, source * per]

    def listed(b, k):
        return spot_s[b, blocks + k]

    tab_copy.wait()
    spot_copy.wait()
    for h in (0, 1):
        serve(h, (0, 0))
        got[0][h, 0:CAP] = jnp.zeros((CAP, half, width), b16)
    for lo in pieces:
        for node in ((0, 3), (0, 1)):
            for h in (0, 1):
                await_hub(h, node, lo)
                feed(h, node, lo)
    for node in ((0, 3), (0, 1)):
        for h in (0, 1):
            serve(h, node)
    for lo in pieces:
        for h in (0, 1):
            await_hub(h, (3, 3), lo)
            feed(h, (3, 3), lo)
    z_up.wait_recv()
    behind, ahead = at(me.z - 1, me.c), at(me.z + 1, me.c)
    across = mod4(me.z + 2) * 2
    far = full.at[across + me.c]
    za = net.send(behind.at[0:two], behind.at[0:two], me.move("z", 1), far.at[0:two])
    pair.append(net.send(behind, behind, me.move("core", 0), at(me.z - 1, 1 - me.c)))
    z_down.wait_recv()
    zb = net.send(ahead.at[two:per], ahead.at[two:per], me.move("z", -1), far.at[two:per])
    pair.append(net.send(ahead, ahead, me.move("core", 0), at(me.z + 1, 1 - me.c)))
    for h in (0, 1):
        serve(h, (3, 3))
    for h in (0, 1):
        for lo in pieces:
            await_hub(h, (1, 1), lo)
        serve(h, (1, 1))
    for h in (0, 1):
        for lo in pieces:
            await_hub(h, (2, 3), lo)
        serve(h, (2, 3))
    za.wait_recv()
    zb.wait_recv()
    pair.append(net.send(far, far, me.move("core", 0), full.at[across + 1 - me.c]))
    for node in HUBS:
        for h in (0, 1):
            keep_own(h, node)

    lane = lax.broadcasted_iota(jnp.int32, (2 * deep, 128), 1)
    sub = lax.broadcasted_iota(jnp.int32, (2 * deep, 128), 0)
    wide_lane = lax.broadcasted_iota(jnp.int32, (2 * deep, queries), 1)
    wide_sub = lax.broadcasted_iota(jnp.int32, (2 * deep, queries), 0)

    def true_row(ch, sub):
        return (sub // deep) * half + ch * deep + lax.rem(sub, deep)

    def load_candidates(b):
        to = cand[b % 2]
        to[0:half] = p_ref[b, 0:half]
        to[half:rows] = p_ref[b, half:rows]
        for k in range(picks):
            block = listed(b, k)
            group = block // per
            r = rank_of(me.dp, block)
            ry = mod4(group // SIDE - me.y)
            rx = mod4(lax.rem(group, SIDE) - me.x)
            base = rows * (k + 1)
            slot = (ry * SIDE + rx) * CAP + r
            to[base:base + half] = got[0][0, slot]
            to[base + half:base + rows] = got[0][1, slot]

    def score(b):
        load_candidates(b)
        q = full[:, b].reshape(queries, width)
        logit[b][...] = lax.dot_general(
            cand[b % 2][...], q, (((1,), (1,)), ((), ())), preferred_element_type=f32) * scale

    line = lax.broadcasted_iota(jnp.int32, (32, 128), 0)
    side = lax.broadcasted_iota(jnp.int32, (32, 128), 1) // 64
    home = line + 32 * side

    def block_of(b, i):
        return me.dp * per + b if i == 0 else listed(b, i - 1)

    def summarise(b):
        peak = jnp.full((1, queries), NEG, f32)
        placed = jnp.full((32, 128), NEG, f32)
        for i in range(cands):
            block = logit[b][i * rows:(i + 1) * rows]
            peak = jnp.maximum(peak, jnp.max(block, axis=0, keepdims=True))
            top = jnp.max(block, axis=1, keepdims=True)
            lse = top + jnp.log2(jnp.sum(jnp.exp2(block - top), axis=1, keepdims=True))
            if i == 0:
                hit = wide_lane == wide_sub + me.inner * rows
                own_sum[...] += jnp.sum(jnp.where(hit, block, 0.0))
            line_of = jnp.sum(jnp.where(lax.rem(lane, 64) == sub, lse, 0.0), axis=0, keepdims=True)
            placed = jnp.where(home == block_of(b, i), line_of, placed)
        cols[b] = placed
        total = jnp.zeros((1, queries), f32)
        for i in range(cands):
            block = logit[b][i * rows:(i + 1) * rows]
            total = total + jnp.sum(jnp.exp2(block - peak), axis=0, keepdims=True)
        row_part[0, b:b + 1] = peak + jnp.log2(total)

    own_sum[...] = jnp.zeros(own_sum.shape, f32)
    for copy in arrivals + pair:
        copy.wait_recv()
    score(0)
    for b in range(1, per):
        score(b)
        summarise(b - 1)
    summarise(per - 1)

    def fold(values):
        top = jnp.max(values, axis=0)
        return top + jnp.log2(jnp.sum(jnp.exp2(values - top[None]), axis=0))

    rows_mine = row_part[0]
    row_src[...] = rows_mine
    stat_waits = [net.send(row_src, all_rows.at[me.inner], to, all_rows.at[origin])
                  for to, origin in zip(in_peers, in_from)]
    dense_mine = fold(cols[...])
    dense_src[...] = dense_mine
    stat_waits += [net.send(dense_src, all_dense.at[me.dp], to, all_dense.at[origin])
                   for to, origin in zip(dp_peers, dp_from)]
    all_rows[me.inner] = rows_mine
    all_dense[me.dp] = dense_mine
    for copy in stat_waits:
        copy.wait_recv()
    rows_all, dense_all = fold(all_rows[...]), fold(all_dense[...])
    row_lse[...] = rows_all
    pass_lse[...] = dense_all
    where = lax.broadcasted_iota(jnp.int32, rows_all.shape, 1) // rows
    loss_own = jnp.sum(jnp.where(where == me.inner, rows_all, 0.0))
    loss_own = loss_own + jnp.sum(jnp.where(home // per == me.dp, dense_all, 0.0))
    loss_mid[0] = loss_own - 2.0 * own_sum[...]

    def weigh(b):
        row = row_lse[b:b + 1] + 1.0
        for i in range(cands):
            block = block_of(b, i)
            values = pass_lse[pl.ds(lax.rem(block, 32), 1)]
            pick = lane == sub + (block // 32) * 64
            col = jnp.sum(jnp.where(pick, values, 0.0), axis=1, keepdims=True) + 1.0
            z = logit[b][i * rows:(i + 1) * rows]
            probs = jnp.exp2(z - row) + jnp.exp2(z - col)
            if i == 0:
                hit = wide_lane == wide_sub + me.inner * rows
                probs = probs - jnp.where(hit, 1.0, 0.0)
            weight[b][i * rows:(i + 1) * rows] = probs.astype(b16)

    def multiply(b):
        q = full[:, b].reshape(queries, width)
        out = jnp.dot(weight[b][...], q, preferred_element_type=f32)
        prod[b][...] = out.reshape(2 * cands, deep, width)

    part_in, sum_in = {}, {}

    def back_of(node):
        return tuple(-v % SIDE for v in node)

    def make(h, node):
        owner = away(h, back_of(node))

        def slot(c, carry):
            block = owner * per + jnp.where(
                c == 0, pick_of(me.dp, owner, 0), pick_of(me.dp, owner, 1))
            acc = jnp.zeros((half, width), f32)
            for b in range(per):
                k = spot_s[b, block]
                live = (k >= 0).astype(f32)
                acc = acc + prod[b][2 * (jnp.maximum(k, 0) + 1) + h] * live
            part[0, h, slot_from(h, node) + c] = acc.astype(b16)
            return carry

        lax.fori_loop(0, CAP, slot, 0)

    def emit(*nodes):
        for node, up, axis, step in TREE:
            if node in nodes:
                for h in (0, 1):
                    make(h, node)
                    part_in[h, node] = net.send(
                        part.at[0, h, pl.ds(slot_from(h, node), CAP)], seen[h][node],
                        toward(h, axis, -step))

    def collect(h, here, j, acc):
        block = away(h, back_of(here)) * per + j
        if here != (0, 0):
            r = rank_of(me.dp, block)
            mine_ = part[0, h, slot_from(h, here) + jnp.maximum(r, 0)]
            acc = acc + mine_.astype(f32) * (r >= 0).astype(f32)
        for node, up, axis, step in TREE:
            if up != here:
                continue
            if node in HUBS:
                acc = acc + hub_sum[h][node][j].astype(f32)
            else:
                hop = tuple((a - b) % SIDE for a, b in zip(node, up))
                r = rank_of(away(h, hop), block)
                piece = seen[h][node][jnp.maximum(r, 0)]
                acc = acc + piece.astype(f32) * (r >= 0).astype(f32)
        return acc

    def climb(*here):
        for lo in pieces:
            for at_hub in here:
                for h in (0, 1):
                    climb_piece(h, at_hub, lo)

    def climb_piece(h, here, lo):
        n = HUBS.index(here)
        axis, step = [(a, s) for node, _, a, s in TREE if node == here][0]
        for node, up, *_ in TREE:
            if up == here and node in HUBS:
                sum_in[h, node, lo].wait_recv()
            elif up == here and lo == 0:
                part_in[h, node].wait_recv()

        def block(j, carry):
            dense[h, n, j] = collect(h, here, j, jnp.zeros((half, width), f32)).astype(b16)
            return carry

        lax.fori_loop(lo, lo + two, block, 0)
        sum_in[h, here, lo] = net.send(
            dense.at[h, n, pl.ds(lo, two)], hub_sum[h][here].at[pl.ds(lo, two)],
            toward(h, axis, -step))

    def query_grad(b):
        load_candidates(b)
        grad = lax.dot_general(weight[b][...], cand[b % 2][...], (((0,), (0,)), ((), ())),
                               preferred_element_type=f32)
        query_part[:, b] = grad.astype(b16).reshape(inners, rows, width)

    swaps = {}

    def swap(lo):
        for dz in (2, 1, 3, 0):
            src = query_part.at[mod4(me.z + dz) * 2 + 1 - me.c, pl.ds(lo, two)]
            swaps[dz, lo] = net.send(src, pair_in.at[dz, pl.ds(lo, two)], me.move("core", 0))

    def join(dz, lo):
        swaps[dz, lo].wait_recv()
        slot = mod4(me.z + dz) * 2 + me.c

        def step(j, carry):
            both = query_part[slot, j].astype(f32) + pair_in[dz, j].astype(f32)
            qsum[dz, j] = both.astype(b16)
            return carry

        lax.fori_loop(lo, lo + two, step, 0)

    def fold_in(target, rd, source, start):
        def step(j, carry):
            both = target[rd, start + j].astype(f32) + source[j].astype(f32)
            target[rd, start + j] = both.astype(b16)
            return carry

        lax.fori_loop(0, two, step, 0)

    weigh(0)
    for b in range(1, per):
        multiply(b - 1)
        weigh(b)
    multiply(per - 1)
    emit((2, 0), (2, 2))
    emit((3, 0), (3, 2))
    query_grad(0)
    emit((1, 2), (2, 1))
    loss_waits = [net.send(loss_mid.at[0], loss_dp.at[me.dp], to, loss_dp.at[origin])
                  for to, origin in zip(dp_peers, dp_from)]
    loss_dp[me.dp] = loss_mid[0]
    for h in (0, 1):
        make(h, (2, 3))
    climb((2, 3))
    query_grad(1)
    swap(0)
    for b in range(two, per):
        query_grad(b)
    swap(two)
    emit((0, 2), (1, 3), (3, 1))
    join(2, 0)
    za = net.send(qsum.at[2, 0:two], zmerge.at[0], me.move("z", 1))
    join(2, two)
    zb = net.send(qsum.at[2, two:per], zmerge.at[1], me.move("z", -1))
    for h in (0, 1):
        make(h, (3, 3))
    climb((3, 3))
    join(1, two)
    z_in = [net.send(qsum.at[1, two:per], zlast.at[0, two:per], me.move("z", 1))]
    join(3, 0)
    z_in.append(net.send(qsum.at[3, 0:two], zlast.at[1, 0:two], me.move("z", -1)))
    for h in (0, 1):
        make(h, (1, 1))
    climb((1, 1))
    emit((1, 0))
    join(1, 0)
    join(3, two)
    for h in (0, 1):
        make(h, (0, 3))
        make(h, (0, 1))
    za.wait_recv()
    fold_in(qsum, 1, zmerge.at[0], 0)
    z_in.append(net.send(qsum.at[1, 0:two], zlast.at[0, 0:two], me.move("z", 1)))
    zb.wait_recv()
    fold_in(qsum, 3, zmerge.at[1], two)
    z_in.append(net.send(qsum.at[3, two:per], zlast.at[1, two:per], me.move("z", -1)))
    climb((0, 3), (0, 1))
    for copy in loss_waits:
        copy.wait_recv()
    mid = jnp.sum(loss_dp[...], axis=0)
    loss_mid[1] = mid
    loss_waits = [net.send(loss_mid.at[1], loss_inner.at[me.inner], to, loss_inner.at[origin])
                  for to, origin in zip(in_peers, in_from)]
    loss_inner[me.inner] = mid
    for lo in (0, two):
        swaps[0, lo].wait_recv()
    for copy in z_in:
        copy.wait_recv()
    def finish_query(j, carry):
        both = query_part[mine, j].astype(f32) + pair_in[0, j].astype(f32)
        both = both + zlast[0, j].astype(f32) + zlast[1, j].astype(f32)
        qg_ref[j] = both.astype(b16)
        return carry

    lax.fori_loop(0, per, finish_query, 0)
    store_q = pltpu.make_async_copy(qg_ref, qg_hbm, local.at[0])
    store_q.start()
    for copy in loss_waits:
        copy.wait_recv()
    loss_out[0, 0] = jnp.max(jnp.sum(loss_inner[...], axis=0)) * (ln2 / count)
    for h in (0, 1):
        part_in[h, (1, 0)].wait_recv()
    store_p = []
    for j in range(per):
        for h in (0, 1):
            if j in pieces:
                for node in ((0, 3), (0, 1)):
                    sum_in[h, node, j].wait_recv()
            acc = collect(h, (0, 0), j, prod[j][h])
            pg_ref[j, h * half:(h + 1) * half] = acc.astype(b16)
        store_p.append(pltpu.make_async_copy(pg_ref.at[j], pg_hbm.at[j], local.at[4 + j]))
        store_p[-1].start()
    net.drain()
    store_q.wait()
    for copy in store_p:
        copy.wait()


def split_list(items, counts):
    out, start = [], 0
    for n in counts:
        out.append(tuple(items[start:start + n]))
        start += n
    return out


def finish_kernel(loss_ref, q_ref, p_ref, loss_out, q_out, p_out, loss_buf, q_buf, p_buf, sem):
    moves = [(loss_ref, loss_buf, loss_out)]
    for j in range(q_ref.shape[0]):
        moves += [(q_ref.at[j], q_buf.at[j], q_out.at[j]), (p_ref.at[j], p_buf.at[j], p_out.at[j])]
    loads = [pltpu.make_async_copy(a, b, sem.at[0, i]) for i, (a, b, c) in enumerate(moves)]
    stores = [pltpu.make_async_copy(b, c, sem.at[1, i]) for i, (a, b, c) in enumerate(moves)]
    for copy in loads:
        copy.start()
    for copy, after in zip(loads, stores):
        copy.wait()
        after.start()
    for copy in stores:
        copy.wait()


CHUNKS = 1


def body(queries, passages, neg_lists):
    per, rows, width = queries.shape
    groups, inners = lax.axis_size("dp"), lax.axis_size("inner")
    picks = neg_lists.shape[1]
    half, two = rows // 2, per // 2
    slots = groups * CAP
    chunks = CHUNKS
    deep = half // chunks
    cands, full_rows = picks + 1, rows * inners
    tall = cands * 2 * deep
    b16, f32 = jnp.bfloat16, jnp.float32
    sds = jax.ShapeDtypeStruct
    v = pltpu.VMEM
    sem_count = 100 + 160 * chunks
    need = {
        "full": [v((inners, per, rows, width), b16)],
        "stage": [v((2, len(TREE) - len(HUBS), CAP, half, width), b16)],
        "got": [v((2, slots, deep, width), b16)] * chunks,
        "logit": [v((tall, full_rows), f32)] * per,
        "weight": [v((tall, full_rows), b16)] * per,
        "prod": [v((2 * cands, deep, width), f32)] * per,
        "cand": [v((tall, width), b16)] * 2,
        "cols": [v((per, 32, 128), f32)],
        "row_part": [v((chunks, per, full_rows), f32)],
        "row_src": [v((per, full_rows), f32)],
        "dense_src": [v((32, 128), f32)],
        "all_rows": [v((inners, per, full_rows), f32)],
        "all_dense": [v((groups, 32, 128), f32)],
        "row_lse": [v((per, full_rows), f32)],
        "pass_lse": [v((32, 128), f32)],
        "part": [v((chunks, 2, slots, deep, width), b16)],
        "query_part": [v((inners, per, rows, width), b16)],
        "own_sum": [v((8, 128), f32)],
        "dense": [v((2, len(HUBS), per, half, width), b16)],
        "hub_sum": [v((per, half, width), b16)] * (2 * len(HUBS)),
        "pair_in": [v((SIDE, per, rows, width), b16)],
        "qsum": [v((SIDE, per, rows, width), b16)],
        "zmerge": [v((2, two, rows, width), b16)],
        "zlast": [v((2, per, rows, width), b16)],
        "loss_dp": [v((groups, 8, 128), f32)],
        "loss_inner": [v((inners, 8, 128), f32)],
        "loss_mid": [v((2, 8, 128), f32)],
        "near": [v((per, half, width), b16)] * (2 * len(HUBS)),
        "seen": [v((CAP, half, width), b16)] * (2 * (len(TREE) - len(HUBS))),
        "send_sem": [pltpu.SemaphoreType.DMA((sem_count,))],
        "recv_sem": [pltpu.SemaphoreType.DMA((sem_count,))],
        "local_sem": [pltpu.SemaphoreType.DMA((4 + per,))],
        "p_own": [v((per, rows, width), b16)],
        "qg": [v((per, rows, width), b16)],
        "pg": [v((per, rows, width), b16)],
        "tab_v": [v((1 + CAP, groups, 128), jnp.int32)],
        "tab_s": [pltpu.SMEM((1 + CAP, groups, 128), jnp.int32)],
        "spot_v": [v((groups, per, 128), jnp.int32)],
        "spot_s": [pltpu.SMEM((per, 128), jnp.int32)],
    }
    spec = {name: len(refs) for name, refs in need.items()}
    loss, query_grad, passage_grad = pl.pallas_call(
        functools.partial(fused_kernel, (chunks, groups, inners), spec),
        out_shape=(sds((1, 1), f32), sds((per, rows, width), b16), sds((per, rows, width), b16)),
        in_specs=[VM, AN, AN], out_specs=(SM, AN, AN),
        scratch_shapes=[ref for refs in need.values() for ref in refs],
        compiler_params=pltpu.CompilerParams(
            vmem_limit_bytes=VMEM_LIMIT, collective_id=0, has_side_effects=True),
        name="fused",
    )(neg_lists.T, queries, passages)
    shape = (per, rows, width)
    loss, query_grad, passage_grad = pl.pallas_call(
        finish_kernel,
        out_shape=(sds((1, 1), f32), sds(shape, b16), sds(shape, b16)),
        in_specs=[AN, AN, AN], out_specs=(AN, AN, AN),
        scratch_shapes=[pltpu.SMEM((1, 1), f32), v(shape, b16), v(shape, b16),
                        pltpu.SemaphoreType.DMA((2, 1 + 2 * per))],
        name="finish",
    )(loss, query_grad, passage_grad)
    return (loss.reshape(()), query_grad, passage_grad)


def solution(mesh):
    in_specs = (P("dp", "inner", None), P("dp", "inner", None), P())
    out_specs = (P(), P("dp", "inner", None), P("dp", "inner", None))
    return jax.shard_map(body, mesh=mesh, in_specs=in_specs, out_specs=out_specs, check_vma=False)
```

```python
import functools
import math

import jax
import jax.numpy as jnp
from jax import lax
from jax.experimental import pallas as pl
from jax.experimental.pallas import tpu as pltpu
from jax.sharding import PartitionSpec as P

MESH = pl.DeviceIdType.MESH
NEG = -1e30
SIDE = 4
CAP = 2
VMEM_LIMIT = 62 * 1024 * 1024

VM = pl.BlockSpec(memory_space=pltpu.VMEM)
SM = pl.BlockSpec(memory_space=pltpu.SMEM)
AN = pl.BlockSpec(memory_space=pl.ANY)


def mod4(v):
    return lax.rem(v + SIDE, SIDE)


class Place:
    def __init__(self):
        self.dp = lax.axis_index("dp")
        self.inner = lax.axis_index("inner")
        self.y, self.x = self.dp // SIDE, lax.rem(self.dp, SIDE)
        self.z, self.c = self.inner // 2, lax.rem(self.inner, 2)

    def move(self, axis, step):
        if axis == "x":
            return (self.y * SIDE + mod4(self.x + step), self.inner)
        if axis == "y":
            return (mod4(self.y + step) * SIDE + self.x, self.inner)
        if axis == "z":
            return (self.dp, mod4(self.z + step) * 2 + self.c)
        return (self.dp, self.z * 2 + (1 - self.c))

    def group(self, first, rf, rt):
        if first == "y":
            return mod4(self.y + rf) * SIDE + mod4(self.x + rt)
        return mod4(self.y + rt) * SIDE + mod4(self.x + rf)


class Copies:
    def __init__(self, send_sem, recv_sem):
        self.send_sem, self.recv_sem, self.count, self.made = send_sem, recv_sem, 0, []

    def send(self, src, dst, device, landing=None):
        i = self.count
        self.count += 1
        copy = pltpu.make_async_remote_copy(
            src_ref=src, dst_ref=dst, send_sem=self.send_sem.at[i], recv_sem=self.recv_sem.at[i],
            device_id=device, device_id_type=MESH)
        copy.start()
        self.made.append(copy)
        if landing is None:
            return copy
        return pltpu.make_async_remote_copy(
            src_ref=src, dst_ref=landing, send_sem=self.send_sem.at[i],
            recv_sem=self.recv_sem.at[i], device_id=device, device_id_type=MESH)

    def drain(self):
        for copy in self.made:
            copy.wait_send()


def neighbours(me):
    return [me.move(a, s) for a in "xyz" for s in (1, -1)] + [me.move("core", 0)]


HUBS = ((0, 1), (0, 3), (1, 1), (3, 3), (2, 3))
TREE = (
    ((0, 1), (0, 0), "x", 1), ((0, 3), (0, 0), "x", -1), ((1, 1), (0, 1), "y", 1),
    ((3, 3), (0, 3), "y", -1), ((2, 3), (3, 3), "y", -1), ((1, 0), (0, 0), "y", 1),
    ((3, 1), (0, 1), "y", -1), ((0, 2), (0, 3), "x", -1), ((1, 3), (0, 3), "y", 1),
    ((1, 2), (1, 1), "x", 1), ((2, 1), (1, 1), "y", 1), ((3, 0), (3, 3), "x", 1),
    ((3, 2), (3, 3), "x", -1), ((2, 0), (2, 3), "x", 1), ((2, 2), (2, 3), "x", -1))


def turn(h, node):
    return node if h == 0 else node[::-1]


HALVES = (("y", "x"), ("x", "y"))


def fused_kernel(dims, spec, list_ref, q_hbm, p_hbm, loss_out, qg_hbm, pg_hbm, *scratch):
    chunks, groups, inners = dims
    me = Place()
    per, rows, width = p_hbm.shape
    half, two = rows // 2, per // 2
    deep = half // chunks
    picks = list_ref.shape[0]
    cands = picks + 1
    queries = inners * rows
    slots = groups * CAP
    f32, b16 = jnp.float32, jnp.bfloat16
    ln2 = math.log(2.0)
    scale = 1.0 / (math.sqrt(width) * ln2)
    count = 2.0 * groups * per * queries
    take = dict(zip(spec, split_list(scratch, spec.values())))
    one = lambda name: take[name][0]
    full, stage = one("full"), one("stage")
    got, logit, weight, prod = take["got"], take["logit"], take["weight"], take["prod"]
    cand, cols, row_part = take["cand"], one("cols"), one("row_part")
    row_src, dense_src, all_rows = one("row_src"), one("dense_src"), one("all_rows")
    all_dense, row_lse, pass_lse = one("all_dense"), one("row_lse"), one("pass_lse")
    part, query_part, own_sum = one("part"), one("query_part"), one("own_sum")
    dense = one("dense")
    pair_in, qsum, zmerge, zlast = one("pair_in"), one("qsum"), one("zmerge"), one("zlast")
    loss_dp, loss_inner, loss_mid = one("loss_dp"), one("loss_inner"), one("loss_mid")
    near = [dict(zip(HUBS, take["near"][h * len(HUBS):(h + 1) * len(HUBS)])) for h in (0, 1)]
    leaves = [node for node, *_ in TREE if node not in HUBS]
    seen = [dict(zip(leaves, take["seen"][h * len(leaves):])) for h in (0, 1)]
    hub_sum = [dict(zip(HUBS, take["hub_sum"][h * len(HUBS):])) for h in (0, 1)]
    net = Copies(one("send_sem"), one("recv_sem"))

    dp_peers = [(lax.rem(me.dp + o, groups), me.inner) for o in range(1, groups)]
    dp_from = [lax.rem(me.dp - o + groups, groups) for o in range(1, groups)]
    in_peers = [(me.dp, lax.rem(me.inner + o, inners)) for o in range(1, inners)]
    in_from = [lax.rem(me.inner - o + inners, inners) for o in range(1, inners)]
    p_ref, qg_ref, pg_ref = one("p_own"), one("qg"), one("pg")
    local = one("local_sem")
    mine = me.z * 2 + me.c
    own_slot = full.at[mine]
    load_q = pltpu.make_async_copy(q_hbm, own_slot, local.at[0])
    load_p = pltpu.make_async_copy(p_hbm, p_ref, local.at[1])
    load_q.start()
    load_p.start()
    barrier = pltpu.get_barrier_semaphore()
    near_devices = neighbours(me)
    for device in near_devices:
        pl.semaphore_signal(barrier, inc=1, device_id=device, device_id_type=MESH)

    pl.semaphore_wait(barrier, len(near_devices))
    load_p.wait()

    whole = lambda h: pl.ds(h * half, half)
    pieces = (0, two)
    hub_in, arrivals = {}, []

    def away(h, node):
        dy, dx = turn(h, node)
        return mod4(me.y + dy) * SIDE + mod4(me.x + dx)

    def toward(h, axis, step):
        return me.move(axis if h == 0 else {"x": "y", "y": "x"}[axis], step)

    def slot_from(h, node):
        dy, dx = turn(h, node)
        return ((-dy % SIDE) * SIDE + (-dx % SIDE)) * CAP

    def feed(h, parent, lo):
        for node, up, axis, step in TREE:
            if up == parent and node in HUBS:
                src = p_ref.at[pl.ds(lo, two), whole(h)] if parent == (0, 0) else (
                    near[h][parent].at[pl.ds(lo, two)])
                hub_in[h, node, lo] = net.send(
                    src, near[h][node].at[pl.ds(lo, two)], toward(h, axis, step))

    def await_hub(h, node, lo):
        hub_in[h, node, lo].wait_recv()

    def pick_block(h, parent, group, c):
        back = tuple(-v % SIDE for v in parent)
        pick = pick_of(group, away(h, back), c)
        return p_ref[pick, whole(h)] if parent == (0, 0) else near[h][parent][pick]

    def serve(h, parent):
        for n, (node, up, axis, step) in enumerate(TREE):
            if up != parent or node in HUBS:
                continue
            hop = tuple((a - b) % SIDE for a, b in zip(node, up))
            group = away(h, hop)
            for c in range(CAP):
                stage[h, n - len(HUBS), c] = pick_block(h, parent, group, c)
            arrivals.append(net.send(
                stage.at[h, n - len(HUBS)], got[0].at[h, pl.ds(slot_from(h, node), CAP)],
                toward(h, axis, step)))

    def keep_own(h, node):
        for c in range(CAP):
            got[0][h, slot_from(h, node) + c] = pick_block(h, node, me.dp, c)

    at = lambda z, c: full.at[mod4(z) * 2 + c]
    for lo in pieces:
        for h in (0, 1):
            feed(h, (0, 0), lo)
    load_q.wait()
    z_up = net.send(own_slot, own_slot, me.move("z", 1), at(me.z - 1, me.c))
    z_down = net.send(own_slot, own_slot, me.move("z", -1), at(me.z + 1, me.c))
    pair = [net.send(own_slot, own_slot, me.move("core", 0), at(me.z, 1 - me.c))]
    tab_v, tab_s, spot_v, spot_s = one("tab_v"), one("tab_s"), one("spot_v"), one("spot_s")
    blocks = list_ref.shape[1]
    every = jnp.transpose(jnp.concatenate(
        [list_ref[...], jnp.zeros((picks, 128 - blocks), jnp.int32)], axis=1))[0:blocks]
    lanes = lax.broadcasted_iota(jnp.int32, (blocks, 128), 1)
    spots = jnp.full((blocks, 128), -1, jnp.int32)
    for k in range(picks):
        entry = every[:, k:k + 1]
        spots = jnp.where(entry == lanes, k, spots)
        spots = jnp.where(lanes == blocks + k, entry, spots)
    spots = spots.reshape(groups, per, 128)
    present = jnp.max(jnp.where(spots >= 0, 1, 0), axis=1)
    quad = lax.rem(lax.broadcasted_iota(jnp.int32, (groups, 128), 1), per)
    earlier = jnp.zeros((groups, 128), jnp.int32)
    for j in range(1, per):
        earlier = earlier + jnp.where(quad >= j, pltpu.roll(present, j, 1), 0)
    ranks = jnp.where(present == 1, earlier, -1)
    tab_v[0] = ranks
    for c in range(CAP):
        first_of = jnp.zeros((groups, 128), jnp.int32)
        for j in range(1, per):
            first_of = first_of + jnp.where(pltpu.roll(ranks, 128 - j, 1) == c, j, 0)
        tab_v[1 + c] = first_of
    spot_v[...] = spots
    tab_copy = pltpu.make_async_copy(tab_v, tab_s, local.at[2])
    spot_copy = pltpu.make_async_copy(spot_v.at[me.dp], spot_s, local.at[3])
    tab_copy.start()
    spot_copy.start()

    def rank_of(group, block):
        return tab_s[0, group, block]

    def pick_of(group, source, c):
        return tab_s[1 + c, group, source * per]

    def listed(b, k):
        return spot_s[b, blocks + k]

    tab_copy.wait()
    spot_copy.wait()
    for h in (0, 1):
        serve(h, (0, 0))
        got[0][h, 0:CAP] = jnp.zeros((CAP, half, width), b16)
    for lo in pieces:
        for node in ((0, 3), (0, 1)):
            for h in (0, 1):
                await_hub(h, node, lo)
                feed(h, node, lo)
    for node in ((0, 3), (0, 1)):
        for h in (0, 1):
            serve(h, node)
    for lo in pieces:
        for h in (0, 1):
            await_hub(h, (3, 3), lo)
            feed(h, (3, 3), lo)
    z_up.wait_recv()
    behind, ahead = at(me.z - 1, me.c), at(me.z + 1, me.c)
    across = mod4(me.z + 2) * 2
    far = full.at[across + me.c]
    za = net.send(behind.at[0:two], behind.at[0:two], me.move("z", 1), far.at[0:two])
    pair.append(net.send(behind, behind, me.move("core", 0), at(me.z - 1, 1 - me.c)))
    z_down.wait_recv()
    zb = net.send(ahead.at[two:per], ahead.at[two:per], me.move("z", -1), far.at[two:per])
    pair.append(net.send(ahead, ahead, me.move("core", 0), at(me.z + 1, 1 - me.c)))
    for h in (0, 1):
        serve(h, (3, 3))
    for h in (0, 1):
        for lo in pieces:
            await_hub(h, (1, 1), lo)
        serve(h, (1, 1))
    for h in (0, 1):
        for lo in pieces:
            await_hub(h, (2, 3), lo)
        serve(h, (2, 3))
    za.wait_recv()
    zb.wait_recv()
    pair.append(net.send(far, far, me.move("core", 0), full.at[across + 1 - me.c]))
    for node in HUBS:
        for h in (0, 1):
            keep_own(h, node)

    lane = lax.broadcasted_iota(jnp.int32, (2 * deep, 128), 1)
    sub = lax.broadcasted_iota(jnp.int32, (2 * deep, 128), 0)
    wide_lane = lax.broadcasted_iota(jnp.int32, (2 * deep, queries), 1)
    wide_sub = lax.broadcasted_iota(jnp.int32, (2 * deep, queries), 0)

    def true_row(ch, sub):
        return (sub // deep) * half + ch * deep + lax.rem(sub, deep)

    def load_candidates(b):
        to = cand[b % 2]
        to[0:half] = p_ref[b, 0:half]
        to[half:rows] = p_ref[b, half:rows]
        for k in range(picks):
            block = listed(b, k)
            group = block // per
            r = rank_of(me.dp, block)
            ry = mod4(group // SIDE - me.y)
            rx = mod4(lax.rem(group, SIDE) - me.x)
            base = rows * (k + 1)
            slot = (ry * SIDE + rx) * CAP + r
            to[base:base + half] = got[0][0, slot]
            to[base + half:base + rows] = got[0][1, slot]

    def score(b):
        load_candidates(b)
        q = full[:, b].reshape(queries, width)
        logit[b][...] = lax.dot_general(
            cand[b % 2][...], q, (((1,), (1,)), ((), ())), preferred_element_type=f32) * scale

    line = lax.broadcasted_iota(jnp.int32, (32, 128), 0)
    side = lax.broadcasted_iota(jnp.int32, (32, 128), 1) // 64
    home = line + 32 * side

    def block_of(b, i):
        return me.dp * per + b if i == 0 else listed(b, i - 1)

    def summarise(b):
        peak = jnp.full((1, queries), NEG, f32)
        placed = jnp.full((32, 128), NEG, f32)
        for i in range(cands):
            block = logit[b][i * rows:(i + 1) * rows]
            peak = jnp.maximum(peak, jnp.max(block, axis=0, keepdims=True))
            top = jnp.max(block, axis=1, keepdims=True)
            lse = top + jnp.log2(jnp.sum(jnp.exp2(block - top), axis=1, keepdims=True))
            if i == 0:
                hit = wide_lane == wide_sub + me.inner * rows
                own_sum[...] += jnp.sum(jnp.where(hit, block, 0.0))
            line_of = jnp.sum(jnp.where(lax.rem(lane, 64) == sub, lse, 0.0), axis=0, keepdims=True)
            placed = jnp.where(home == block_of(b, i), line_of, placed)
        cols[b] = placed
        total = jnp.zeros((1, queries), f32)
        for i in range(cands):
            block = logit[b][i * rows:(i + 1) * rows]
            total = total + jnp.sum(jnp.exp2(block - peak), axis=0, keepdims=True)
        row_part[0, b:b + 1] = peak + jnp.log2(total)

    own_sum[...] = jnp.zeros(own_sum.shape, f32)
    for copy in arrivals + pair:
        copy.wait_recv()
    score(0)
    for b in range(1, per):
        score(b)
        summarise(b - 1)
    summarise(per - 1)

    def fold(values):
        top = jnp.max(values, axis=0)
        return top + jnp.log2(jnp.sum(jnp.exp2(values - top[None]), axis=0))

    rows_mine = row_part[0]
    row_src[...] = rows_mine
    stat_waits = [net.send(row_src, all_rows.at[me.inner], to, all_rows.at[origin])
                  for to, origin in zip(in_peers, in_from)]
    dense_mine = fold(cols[...])
    dense_src[...] = dense_mine
    stat_waits += [net.send(dense_src, all_dense.at[me.dp], to, all_dense.at[origin])
                   for to, origin in zip(dp_peers, dp_from)]
    all_rows[me.inner] = rows_mine
    all_dense[me.dp] = dense_mine
    for copy in stat_waits[:len(in_peers)]:
        copy.wait_recv()
    rows_all = fold(all_rows[...])
    row_lse[...] = rows_all
    for b in range(per):
        row = row_lse[b:b + 1] + 1.0
        for i in range(cands):
            probs = jnp.exp2(logit[b][i * rows:(i + 1) * rows] - row)
            if i == 0:
                hit = wide_lane == wide_sub + me.inner * rows
                probs = probs - jnp.where(hit, 1.0, 0.0)
            prod[b][2 * i:2 * i + 2, :, 0:queries] = probs.reshape(2, half, queries)
    for copy in stat_waits[len(in_peers):]:
        copy.wait_recv()
    dense_all = fold(all_dense[...])
    pass_lse[...] = dense_all
    where = lax.broadcasted_iota(jnp.int32, rows_all.shape, 1) // rows
    loss_own = jnp.sum(jnp.where(where == me.inner, rows_all, 0.0))
    loss_own = loss_own + jnp.sum(jnp.where(home // per == me.dp, dense_all, 0.0))
    loss_mid[0] = loss_own - 2.0 * own_sum[...]

    def weigh(b):
        for i in range(cands):
            block = block_of(b, i)
            values = pass_lse[pl.ds(lax.rem(block, 32), 1)]
            pick = lane == sub + (block // 32) * 64
            col = jnp.sum(jnp.where(pick, values, 0.0), axis=1, keepdims=True) + 1.0
            z = logit[b][i * rows:(i + 1) * rows]
            probs = prod[b][2 * i:2 * i + 2, :, 0:queries].reshape(rows, queries)
            probs = probs + jnp.exp2(z - col)
            weight[b][i * rows:(i + 1) * rows] = probs.astype(b16)

    def multiply(b):
        q = full[:, b].reshape(queries, width)
        out = jnp.dot(weight[b][...], q, preferred_element_type=f32)
        prod[b][...] = out.reshape(2 * cands, deep, width)

    part_in, sum_in = {}, {}

    def back_of(node):
        return tuple(-v % SIDE for v in node)

    def make(h, node):
        owner = away(h, back_of(node))

        def slot(c, carry):
            block = owner * per + jnp.where(
                c == 0, pick_of(me.dp, owner, 0), pick_of(me.dp, owner, 1))
            acc = jnp.zeros((half, width), f32)
            for b in range(per):
                k = spot_s[b, block]
                live = (k >= 0).astype(f32)
                acc = acc + prod[b][2 * (jnp.maximum(k, 0) + 1) + h] * live
            part[0, h, slot_from(h, node) + c] = acc.astype(b16)
            return carry

        lax.fori_loop(0, CAP, slot, 0)

    def emit(*nodes):
        for node, up, axis, step in TREE:
            if node in nodes:
                for h in (0, 1):
                    make(h, node)
                    part_in[h, node] = net.send(
                        part.at[0, h, pl.ds(slot_from(h, node), CAP)], seen[h][node],
                        toward(h, axis, -step))

    def collect(h, here, j, acc):
        block = away(h, back_of(here)) * per + j
        if here != (0, 0):
            r = rank_of(me.dp, block)
            mine_ = part[0, h, slot_from(h, here) + jnp.maximum(r, 0)]
            acc = acc + mine_.astype(f32) * (r >= 0).astype(f32)
        for node, up, axis, step in TREE:
            if up != here:
                continue
            if node in HUBS:
                acc = acc + hub_sum[h][node][j].astype(f32)
            else:
                hop = tuple((a - b) % SIDE for a, b in zip(node, up))
                r = rank_of(away(h, hop), block)
                piece = seen[h][node][jnp.maximum(r, 0)]
                acc = acc + piece.astype(f32) * (r >= 0).astype(f32)
        return acc

    def climb(*here):
        for lo in pieces:
            for at_hub in here:
                for h in (0, 1):
                    climb_piece(h, at_hub, lo)

    def climb_piece(h, here, lo):
        n = HUBS.index(here)
        axis, step = [(a, s) for node, _, a, s in TREE if node == here][0]
        for node, up, *_ in TREE:
            if up == here and node in HUBS:
                sum_in[h, node, lo].wait_recv()
            elif up == here and lo == 0:
                part_in[h, node].wait_recv()

        def block(j, carry):
            dense[h, n, j] = collect(h, here, j, jnp.zeros((half, width), f32)).astype(b16)
            return carry

        lax.fori_loop(lo, lo + two, block, 0)
        sum_in[h, here, lo] = net.send(
            dense.at[h, n, pl.ds(lo, two)], hub_sum[h][here].at[pl.ds(lo, two)],
            toward(h, axis, -step))

    def query_grad(b):
        load_candidates(b)
        grad = lax.dot_general(weight[b][...], cand[b % 2][...], (((0,), (0,)), ((), ())),
                               preferred_element_type=f32)
        query_part[:, b] = grad.astype(b16).reshape(inners, rows, width)

    swaps = {}

    def swap(lo):
        for dz in (2, 1, 3, 0):
            src = query_part.at[mod4(me.z + dz) * 2 + 1 - me.c, pl.ds(lo, two)]
            swaps[dz, lo] = net.send(src, pair_in.at[dz, pl.ds(lo, two)], me.move("core", 0))

    def join(dz, lo):
        swaps[dz, lo].wait_recv()
        slot = mod4(me.z + dz) * 2 + me.c

        def step(j, carry):
            both = query_part[slot, j].astype(f32) + pair_in[dz, j].astype(f32)
            qsum[dz, j] = both.astype(b16)
            return carry

        lax.fori_loop(lo, lo + two, step, 0)

    def fold_in(target, rd, source, start):
        def step(j, carry):
            both = target[rd, start + j].astype(f32) + source[j].astype(f32)
            target[rd, start + j] = both.astype(b16)
            return carry

        lax.fori_loop(0, two, step, 0)

    weigh(0)
    for b in range(1, per):
        multiply(b - 1)
        weigh(b)
    multiply(per - 1)
    emit((2, 0), (2, 2))
    emit((3, 0), (3, 2))
    query_grad(0)
    emit((1, 2), (2, 1))
    loss_waits = [net.send(loss_mid.at[0], loss_dp.at[me.dp], to, loss_dp.at[origin])
                  for to, origin in zip(dp_peers, dp_from)]
    loss_dp[me.dp] = loss_mid[0]
    for h in (0, 1):
        make(h, (2, 3))
    climb((2, 3))
    query_grad(1)
    swap(0)
    for b in range(two, per):
        query_grad(b)
    swap(two)
    emit((0, 2), (1, 3), (3, 1))
    join(2, 0)
    za = net.send(qsum.at[2, 0:two], zmerge.at[0], me.move("z", 1))
    join(2, two)
    zb = net.send(qsum.at[2, two:per], zmerge.at[1], me.move("z", -1))
    for h in (0, 1):
        make(h, (3, 3))
    climb((3, 3))
    join(1, two)
    z_in = [net.send(qsum.at[1, two:per], zlast.at[0, two:per], me.move("z", 1))]
    join(3, 0)
    z_in.append(net.send(qsum.at[3, 0:two], zlast.at[1, 0:two], me.move("z", -1)))
    for h in (0, 1):
        make(h, (1, 1))
    climb((1, 1))
    emit((1, 0))
    join(1, 0)
    join(3, two)
    for h in (0, 1):
        make(h, (0, 3))
        make(h, (0, 1))
    za.wait_recv()
    fold_in(qsum, 1, zmerge.at[0], 0)
    z_in.append(net.send(qsum.at[1, 0:two], zlast.at[0, 0:two], me.move("z", 1)))
    zb.wait_recv()
    fold_in(qsum, 3, zmerge.at[1], two)
    z_in.append(net.send(qsum.at[3, two:per], zlast.at[1, two:per], me.move("z", -1)))
    climb((0, 3), (0, 1))
    for copy in loss_waits:
        copy.wait_recv()
    mid = jnp.sum(loss_dp[...], axis=0)
    loss_mid[1] = mid
    loss_waits = [net.send(loss_mid.at[1], loss_inner.at[me.inner], to, loss_inner.at[origin])
                  for to, origin in zip(in_peers, in_from)]
    loss_inner[me.inner] = mid
    for lo in (0, two):
        swaps[0, lo].wait_recv()
    for copy in z_in:
        copy.wait_recv()
    def finish_query(j, carry):
        both = query_part[mine, j].astype(f32) + pair_in[0, j].astype(f32)
        both = both + zlast[0, j].astype(f32) + zlast[1, j].astype(f32)
        qg_ref[j] = both.astype(b16)
        return carry

    lax.fori_loop(0, per, finish_query, 0)
    store_q = pltpu.make_async_copy(qg_ref, qg_hbm, local.at[0])
    store_q.start()
    for copy in loss_waits:
        copy.wait_recv()
    loss_out[0, 0] = jnp.max(jnp.sum(loss_inner[...], axis=0)) * (ln2 / count)
    for h in (0, 1):
        part_in[h, (1, 0)].wait_recv()
    store_p = []
    for j in range(per):
        for h in (0, 1):
            if j in pieces:
                for node in ((0, 3), (0, 1)):
                    sum_in[h, node, j].wait_recv()
            acc = collect(h, (0, 0), j, prod[j][h])
            pg_ref[j, h * half:(h + 1) * half] = acc.astype(b16)
        store_p.append(pltpu.make_async_copy(pg_ref.at[j], pg_hbm.at[j], local.at[4 + j]))
        store_p[-1].start()
    net.drain()
    store_q.wait()
    for copy in store_p:
        copy.wait()


def split_list(items, counts):
    out, start = [], 0
    for n in counts:
        out.append(tuple(items[start:start + n]))
        start += n
    return out


def finish_kernel(loss_ref, q_ref, p_ref, loss_out, q_out, p_out, loss_buf, q_buf, p_buf, sem):
    moves = [(loss_ref, loss_buf, loss_out)]
    for j in range(q_ref.shape[0]):
        moves += [(q_ref.at[j], q_buf.at[j], q_out.at[j]), (p_ref.at[j], p_buf.at[j], p_out.at[j])]
    loads = [pltpu.make_async_copy(a, b, sem.at[0, i]) for i, (a, b, c) in enumerate(moves)]
    stores = [pltpu.make_async_copy(b, c, sem.at[1, i]) for i, (a, b, c) in enumerate(moves)]
    for copy in loads:
        copy.start()
    for copy, after in zip(loads, stores):
        copy.wait()
        after.start()
    for copy in stores:
        copy.wait()


CHUNKS = 1


def body(queries, passages, neg_lists):
    per, rows, width = queries.shape
    groups, inners = lax.axis_size("dp"), lax.axis_size("inner")
    picks = neg_lists.shape[1]
    half, two = rows // 2, per // 2
    slots = groups * CAP
    chunks = CHUNKS
    deep = half // chunks
    cands, full_rows = picks + 1, rows * inners
    tall = cands * 2 * deep
    b16, f32 = jnp.bfloat16, jnp.float32
    sds = jax.ShapeDtypeStruct
    v = pltpu.VMEM
    sem_count = 100 + 160 * chunks
    need = {
        "full": [v((inners, per, rows, width), b16)],
        "stage": [v((2, len(TREE) - len(HUBS), CAP, half, width), b16)],
        "got": [v((2, slots, deep, width), b16)] * chunks,
        "logit": [v((tall, full_rows), f32)] * per,
        "weight": [v((tall, full_rows), b16)] * per,
        "prod": [v((2 * cands, deep, width), f32)] * per,
        "cand": [v((tall, width), b16)] * 2,
        "cols": [v((per, 32, 128), f32)],
        "row_part": [v((chunks, per, full_rows), f32)],
        "row_src": [v((per, full_rows), f32)],
        "dense_src": [v((32, 128), f32)],
        "all_rows": [v((inners, per, full_rows), f32)],
        "all_dense": [v((groups, 32, 128), f32)],
        "row_lse": [v((per, full_rows), f32)],
        "pass_lse": [v((32, 128), f32)],
        "part": [v((chunks, 2, slots, deep, width), b16)],
        "query_part": [v((inners, per, rows, width), b16)],
        "own_sum": [v((8, 128), f32)],
        "dense": [v((2, len(HUBS), per, half, width), b16)],
        "hub_sum": [v((per, half, width), b16)] * (2 * len(HUBS)),
        "pair_in": [v((SIDE, per, rows, width), b16)],
        "qsum": [v((SIDE, per, rows, width), b16)],
        "zmerge": [v((2, two, rows, width), b16)],
        "zlast": [v((2, per, rows, width), b16)],
        "loss_dp": [v((groups, 8, 128), f32)],
        "loss_inner": [v((inners, 8, 128), f32)],
        "loss_mid": [v((2, 8, 128), f32)],
        "near": [v((per, half, width), b16)] * (2 * len(HUBS)),
        "seen": [v((CAP, half, width), b16)] * (2 * (len(TREE) - len(HUBS))),
        "send_sem": [pltpu.SemaphoreType.DMA((sem_count,))],
        "recv_sem": [pltpu.SemaphoreType.DMA((sem_count,))],
        "local_sem": [pltpu.SemaphoreType.DMA((4 + per,))],
        "p_own": [v((per, rows, width), b16)],
        "qg": [v((per, rows, width), b16)],
        "pg": [v((per, rows, width), b16)],
        "tab_v": [v((1 + CAP, groups, 128), jnp.int32)],
        "tab_s": [pltpu.SMEM((1 + CAP, groups, 128), jnp.int32)],
        "spot_v": [v((groups, per, 128), jnp.int32)],
        "spot_s": [pltpu.SMEM((per, 128), jnp.int32)],
    }
    spec = {name: len(refs) for name, refs in need.items()}
    loss, query_grad, passage_grad = pl.pallas_call(
        functools.partial(fused_kernel, (chunks, groups, inners), spec),
        out_shape=(sds((1, 1), f32), sds((per, rows, width), b16), sds((per, rows, width), b16)),
        in_specs=[VM, AN, AN], out_specs=(SM, AN, AN),
        scratch_shapes=[ref for refs in need.values() for ref in refs],
        compiler_params=pltpu.CompilerParams(
            vmem_limit_bytes=VMEM_LIMIT, collective_id=0, has_side_effects=True),
        name="fused",
    )(neg_lists.T, queries, passages)
    shape = (per, rows, width)
    loss, query_grad, passage_grad = pl.pallas_call(
        finish_kernel,
        out_shape=(sds((1, 1), f32), sds(shape, b16), sds(shape, b16)),
        in_specs=[AN, AN, AN], out_specs=(AN, AN, AN),
        scratch_shapes=[pltpu.SMEM((1, 1), f32), v(shape, b16), v(shape, b16),
                        pltpu.SemaphoreType.DMA((2, 1 + 2 * per))],
        name="finish",
    )(loss, query_grad, passage_grad)
    return (loss.reshape(()), query_grad, passage_grad)


def solution(mesh):
    in_specs = (P("dp", "inner", None), P("dp", "inner", None), P())
    out_specs = (P(), P("dp", "inner", None), P("dp", "inner", None))
    return jax.shard_map(body, mesh=mesh, in_specs=in_specs, out_specs=out_specs, check_vma=False)
```
